128 devices in a mesh: scene: 8 (over z, core), rows: 16 (over y, x).
Axes of the slice: x: 4, y: 4, z: 4, core: 2. Of those that a mesh axis runs over, the one named last changes fastest.
Arguments:
- observations: float32 [2048, 256, 512], P(('scene', 'rows')), may hold values from -100 to 100
- inverse_factor: float32 [512, 512], replicated, may hold values from -2 to 2, as said below
- tile_count: int32 [128], P(('scene', 'rows')), may hold values from 0 to 16
- tile_owner: int32 [2048], P(('scene', 'rows')), may hold values from 0 to 7, as said below
- tile_slot: int32 [2048], P(('scene', 'rows')), may hold values from 0 to 7
Outputs:
- orthonormal: float32 [1024, 256, 512], P(('scene', 'rows'))
- factor: float32 [512, 512], replicated
The draws below stay inside these ranges and needn't reach their ends.
Inputs may be any that keep to these rules, and one draw needn't show every extreme that they name: `tile_owner`: within each group (fixed rows index), every row-block owner's 8 slots are each named by exactly one live tile of that group; at most 2 live tiles of one device name the same owner, and in every group one device names every owner 2 times. `inverse_factor`: upper triangular with a positive diagonal.
All inputs are finite; a program needn't handle non-finite values.
Results may differ from the reference program's by a relative error of at most 0.0001.
Values sent between devices are 32-bit elements; how exact they have to be, the bound alone decides.
No kernel may reach another device: no remote copies, remote signals or barrier semaphores. Data moves between devices by JAX's collectives and lax.ppermute only.
A program may use at most 128 MiB of HBM per device.

```python
import math
import jax
import jax.numpy as jnp
from jax import lax

NSRC = 512
TILE = 256
OWN_TILES = 8
SCENES = 8
GROUPS = 16
PAIR = 2
CAP = 16
ROWS_ALL = 262144


def plan_tiles(key):
    base_key = jax.random.fold_in(key, 7)
    heavy_key, bias_key, noise_key, order_key, list_key, dead_key = jax.random.split(base_key, 6)
    seat_count = SCENES * PAIR
    seat_index = jnp.arange(seat_count, dtype=jnp.int32)
    seat_src = seat_index // PAIR
    heavy_src = jax.random.randint(heavy_key, (GROUPS,), 0, SCENES)
    src_bias = jax.random.randint(bias_key, (GROUPS, SCENES), 0, 2 ** 18)
    seat_noise = jax.random.randint(noise_key, (GROUPS, SCENES, seat_count), 0, 2 ** 18)
    seat_score = (seat_noise + src_bias[:, None, :][:, :, seat_src]) * seat_count + seat_index
    seat_score = seat_score + jnp.where(seat_src[None, None, :] == heavy_src[:, None, None], 2 ** 28, 0)
    top_values, top_index = lax.top_k(seat_score, OWN_TILES)
    chosen = (top_index[..., None] == seat_index).any(-2)
    rank_key = jax.random.randint(order_key, (GROUPS, SCENES, seat_count), 0, 2 ** 20) * seat_count + seat_index
    smaller = chosen[:, :, None, :] & (rank_key[:, :, None, :] < rank_key[:, :, :, None])
    dest_slot = smaller.sum(-1).astype(jnp.int32)
    dead_slot = jax.random.randint(dead_key, (GROUPS, SCENES, seat_count), 0, OWN_TILES)
    dest_slot = jnp.where(chosen, dest_slot, dead_slot)
    dest_owner = jnp.broadcast_to(jnp.arange(SCENES, dtype=jnp.int32)[None, :, None], (GROUPS, SCENES, seat_count))

    def source_view(values):
        shaped = values.reshape(GROUPS, SCENES, SCENES, PAIR)
        return jnp.transpose(shaped, (2, 0, 1, 3)).reshape(SCENES, GROUPS, CAP)
    is_live = source_view(chosen.astype(jnp.int32))
    owner_view = source_view(dest_owner)
    slot_view = source_view(dest_slot)
    list_key_values = jax.random.randint(list_key, (SCENES, GROUPS, CAP), 0, 2 ** 20) * CAP + jnp.arange(CAP, dtype=jnp.int32)
    list_key_values = list_key_values + jnp.where(is_live > 0, 0, 2 ** 26)
    list_order = jnp.argsort(list_key_values, axis=-1)
    owner_list = jnp.take_along_axis(owner_view, list_order, axis=-1)
    slot_list = jnp.take_along_axis(slot_view, list_order, axis=-1)
    live_count = is_live.sum(-1).astype(jnp.int32)
    return (live_count.reshape(-1), owner_list.reshape(-1).astype(jnp.int32), slot_list.reshape(-1).astype(jnp.int32))


def draw_tile_count(key, part):
    return plan_tiles(key)[0]


def draw_tile_owner(key, part):
    return plan_tiles(key)[1]


def draw_tile_slot(key, part):
    return plan_tiles(key)[2]


def draw_observations(key, part):
    rows_total = SCENES * GROUPS * CAP
    normal_key, scale_key, column_key = jax.random.split(key, 3)
    base_values = jnp.clip(jax.random.normal(normal_key, (rows_total, TILE, NSRC), jnp.float32), -4.0, 4.0)
    row_scale = 0.3 * 10.0 ** jax.random.uniform(scale_key, (rows_total, TILE, 1), jnp.float32)
    block_id = jnp.arange(rows_total, dtype=jnp.int32) // CAP
    group_id = (block_id % GROUPS).astype(jnp.float32)
    rising = 3.0 ** (0.5 * group_id / max(GROUPS - 1, 1))
    column_scale = 10.0 ** (0.5 * jax.random.uniform(column_key, (NSRC,), jnp.float32))
    result = base_values * row_scale * rising[:, None, None] * column_scale
    return result.astype(jnp.float32)


def draw_inverse_factor(key, part):
    diag_key, off_key = jax.random.split(key)
    diagonal = 0.5 * 4.0 ** jax.random.uniform(diag_key, (NSRC,), jnp.float32)
    off_values = jnp.clip(jax.random.normal(off_key, (NSRC, NSRC), jnp.float32), -4.0, 4.0) * (0.5 / math.sqrt(NSRC))
    return (jnp.triu(off_values, 1) + jnp.diag(diagonal)).astype(jnp.float32)


def setup_inputs(seed: int = 0) -> dict:
    key_list = jax.random.split(jax.random.key(seed), 6)
    return {
        "observations": draw_observations(jax.random.fold_in(key_list[5], 71), 0),
        "inverse_factor": draw_inverse_factor(jax.random.fold_in(key_list[5], 71), 0),
        "tile_count": draw_tile_count(jax.random.fold_in(key_list[5], 71), 0),
        "tile_owner": draw_tile_owner(jax.random.fold_in(key_list[5], 71), 0),
        "tile_slot": draw_tile_slot(jax.random.fold_in(key_list[5], 71), 0),
    }


def reference(observations, inverse_factor, tile_count, tile_owner, tile_slot):
    blocks = SCENES * GROUPS
    block_id = jnp.arange(blocks, dtype=jnp.int32)
    group_id = block_id % GROUPS
    is_live = jnp.arange(CAP, dtype=jnp.int32)[None, :] < tile_count[:, None]
    dest_index = (tile_owner.reshape(blocks, CAP) * GROUPS + group_id[:, None]) * OWN_TILES + tile_slot.reshape(blocks, CAP)
    dest_index = jnp.where(is_live, dest_index, blocks * OWN_TILES).astype(jnp.int32)
    source_of = jnp.zeros((blocks * OWN_TILES + 1,), jnp.int32)
    source_of = source_of.at[dest_index.reshape(-1)].set(jnp.arange(blocks * CAP, dtype=jnp.int32))
    source_of = source_of[:blocks * OWN_TILES].reshape(blocks, OWN_TILES)

    def project(indices):
        tile_block = jnp.take(observations, indices, axis=0).reshape(-1, NSRC)
        return jnp.dot(tile_block.astype(jnp.float32), inverse_factor.astype(jnp.float32), precision=lax.Precision.HIGHEST, preferred_element_type=jnp.float32)

    def accumulate(carry, indices):
        projected = project(indices)
        term = lax.dot_general(projected.astype(jnp.float32), projected.astype(jnp.float32), (((0,), (0,)), ((), ())), precision=lax.Precision.HIGHEST, preferred_element_type=jnp.float32)
        return (carry + term, None)
    gram_sum, unused = lax.scan(accumulate, jnp.zeros((NSRC, NSRC), jnp.float32), source_of)
    weight = gram_sum / ROWS_ALL
    lower_factor = jnp.linalg.cholesky(weight)
    inv_upper = jax.scipy.linalg.solve_triangular(lower_factor, jnp.eye(NSRC, dtype=jnp.float32), lower=True).T

    def finish(indices):
        result = jnp.dot(project(indices).astype(jnp.float32), inv_upper.astype(jnp.float32), precision=lax.Precision.HIGHEST, preferred_element_type=jnp.float32)
        return result.reshape(OWN_TILES, TILE, NSRC)
    orthonormal = lax.map(finish, source_of).reshape(blocks * OWN_TILES, TILE, NSRC)
    return (orthonormal, lower_factor.T)
```

```python
import functools

import jax
import jax.numpy as jnp
from jax import lax
from jax.experimental import pallas as pl
from jax.experimental.pallas import tpu as pltpu
from jax.sharding import PartitionSpec as P

OWN_TILES = 8
BLOCK = 128
PIVOT = 8
HALF = 256


def split(value):
    head = value.astype(jnp.bfloat16)
    return head, (value - head.astype(jnp.float32)).astype(jnp.bfloat16)


def dot16(left, right, left_dim=1, right_dim=0):
    return lax.dot_general(
        left,
        right,
        (((left_dim,), (right_dim,)), ((), ())),
        preferred_element_type=jnp.float32,
    )


def dot32(left, right, left_dim=1, right_dim=0):
    return lax.dot_general(
        left,
        right,
        (((left_dim,), (right_dim,)), ((), ())),
        precision=lax.Precision.HIGHEST,
        preferred_element_type=jnp.float32,
    )


def dot_split(left, right):
    return dot16(left[0], right[0]) + (dot16(left[0], right[1]) + dot16(left[1], right[0]))


def pack_kernel(count_ref, owner_ref, slot_ref, tiles_ref, packed_ref, seat_slot_ref, used, sems):
    capacity, scenes = owner_ref.shape[0], used.shape[0]
    for seat in range(capacity):
        seat_slot_ref[seat] = -1
    for owner in range(scenes):
        used[owner] = 0
    for i in range(capacity):

        @pl.when(i < count_ref[0])
        def _():
            owner = owner_ref[i]
            rank = used[owner]
            used[owner] = rank + 1
            seat = owner * (capacity // scenes) + rank
            seat_slot_ref[seat] = slot_ref[i]
            pltpu.make_async_copy(tiles_ref.at[i], packed_ref.at[seat], sems.at[i]).start()

    for i in range(capacity):

        @pl.when(i < count_ref[0])
        def _():
            pltpu.make_async_copy(tiles_ref.at[i], packed_ref.at[0], sems.at[i]).wait()


def pack(tiles, tile_count, tile_owner, tile_slot, scenes):
    smem = pl.BlockSpec(memory_space=pltpu.SMEM)
    hbm = pl.BlockSpec(memory_space=pl.ANY)
    capacity = tile_owner.shape[0]
    return pl.pallas_call(
        pack_kernel,
        out_shape=(
            jax.ShapeDtypeStruct(tiles.shape, tiles.dtype),
            jax.ShapeDtypeStruct((capacity,), jnp.int32),
        ),
        in_specs=[smem, smem, smem, hbm],
        out_specs=(hbm, smem),
        scratch_shapes=[pltpu.SMEM((scenes,), jnp.int32), pltpu.SemaphoreType.DMA((capacity,))],
        cost_estimate=pl.CostEstimate(flops=0, bytes_accessed=2 * tiles.size * 4, transcendentals=0),
        name="pack",
    )(tile_count, tile_owner, tile_slot, tiles)


def gram_kernel(count_ref, tile_ref, inverse_ref, gram_ref, inv_head, inv_tail, cross):
    step = pl.program_id(0)

    @pl.when(step == 0)
    def _():
        head, tail = split(inverse_ref[...])
        inv_head[...] = head
        inv_tail[...] = tail
        gram_ref[...] = jnp.zeros_like(gram_ref)
        cross[...] = jnp.zeros_like(cross)

    @pl.when(step < count_ref[0])
    def _():
        head, tail = split(tile_ref[0])
        left = dot_split(
            (head[:, :HALF], tail[:, :HALF]), (inv_head[:HALF, :HALF], inv_tail[:HALF, :HALF])
        )
        right = dot_split((head, tail), (inv_head[:, HALF:], inv_tail[:, HALF:]))
        left_head, left_tail = split(left)
        right_head, right_tail = split(right)
        gram_ref[:HALF, :] += dot16(left_head, left_head, 0, 0)
        cross[:HALF, :] += dot16(left_head, left_tail, 0, 0)
        gram_ref[HALF : 2 * HALF, :] += (
            dot16(left_head, right_head, 0, 0)
            + dot16(left_head, right_tail, 0, 0)
            + dot16(left_tail, right_head, 0, 0)
        )
        gram_ref[2 * HALF :, :] += dot16(right_head, right_head, 0, 0)
        cross[HALF:, :] += dot16(right_head, right_tail, 0, 0)

    @pl.when(step == pl.num_programs(0) - 1)
    def _():
        gram_ref[:HALF, :] += cross[:HALF, :] + cross[:HALF, :].T
        gram_ref[2 * HALF :, :] += cross[HALF:, :] + cross[HALF:, :].T


def gram(tiles, inverse_factor, tile_count):
    capacity, rows, columns = tiles.shape
    return pl.pallas_call(
        gram_kernel,
        out_shape=jax.ShapeDtypeStruct((3 * HALF, HALF), jnp.float32),
        grid_spec=pltpu.PrefetchScalarGridSpec(
            num_scalar_prefetch=1,
            grid=(capacity,),
            in_specs=[
                pl.BlockSpec(
                    (1, rows, columns),
                    lambda i, count: (jnp.minimum(i, jnp.maximum(count[0] - 1, 0)), 0, 0),
                ),
                pl.BlockSpec((columns, columns), lambda i, count: (0, 0)),
            ],
            out_specs=pl.BlockSpec((3 * HALF, HALF), lambda i, count: (0, 0)),
            scratch_shapes=[
                pltpu.VMEM((columns, columns), jnp.bfloat16),
                pltpu.VMEM((columns, columns), jnp.bfloat16),
                pltpu.VMEM((2 * HALF, HALF), jnp.float32),
            ],
        ),
        compiler_params=pltpu.CompilerParams(
            dimension_semantics=("arbitrary",), vmem_limit_bytes=56 << 20
        ),
        cost_estimate=pl.CostEstimate(
            flops=1_000_000, bytes_accessed=1 << 16, transcendentals=0
        ),
        name="gram",
    )(tile_count, tiles, inverse_factor)


def ring_pairs(size, span, stride, shift):
    ring = [i // stride % span for i in range(size)]
    return [(i, i + ((r + shift) % span - r) * stride) for i, r in enumerate(ring)]


def scatter_sum(value, axis, span, stride):
    size = lax.axis_size(axis)
    me = lax.axis_index(axis) // stride % span
    parts = value.reshape((span, -1) + value.shape[1:])
    total = lax.dynamic_index_in_dim(parts, me, 0, keepdims=False)
    for shift in range(1, span):
        sent = lax.dynamic_index_in_dim(parts, (me + shift) % span, 0, keepdims=False)
        total = total + lax.ppermute(sent, axis, ring_pairs(size, span, stride, shift))
    return total


def select_one(tests, values):
    chosen = values[0]
    for test, value in zip(tests[1:], values[1:]):
        chosen = jnp.where(test, value, chosen)
    return chosen


def gather(value, axis, span, stride):
    size = lax.axis_size(axis)
    me = lax.axis_index(axis) // stride % span
    onward = [value] + [
        lax.ppermute(value, axis, ring_pairs(size, span, stride, span - ahead))
        for ahead in range(1, span)
    ]
    ordered = [
        select_one([(me + ahead) % span == place for ahead in range(span)], onward)
        for place in range(span)
    ]
    return jnp.concatenate(ordered, 0)


def sum_everywhere(value, scenes, rows):
    side = 4
    stages = [("scene", 2, 1), ("rows", side, 1), ("rows", rows // side, side), ("scene", scenes // 2, 2)]
    for axis, span, stride in stages:
        value = scatter_sum(value, axis, span, stride)
    for axis, span, stride in reversed(stages):
        value = gather(value, axis, span, stride)
    return value


def sweep(block):
    shape = (PIVOT, BLOCK)
    lane = lax.broadcasted_iota(jnp.int32, shape, 1)
    sub = lax.broadcasted_iota(jnp.int32, shape, 0)
    strips = [block[PIVOT * v : PIVOT * (v + 1), :] for v in range(BLOCK // PIVOT)]
    upper = []
    for s in range(len(strips)):
        base = PIVOT * s
        inside = (lane >= base) & (lane < base + PIVOT)
        own = [jnp.broadcast_to(strips[s][q : q + 1, :], shape) for q in range(PIVOT)]
        pivot = {
            (r, c): jnp.broadcast_to(own[r][:, base + c : base + c + 1], shape)
            for r in range(PIVOT)
            for c in range(r, PIVOT)
        }
        u = {}
        scale = []
        for q in range(PIVOT):
            scale.append(lax.rsqrt(pivot[q, q]))
            for c in range(q + 1, PIVOT):
                u[q, c] = pivot[q, c] * scale[q]
            for r in range(q + 1, PIVOT):
                for c in range(r, PIVOT):
                    pivot[r, c] = pivot[r, c] - u[q, r] * u[q, c]
        swept = [
            jnp.where(inside, jnp.where(lane == base + q, 1.0, 0.0), own[q]) for q in range(PIVOT)
        ]
        for q in range(PIVOT):
            for r in range(q):
                own[q] = own[q] - u[r, q] * own[r]
                swept[q] = swept[q] - u[r, q] * swept[r]
            own[q] = own[q] * scale[q]
            swept[q] = swept[q] * scale[q]
        for v in range(s + 1, len(strips)):
            column = []
            for q in range(PIVOT):
                entry = jnp.broadcast_to(strips[v][:, base + q : base + q + 1], shape)
                for r in range(q):
                    entry = entry - u[r, q] * column[r]
                column.append(entry * scale[q])
            rest = jnp.where(inside, 0.0, strips[v])
            for q in range(PIVOT):
                rest = rest - column[q] * swept[q]
            strips[v] = rest
        factor_rows, inverse_rows = own[0], swept[0]
        for q in range(1, PIVOT):
            factor_rows = jnp.where(sub == q, own[q], factor_rows)
            inverse_rows = jnp.where(sub == q, swept[q], inverse_rows)
        upper.append(jnp.where(lane >= base + sub, factor_rows, 0.0))
        strips[s] = jnp.where(lane <= base + sub, inverse_rows, 0.0)
    return jnp.concatenate(upper, 0), jnp.concatenate(strips, 0)


def factor_kernel(row_count, gram_ref, inverse_ref, factor_ref, head_ref, tail_ref, work):
    size = work.shape[0]
    work[:HALF, :HALF] = gram_ref[:HALF, :] / row_count
    work[:HALF, HALF:] = gram_ref[HALF : 2 * HALF, :] / row_count
    work[HALF:, HALF:] = gram_ref[2 * HALF :, :] / row_count
    work[HALF:, :HALF] = jnp.zeros((HALF, HALF), jnp.float32)

    @pl.loop(0, size // BLOCK)
    def _(k):
        offset = pl.multiple_of(k * BLOCK, BLOCK)
        here = pl.ds(offset, BLOCK)
        upper, inverse = sweep(work[here, here])
        right = dot32(inverse, work[here, :])
        lane = lax.broadcasted_iota(jnp.int32, (BLOCK, size), 1)
        beyond = jnp.where(lane >= offset + BLOCK, right, 0.0)
        factor_ref[here, :] = beyond
        factor_ref[here, here] = upper
        work[here, :] = right
        work[here, here] = inverse

        @pl.when(k < size // BLOCK - 1)
        def _():
            row = lax.broadcasted_iota(jnp.int32, (size, BLOCK), 0)
            work[:, here] = jnp.where(row >= offset + BLOCK, 0.0, work[:, here])
            work[...] = work[...] - dot32(beyond, work[here, :], 0, 0)

    row = lax.broadcasted_iota(jnp.int32, work.shape, 0)
    lane = lax.broadcasted_iota(jnp.int32, work.shape, 1)
    inverse = jnp.where(lane <= row, work[...], 0.0)
    head_ref[...], tail_ref[...] = split(dot32(inverse_ref[...], inverse, 1, 1))


def factor(gram_sum, inverse_factor, row_count):
    vmem = pl.BlockSpec(memory_space=pltpu.VMEM)
    size = inverse_factor.shape[0]
    return pl.pallas_call(
        functools.partial(factor_kernel, row_count),
        out_shape=(
            jax.ShapeDtypeStruct((size, size), jnp.float32),
            jax.ShapeDtypeStruct((size, size), jnp.bfloat16),
            jax.ShapeDtypeStruct((size, size), jnp.bfloat16),
        ),
        in_specs=[vmem, vmem],
        out_specs=(vmem, vmem, vmem),
        scratch_shapes=[pltpu.VMEM((size, size), jnp.float32)],
        compiler_params=pltpu.CompilerParams(vmem_limit_bytes=24 << 20),
        cost_estimate=pl.CostEstimate(
            flops=1_000_000, bytes_accessed=1 << 16, transcendentals=0
        ),
        name="factor",
    )(gram_sum, inverse_factor)


def finish_kernel(
    slot_ref, head_ref, tail_ref, received, out_ref, tiles, results, in_sems, out_sems
):
    for seat in range(slot_ref.shape[0]):
        slot = slot_ref[seat]

        @pl.when(slot >= 0)
        def _():
            pltpu.make_async_copy(received.at[seat], tiles.at[slot], in_sems.at[slot]).start()

    def result_copy(j):
        return pltpu.make_async_copy(results.at[j], out_ref.at[j], out_sems.at[j])

    @pl.loop(0, OWN_TILES)
    def _(j):
        pltpu.make_async_copy(received.at[0], tiles.at[j], in_sems.at[j]).wait()
        head, tail = split(tiles[j])
        results[j, :, :HALF] = dot_split(
            (head[:, :HALF], tail[:, :HALF]), (head_ref[:HALF, :HALF], tail_ref[:HALF, :HALF])
        )
        results[j, :, HALF:] = dot_split((head, tail), (head_ref[:, HALF:], tail_ref[:, HALF:]))
        result_copy(j).start()

    @pl.loop(0, OWN_TILES)
    def _(j):
        result_copy(j).wait()


def finish(slots, received, head, tail):
    _, rows, columns = received.shape
    hbm = pl.BlockSpec(memory_space=pl.ANY)
    vmem = pl.BlockSpec(memory_space=pltpu.VMEM)
    return pl.pallas_call(
        finish_kernel,
        out_shape=jax.ShapeDtypeStruct((OWN_TILES, rows, columns), jnp.float32),
        in_specs=[pl.BlockSpec(memory_space=pltpu.SMEM), vmem, vmem, hbm],
        out_specs=hbm,
        scratch_shapes=[
            pltpu.VMEM((OWN_TILES, rows, columns), jnp.float32),
            pltpu.VMEM((OWN_TILES, rows, columns), jnp.float32),
            pltpu.SemaphoreType.DMA((OWN_TILES,)),
            pltpu.SemaphoreType.DMA((OWN_TILES,)),
        ],
        compiler_params=pltpu.CompilerParams(vmem_limit_bytes=48 << 20),
        cost_estimate=pl.CostEstimate(
            flops=5_000_000_000, bytes_accessed=8 << 20, transcendentals=0
        ),
        name="finish",
    )(slots, head, tail, received)


def shards(observations, inverse_factor, tile_count, tile_owner, tile_slot):
    scenes, rows = lax.axis_size("scene"), lax.axis_size("rows")
    capacity, tile_rows, _ = observations.shape
    packed, seat_slot = pack(observations, tile_count, tile_owner, tile_slot, scenes)
    me = lax.axis_index("scene")
    group_slots = lax.all_gather(seat_slot.reshape(scenes, capacity // scenes), "scene")
    slots = lax.dynamic_index_in_dim(group_slots, me, 1, keepdims=False).reshape(capacity)
    received = lax.all_to_all(
        packed.reshape((scenes, capacity // scenes) + packed.shape[1:]), "scene", 0, 0, tiled=True
    ).reshape(packed.shape)
    tiles, _ = lax.optimization_barrier((observations, seat_slot))
    gram_sum = sum_everywhere(gram(tiles, inverse_factor, tile_count), scenes, rows)
    upper, head, tail = factor(gram_sum, inverse_factor, scenes * rows * OWN_TILES * tile_rows)
    return finish(slots, received, head, tail), upper


def solution(mesh):
    in_specs = (
        P(("scene", "rows"), None, None),
        P(),
        P(("scene", "rows")),
        P(("scene", "rows")),
        P(("scene", "rows")),
    )
    out_specs = (P(("scene", "rows"), None, None), P())
    return jax.shard_map(shards, mesh=mesh, in_specs=in_specs, out_specs=out_specs, check_vma=False)
```

```python
import functools

import jax
import jax.numpy as jnp
from jax import lax
from jax.experimental import pallas as pl
from jax.experimental.pallas import tpu as pltpu
from jax.sharding import PartitionSpec as P

OWN_TILES = 8
BLOCK = 128
PIVOT = 8
HALF = 256
EARLY = 120
HEADER = 8


def split(value):
    head = value.astype(jnp.bfloat16)
    return head, (value - head.astype(jnp.float32)).astype(jnp.bfloat16)


def dot16(left, right, left_dim=1, right_dim=0):
    return lax.dot_general(
        left,
        right,
        (((left_dim,), (right_dim,)), ((), ())),
        preferred_element_type=jnp.float32,
    )


def dot32(left, right, left_dim=1, right_dim=0):
    return lax.dot_general(
        left,
        right,
        (((left_dim,), (right_dim,)), ((), ())),
        precision=lax.Precision.HIGHEST,
        preferred_element_type=jnp.float32,
    )


def dot_split(left, right):
    return dot16(left[0], right[0]) + (dot16(left[0], right[1]) + dot16(left[1], right[0]))


def seat_of(i, owner_ref, used):
    owner = owner_ref[i]
    rank = used[owner]
    used[owner] = rank + 1
    return owner, rank


def pack_kernel(
    count_ref, owner_ref, slot_ref, tiles_ref, early_ref, staged, header, used, slots, sems, out_sems
):
    scenes, capacity = used.shape[0], owner_ref.shape[0]
    for i in range(capacity):

        @pl.when(i < count_ref[0])
        def _():
            source = tiles_ref.at[i, pl.ds(0, EARLY)]
            pltpu.make_async_copy(source, staged.at[i], sems.at[i]).start()

    for seat in range(capacity):
        slots[seat] = -1
    for owner in range(scenes):
        used[owner] = 0

    def store(i, owner, rank):
        target = early_ref.at[owner, pl.ds(pl.multiple_of(rank * EARLY, 8), EARLY)]
        return pltpu.make_async_copy(staged.at[i], target, sems.at[i])

    for i in range(capacity):

        @pl.when(i < count_ref[0])
        def _():
            owner, rank = seat_of(i, owner_ref, used)
            slots[2 * owner + rank] = slot_ref[i]
            source = tiles_ref.at[i, pl.ds(0, EARLY)]
            pltpu.make_async_copy(source, staged.at[i], sems.at[i]).wait()
            store(i, owner, rank).start()

    lane = lax.broadcasted_iota(jnp.int32, header.shape[1:], 1)
    half = header.shape[2] // 2
    headers = []
    for owner in range(scenes):
        pair = jnp.where(lane < half, slots[2 * owner], slots[2 * owner + 1])
        header[owner] = pair.astype(jnp.float32)
        target = early_ref.at[owner, pl.ds(2 * EARLY, HEADER)]
        headers.append(pltpu.make_async_copy(header.at[owner], target, out_sems.at[owner]))
        headers[-1].start()
    for i in range(capacity):

        @pl.when(i < count_ref[0])
        def _():
            store(i, 0, 0).wait()

    for copy in headers:
        copy.wait()


def pack(tiles, tile_count, tile_owner, tile_slot, scenes):
    smem = pl.BlockSpec(memory_space=pltpu.SMEM)
    hbm = pl.BlockSpec(memory_space=pl.ANY)
    capacity, columns = tile_owner.shape[0], tiles.shape[2]
    return pl.pallas_call(
        pack_kernel,
        out_shape=jax.ShapeDtypeStruct((scenes, 2 * EARLY + HEADER, columns), tiles.dtype),
        in_specs=[smem, smem, smem, hbm],
        out_specs=hbm,
        scratch_shapes=[
            pltpu.VMEM((capacity, EARLY, columns), jnp.float32),
            pltpu.VMEM((scenes, HEADER, columns), jnp.float32),
            pltpu.SMEM((scenes,), jnp.int32),
            pltpu.SMEM((capacity,), jnp.int32),
            pltpu.SemaphoreType.DMA((capacity,)),
            pltpu.SemaphoreType.DMA((scenes,)),
        ],
        compiler_params=pltpu.CompilerParams(vmem_limit_bytes=56 << 20),
        cost_estimate=pl.CostEstimate(flops=0, bytes_accessed=8 << 20, transcendentals=0),
        name="pack",
    )(tile_count, tile_owner, tile_slot, tiles)


def gram_kernel(
    count_ref, owner_ref, tile_ref, inverse_ref, gram_ref, late_ref, inv_head, inv_tail, cross, used, sem
):
    step = pl.program_id(0)

    @pl.when(step == 0)
    def _():
        head, tail = split(inverse_ref[...])
        inv_head[...] = head
        inv_tail[...] = tail
        gram_ref[...] = jnp.zeros_like(gram_ref)
        cross[...] = jnp.zeros_like(cross)
        for owner in range(used.shape[0]):
            used[owner] = 0

    @pl.when(step < count_ref[0])
    def _():
        owner, rank = seat_of(step, owner_ref, used)
        late = late_ref.shape[1] // 2
        target = late_ref.at[owner, pl.ds(pl.multiple_of(rank * late, 8), late)]
        copy = pltpu.make_async_copy(tile_ref.at[0, pl.ds(EARLY, late)], target, sem)
        copy.start()
        head, tail = split(tile_ref[0])
        left = dot_split(
            (head[:, :HALF], tail[:, :HALF]), (inv_head[:HALF, :HALF], inv_tail[:HALF, :HALF])
        )
        right = dot_split((head, tail), (inv_head[:, HALF:], inv_tail[:, HALF:]))
        left_head, left_tail = split(left)
        right_head, right_tail = split(right)
        gram_ref[:HALF, :] += dot16(left_head, left_head, 0, 0)
        cross[:HALF, :] += dot16(left_head, left_tail, 0, 0)
        gram_ref[HALF : 2 * HALF, :] += (
            dot16(left_head, right_head, 0, 0)
            + dot16(left_head, right_tail, 0, 0)
            + dot16(left_tail, right_head, 0, 0)
        )
        gram_ref[2 * HALF :, :] += dot16(right_head, right_head, 0, 0)
        cross[HALF:, :] += dot16(right_head, right_tail, 0, 0)
        copy.wait()

    @pl.when(step == pl.num_programs(0) - 1)
    def _():
        gram_ref[:HALF, :] += cross[:HALF, :] + cross[:HALF, :].T
        gram_ref[2 * HALF :, :] += cross[HALF:, :] + cross[HALF:, :].T


def gram(tiles, inverse_factor, tile_count, tile_owner, scenes):
    capacity, rows, columns = tiles.shape
    return pl.pallas_call(
        gram_kernel,
        out_shape=(
            jax.ShapeDtypeStruct((3 * HALF, HALF), jnp.float32),
            jax.ShapeDtypeStruct((scenes, 2 * (rows - EARLY), columns), jnp.float32),
        ),
        grid_spec=pltpu.PrefetchScalarGridSpec(
            num_scalar_prefetch=2,
            grid=(capacity,),
            in_specs=[
                pl.BlockSpec(
                    (1, rows, columns),
                    lambda i, count, _: (jnp.minimum(i, jnp.maximum(count[0] - 1, 0)), 0, 0),
                ),
                pl.BlockSpec((columns, columns), lambda i, *_: (0, 0)),
            ],
            out_specs=(
                pl.BlockSpec((3 * HALF, HALF), lambda i, *_: (0, 0)),
                pl.BlockSpec(memory_space=pl.ANY),
            ),
            scratch_shapes=[
                pltpu.VMEM((columns, columns), jnp.bfloat16),
                pltpu.VMEM((columns, columns), jnp.bfloat16),
                pltpu.VMEM((2 * HALF, HALF), jnp.float32),
                pltpu.SMEM((scenes,), jnp.int32),
                pltpu.SemaphoreType.DMA,
            ],
        ),
        compiler_params=pltpu.CompilerParams(
            dimension_semantics=("arbitrary",), vmem_limit_bytes=56 << 20
        ),
        cost_estimate=pl.CostEstimate(
            flops=1_000_000, bytes_accessed=1 << 16, transcendentals=0
        ),
        name="gram",
    )(tile_count, tile_owner, tiles, inverse_factor)


def ring_pairs(size, span, stride, shift):
    ring = [i // stride % span for i in range(size)]
    return [(i, i + ((r + shift) % span - r) * stride) for i, r in enumerate(ring)]


def scatter_sum(value, axis, span, stride):
    size = lax.axis_size(axis)
    me = lax.axis_index(axis) // stride % span
    parts = value.reshape((span, -1) + value.shape[1:])
    total = lax.dynamic_index_in_dim(parts, me, 0, keepdims=False)
    for shift in range(1, span):
        sent = lax.dynamic_index_in_dim(parts, (me + shift) % span, 0, keepdims=False)
        total = total + lax.ppermute(sent, axis, ring_pairs(size, span, stride, shift))
    return total


def select_one(tests, values):
    chosen = values[0]
    for test, value in zip(tests[1:], values[1:]):
        chosen = jnp.where(test, value, chosen)
    return chosen


def gather(value, axis, span, stride):
    size = lax.axis_size(axis)
    me = lax.axis_index(axis) // stride % span
    onward = [value] + [
        lax.ppermute(value, axis, ring_pairs(size, span, stride, span - ahead))
        for ahead in range(1, span)
    ]
    ordered = [
        select_one([(me + ahead) % span == place for ahead in range(span)], onward)
        for place in range(span)
    ]
    return jnp.concatenate(ordered, 0)


def reduction_stages(scenes, rows):
    side = 4
    return [("scene", 2, 1), ("rows", side, 1), ("rows", rows // side, side)]


def sum_along_z(value, scenes):
    parts = gather(value, "scene", scenes // 2, 2).reshape((scenes // 2,) + value.shape)
    total = parts[0]
    for place in range(1, scenes // 2):
        total = total + parts[place]
    return total


def sweep(block):
    shape = (PIVOT, BLOCK)
    lane = lax.broadcasted_iota(jnp.int32, shape, 1)
    sub = lax.broadcasted_iota(jnp.int32, shape, 0)
    strips = [block[PIVOT * v : PIVOT * (v + 1), :] for v in range(BLOCK // PIVOT)]
    upper = []
    for s in range(len(strips)):
        base = PIVOT * s
        inside = (lane >= base) & (lane < base + PIVOT)
        own = [jnp.broadcast_to(strips[s][q : q + 1, :], shape) for q in range(PIVOT)]
        pivot = {
            (r, c): jnp.broadcast_to(own[r][:, base + c : base + c + 1], shape)
            for r in range(PIVOT)
            for c in range(r, PIVOT)
        }
        u = {}
        scale = []
        for q in range(PIVOT):
            scale.append(lax.rsqrt(pivot[q, q]))
            for c in range(q + 1, PIVOT):
                u[q, c] = pivot[q, c] * scale[q]
            for r in range(q + 1, PIVOT):
                for c in range(r, PIVOT):
                    pivot[r, c] = pivot[r, c] - u[q, r] * u[q, c]
        swept = [
            jnp.where(inside, jnp.where(lane == base + q, 1.0, 0.0), own[q]) for q in range(PIVOT)
        ]
        for q in range(PIVOT):
            for r in range(q):
                own[q] = own[q] - u[r, q] * own[r]
                swept[q] = swept[q] - u[r, q] * swept[r]
            own[q] = own[q] * scale[q]
            swept[q] = swept[q] * scale[q]
        for v in range(s + 1, len(strips)):
            column = []
            for q in range(PIVOT):
                entry = jnp.broadcast_to(strips[v][:, base + q : base + q + 1], shape)
                for r in range(q):
                    entry = entry - u[r, q] * column[r]
                column.append(entry * scale[q])
            rest = jnp.where(inside, 0.0, strips[v])
            for q in range(PIVOT):
                rest = rest - column[q] * swept[q]
            strips[v] = rest
        factor_rows, inverse_rows = own[0], swept[0]
        for q in range(1, PIVOT):
            factor_rows = jnp.where(sub == q, own[q], factor_rows)
            inverse_rows = jnp.where(sub == q, swept[q], inverse_rows)
        upper.append(jnp.where(lane >= base + sub, factor_rows, 0.0))
        strips[s] = jnp.where(lane <= base + sub, inverse_rows, 0.0)
    return jnp.concatenate(upper, 0), jnp.concatenate(strips, 0)


def factor_kernel(row_count, gram_ref, inverse_ref, factor_ref, head_ref, tail_ref, work):
    size = work.shape[0]
    work[:HALF, :HALF] = gram_ref[:HALF, :] / row_count
    work[:HALF, HALF:] = gram_ref[HALF : 2 * HALF, :] / row_count
    work[HALF:, HALF:] = gram_ref[2 * HALF :, :] / row_count
    work[HALF:, :HALF] = jnp.zeros((HALF, HALF), jnp.float32)

    @pl.loop(0, size // BLOCK)
    def _(k):
        offset = pl.multiple_of(k * BLOCK, BLOCK)
        here = pl.ds(offset, BLOCK)
        upper, inverse = sweep(work[here, here])
        right = dot32(inverse, work[here, :])
        lane = lax.broadcasted_iota(jnp.int32, (BLOCK, size), 1)
        beyond = jnp.where(lane >= offset + BLOCK, right, 0.0)
        factor_ref[here, :] = beyond
        factor_ref[here, here] = upper
        work[here, :] = right
        work[here, here] = inverse

        @pl.when(k < size // BLOCK - 1)
        def _():
            row = lax.broadcasted_iota(jnp.int32, (size, BLOCK), 0)
            work[:, here] = jnp.where(row >= offset + BLOCK, 0.0, work[:, here])
            work[...] = work[...] - dot32(beyond, work[here, :], 0, 0)

    row = lax.broadcasted_iota(jnp.int32, work.shape, 0)
    lane = lax.broadcasted_iota(jnp.int32, work.shape, 1)
    inverse = jnp.where(lane <= row, work[...], 0.0)
    head_ref[...], tail_ref[...] = split(dot32(inverse_ref[...], inverse, 1, 1))


def factor(gram_sum, inverse_factor, row_count):
    vmem = pl.BlockSpec(memory_space=pltpu.VMEM)
    size = inverse_factor.shape[0]
    return pl.pallas_call(
        functools.partial(factor_kernel, row_count),
        out_shape=(
            jax.ShapeDtypeStruct((size, size), jnp.float32),
            jax.ShapeDtypeStruct((size, size), jnp.bfloat16),
            jax.ShapeDtypeStruct((size, size), jnp.bfloat16),
        ),
        in_specs=[vmem, vmem],
        out_specs=(vmem, vmem, vmem),
        scratch_shapes=[pltpu.VMEM((size, size), jnp.float32)],
        compiler_params=pltpu.CompilerParams(vmem_limit_bytes=24 << 20),
        cost_estimate=pl.CostEstimate(
            flops=1_000_000, bytes_accessed=1 << 16, transcendentals=0
        ),
        name="factor",
    )(gram_sum, inverse_factor)


def finish_kernel(
    slot_ref, head_ref, tail_ref, early_ref, late_ref, out_ref, tiles, results, in_sems, out_sems
):
    late = late_ref.shape[1] // 2

    def fetch(owner, rank, slot):
        return (
            pltpu.make_async_copy(
                early_ref.at[owner, pl.ds(rank * EARLY, EARLY)],
                tiles.at[slot, pl.ds(0, EARLY)],
                in_sems.at[slot, 0],
            ),
            pltpu.make_async_copy(
                late_ref.at[owner, pl.ds(rank * late, late)],
                tiles.at[slot, pl.ds(EARLY, late)],
                in_sems.at[slot, 1],
            ),
        )

    for seat in range(slot_ref.shape[0]):
        slot = slot_ref[seat]

        @pl.when(slot >= 0)
        def _():
            for copy in fetch(seat // 2, seat % 2, slot):
                copy.start()

    def result_copy(j):
        return pltpu.make_async_copy(results.at[j], out_ref.at[j], out_sems.at[j])

    @pl.loop(0, OWN_TILES)
    def _(j):
        for copy in fetch(0, 0, j):
            copy.wait()
        head, tail = split(tiles[j])
        results[j, :, :HALF] = dot_split(
            (head[:, :HALF], tail[:, :HALF]), (head_ref[:HALF, :HALF], tail_ref[:HALF, :HALF])
        )
        results[j, :, HALF:] = dot_split((head, tail), (head_ref[:, HALF:], tail_ref[:, HALF:]))
        result_copy(j).start()

    @pl.loop(0, OWN_TILES)
    def _(j):
        result_copy(j).wait()


def finish(slots, early, late, head, tail):
    columns = early.shape[2]
    rows = EARLY + late.shape[1] // 2
    hbm = pl.BlockSpec(memory_space=pl.ANY)
    vmem = pl.BlockSpec(memory_space=pltpu.VMEM)
    return pl.pallas_call(
        finish_kernel,
        out_shape=jax.ShapeDtypeStruct((OWN_TILES, rows, columns), jnp.float32),
        in_specs=[pl.BlockSpec(memory_space=pltpu.SMEM), vmem, vmem, hbm, hbm],
        out_specs=hbm,
        scratch_shapes=[
            pltpu.VMEM((OWN_TILES, rows, columns), jnp.float32),
            pltpu.VMEM((OWN_TILES, rows, columns), jnp.float32),
            pltpu.SemaphoreType.DMA((OWN_TILES, 2)),
            pltpu.SemaphoreType.DMA((OWN_TILES,)),
        ],
        compiler_params=pltpu.CompilerParams(vmem_limit_bytes=32 << 20),
        cost_estimate=pl.CostEstimate(
            flops=5_000_000_000, bytes_accessed=8 << 20, transcendentals=0
        ),
        name="finish",
    )(slots, head, tail, early, late)


def shards(observations, inverse_factor, tile_count, tile_owner, tile_slot):
    scenes, rows = lax.axis_size("scene"), lax.axis_size("rows")
    tile_rows, columns = observations.shape[1:]

    def exchange(packed):
        return lax.all_to_all(packed, "scene", 0, 0, tiled=True)

    packed = pack(observations, tile_count, tile_owner, tile_slot, scenes)
    early = exchange(packed)
    tiles, _ = lax.optimization_barrier((observations, packed))
    value, rest = gram(tiles, inverse_factor, tile_count, tile_owner, scenes)
    stages = reduction_stages(scenes, rows)
    for axis, span, stride in stages:
        value = scatter_sum(value, axis, span, stride)
    value = sum_along_z(value, scenes)
    rest, value = lax.optimization_barrier((rest, value))
    late = exchange(rest)
    for axis, span, stride in reversed(stages):
        value = gather(value, axis, span, stride)
    upper, head, tail = factor(value, inverse_factor, scenes * rows * OWN_TILES * tile_rows)
    slots = early[:, 2 * EARLY, :: columns // 2].astype(jnp.int32).reshape(-1)
    return finish(slots, early, late, head, tail), upper


def solution(mesh):
    in_specs = (
        P(("scene", "rows"), None, None),
        P(),
        P(("scene", "rows")),
        P(("scene", "rows")),
        P(("scene", "rows")),
    )
    out_specs = (P(("scene", "rows"), None, None), P())
    return jax.shard_map(shards, mesh=mesh, in_specs=in_specs, out_specs=out_specs, check_vma=False)
```

```python
import functools

import jax
import jax.numpy as jnp
from jax import lax
from jax.experimental import pallas as pl
from jax.experimental.pallas import tpu as pltpu
from jax.sharding import PartitionSpec as P

OWN_TILES = 8
BLOCK = 128
PIVOT = 8
HALF = 256
EARLY = 128
HEADER = 8
GROUP = 4


def split(value):
    head = value.astype(jnp.bfloat16)
    return head, (value - head.astype(jnp.float32)).astype(jnp.bfloat16)


def dot16(left, right, left_dim=1, right_dim=0):
    return lax.dot_general(
        left,
        right,
        (((left_dim,), (right_dim,)), ((), ())),
        preferred_element_type=jnp.float32,
    )


def dot32(left, right, left_dim=1, right_dim=0):
    return lax.dot_general(
        left,
        right,
        (((left_dim,), (right_dim,)), ((), ())),
        precision=lax.Precision.HIGHEST,
        preferred_element_type=jnp.float32,
    )


def dot_split(left, right):
    return dot16(left[0], right[0]) + (dot16(left[0], right[1]) + dot16(left[1], right[0]))


def seat_of(i, owner_ref, used):
    owner = owner_ref[i]
    rank = used[owner]
    used[owner] = rank + 1
    return owner, rank


def pack_kernel(
    count_ref, owner_ref, slot_ref, tiles_ref, early_ref, staged, header, used, slots, sems, out_sems
):
    scenes, capacity = used.shape[0], owner_ref.shape[0]
    for i in range(capacity):

        @pl.when(i < count_ref[0])
        def _():
            source = tiles_ref.at[i, pl.ds(0, EARLY)]
            pltpu.make_async_copy(source, staged.at[i], sems.at[i]).start()

    for seat in range(capacity):
        slots[seat] = -1
    for owner in range(scenes):
        used[owner] = 0

    def store(i, owner, rank):
        target = early_ref.at[owner, pl.ds(pl.multiple_of(rank * EARLY, 8), EARLY)]
        return pltpu.make_async_copy(staged.at[i], target, sems.at[i])

    for i in range(capacity):

        @pl.when(i < count_ref[0])
        def _():
            owner, rank = seat_of(i, owner_ref, used)
            slots[2 * owner + rank] = slot_ref[i]
            source = tiles_ref.at[i, pl.ds(0, EARLY)]
            pltpu.make_async_copy(source, staged.at[i], sems.at[i]).wait()
            store(i, owner, rank).start()

    lane = lax.broadcasted_iota(jnp.int32, header.shape[1:], 1)
    half = header.shape[2] // 2
    headers = []
    for owner in range(scenes):
        pair = jnp.where(lane < half, slots[2 * owner], slots[2 * owner + 1])
        header[owner] = pair.astype(jnp.float32)
        target = early_ref.at[owner, pl.ds(2 * EARLY, HEADER)]
        headers.append(pltpu.make_async_copy(header.at[owner], target, out_sems.at[owner]))
        headers[-1].start()
    for i in range(capacity):

        @pl.when(i < count_ref[0])
        def _():
            store(i, 0, 0).wait()

    for copy in headers:
        copy.wait()


def pack(tiles, tile_count, tile_owner, tile_slot, scenes):
    smem = pl.BlockSpec(memory_space=pltpu.SMEM)
    hbm = pl.BlockSpec(memory_space=pl.ANY)
    capacity, columns = tile_owner.shape[0], tiles.shape[2]
    return pl.pallas_call(
        pack_kernel,
        out_shape=jax.ShapeDtypeStruct((scenes, 2 * EARLY + HEADER, columns), tiles.dtype),
        in_specs=[smem, smem, smem, hbm],
        out_specs=hbm,
        scratch_shapes=[
            pltpu.VMEM((capacity, EARLY, columns), jnp.float32),
            pltpu.VMEM((scenes, HEADER, columns), jnp.float32),
            pltpu.SMEM((scenes,), jnp.int32),
            pltpu.SMEM((capacity,), jnp.int32),
            pltpu.SemaphoreType.DMA((capacity,)),
            pltpu.SemaphoreType.DMA((scenes,)),
        ],
        compiler_params=pltpu.CompilerParams(vmem_limit_bytes=56 << 20),
        cost_estimate=pl.CostEstimate(flops=0, bytes_accessed=8 << 20, transcendentals=0),
        name="pack",
    )(tile_count, tile_owner, tile_slot, tiles)


def gram_kernel(
    count_ref, owner_ref, tile_ref, inverse_ref, gram_ref, late_ref, inv_head, inv_tail, cross, used, sems
):
    step = pl.program_id(0)
    late = late_ref.shape[1] // 2

    def late_copy(i, owner, rank):
        target = late_ref.at[owner, pl.ds(pl.multiple_of(rank * late, 8), late)]
        return pltpu.make_async_copy(tile_ref.at[i, pl.ds(EARLY, late)], target, sems.at[i])

    @pl.when(step == 0)
    def _():
        head, tail = split(inverse_ref[...])
        inv_head[...] = head
        inv_tail[...] = tail
        gram_ref[...] = jnp.zeros_like(gram_ref)
        cross[...] = jnp.zeros_like(cross)
        for owner in range(used.shape[0]):
            used[owner] = 0

    tiles = tile_ref.shape[0]
    for i in range(tiles):

        @pl.when(tiles * step + i < count_ref[0])
        def _():
            owner, rank = seat_of(tiles * step + i, owner_ref, used)
            late_copy(i, owner, rank).start()

    @pl.when(tiles * step < count_ref[0])
    def _():
        live = [tile_ref[0]]
        for i in range(1, tiles):
            live.append(jnp.where(tiles * step + i < count_ref[0], tile_ref[i], 0.0))
        head, tail = split(jnp.concatenate(live, 0))
        left = dot_split(
            (head[:, :HALF], tail[:, :HALF]), (inv_head[:HALF, :HALF], inv_tail[:HALF, :HALF])
        )
        right = dot_split((head, tail), (inv_head[:, HALF:], inv_tail[:, HALF:]))
        left_head, left_tail = split(left)
        right_head, right_tail = split(right)
        gram_ref[:HALF, :] += dot16(left_head, left_head, 0, 0)
        cross[:HALF, :] += dot16(left_head, left_tail, 0, 0)
        gram_ref[HALF : 2 * HALF, :] += (
            dot16(left_head, right_head, 0, 0)
            + dot16(left_head, right_tail, 0, 0)
            + dot16(left_tail, right_head, 0, 0)
        )
        gram_ref[2 * HALF :, :] += dot16(right_head, right_head, 0, 0)
        cross[HALF:, :] += dot16(right_head, right_tail, 0, 0)

    for i in range(tiles):

        @pl.when(tiles * step + i < count_ref[0])
        def _():
            late_copy(i, 0, 0).wait()

    @pl.when(step == pl.num_programs(0) - 1)
    def _():
        gram_ref[:HALF, :] += cross[:HALF, :] + cross[:HALF, :].T
        gram_ref[2 * HALF :, :] += cross[HALF:, :] + cross[HALF:, :].T


def gram(tiles, inverse_factor, tile_count, tile_owner, scenes):
    capacity, rows, columns = tiles.shape
    return pl.pallas_call(
        gram_kernel,
        out_shape=(
            jax.ShapeDtypeStruct((3 * HALF, HALF), jnp.float32),
            jax.ShapeDtypeStruct((scenes, 2 * (rows - EARLY), columns), jnp.float32),
        ),
        grid_spec=pltpu.PrefetchScalarGridSpec(
            num_scalar_prefetch=2,
            grid=(capacity // GROUP,),
            in_specs=[
                pl.BlockSpec(
                    (GROUP, rows, columns),
                    lambda i, count, _: (
                        jnp.minimum(i, jnp.maximum(count[0] - 1, 0) // GROUP), 0, 0
                    ),
                ),
                pl.BlockSpec((columns, columns), lambda i, *_: (0, 0)),
            ],
            out_specs=(
                pl.BlockSpec((3 * HALF, HALF), lambda i, *_: (0, 0)),
                pl.BlockSpec(memory_space=pl.ANY),
            ),
            scratch_shapes=[
                pltpu.VMEM((columns, columns), jnp.bfloat16),
                pltpu.VMEM((columns, columns), jnp.bfloat16),
                pltpu.VMEM((2 * HALF, HALF), jnp.float32),
                pltpu.SMEM((scenes,), jnp.int32),
                pltpu.SemaphoreType.DMA((GROUP,)),
            ],
        ),
        compiler_params=pltpu.CompilerParams(
            dimension_semantics=("arbitrary",), vmem_limit_bytes=56 << 20
        ),
        cost_estimate=pl.CostEstimate(
            flops=1_000_000, bytes_accessed=1 << 16, transcendentals=0
        ),
        name="gram",
    )(tile_count, tile_owner, tiles, inverse_factor)


def ring_pairs(size, span, stride, shift):
    ring = [i // stride % span for i in range(size)]
    return [(i, i + ((r + shift) % span - r) * stride) for i, r in enumerate(ring)]


def scatter_sum(value, axis, span, stride):
    size = lax.axis_size(axis)
    me = lax.axis_index(axis) // stride % span
    parts = value.reshape((span, -1) + value.shape[1:])
    total = lax.dynamic_index_in_dim(parts, me, 0, keepdims=False)
    for shift in range(1, span):
        sent = lax.dynamic_index_in_dim(parts, (me + shift) % span, 0, keepdims=False)
        total = total + lax.ppermute(sent, axis, ring_pairs(size, span, stride, shift))
    return total


def select_one(tests, values):
    chosen = values[0]
    for test, value in zip(tests[1:], values[1:]):
        chosen = jnp.where(test, value, chosen)
    return chosen


def from_ahead(value, axis, span, stride):
    size = lax.axis_size(axis)
    return [value] + [
        lax.ppermute(value, axis, ring_pairs(size, span, stride, span - ahead))
        for ahead in range(1, span)
    ]


def in_order(ahead_values, axis, stride):
    span = len(ahead_values)
    me = lax.axis_index(axis) // stride % span
    return [
        select_one([(me + ahead) % span == place for ahead in range(span)], ahead_values)
        for place in range(span)
    ]


def gather(value, axis, span, stride):
    return jnp.concatenate(in_order(from_ahead(value, axis, span, stride), axis, stride), 0)


def reduction_stages(scenes, rows):
    side = 4
    return [("scene", 2, 1), ("rows", side, 1), ("rows", rows // side, side)]


def sum_along_z(value, scenes, rest):
    parts = from_ahead(value, "scene", scenes // 2, 2)
    rest, *parts = lax.optimization_barrier((rest, *parts))
    total, *more = in_order(parts, "scene", 2)
    for part in more:
        total = total + part
    return total, rest


def sweep(block):
    shape = (PIVOT, BLOCK)
    lane = lax.broadcasted_iota(jnp.int32, shape, 1)
    sub = lax.broadcasted_iota(jnp.int32, shape, 0)
    strips = [block[PIVOT * v : PIVOT * (v + 1), :] for v in range(BLOCK // PIVOT)]
    upper = []
    for s in range(len(strips)):
        base = PIVOT * s
        inside = (lane >= base) & (lane < base + PIVOT)
        own = [jnp.broadcast_to(strips[s][q : q + 1, :], shape) for q in range(PIVOT)]
        pivot = {
            (r, c): jnp.broadcast_to(own[r][:, base + c : base + c + 1], shape)
            for r in range(PIVOT)
            for c in range(r, PIVOT)
        }
        u = {}
        scale = []
        for q in range(PIVOT):
            scale.append(lax.rsqrt(pivot[q, q]))
            for c in range(q + 1, PIVOT):
                u[q, c] = pivot[q, c] * scale[q]
            for r in range(q + 1, PIVOT):
                for c in range(r, PIVOT):
                    pivot[r, c] = pivot[r, c] - u[q, r] * u[q, c]
        swept = [
            jnp.where(inside, jnp.where(lane == base + q, 1.0, 0.0), own[q]) for q in range(PIVOT)
        ]
        for q in range(PIVOT):
            for r in range(q):
                own[q] = own[q] - u[r, q] * own[r]
                swept[q] = swept[q] - u[r, q] * swept[r]
            own[q] = own[q] * scale[q]
            swept[q] = swept[q] * scale[q]
        for v in range(s + 1, len(strips)):
            column = []
            for q in range(PIVOT):
                entry = jnp.broadcast_to(strips[v][:, base + q : base + q + 1], shape)
                for r in range(q):
                    entry = entry - u[r, q] * column[r]
                column.append(entry * scale[q])
            rest = jnp.where(inside, 0.0, strips[v])
            for q in range(PIVOT):
                rest = rest - column[q] * swept[q]
            strips[v] = rest
        factor_rows, inverse_rows = own[0], swept[0]
        for q in range(1, PIVOT):
            factor_rows = jnp.where(sub == q, own[q], factor_rows)
            inverse_rows = jnp.where(sub == q, swept[q], inverse_rows)
        upper.append(jnp.where(lane >= base + sub, factor_rows, 0.0))
        strips[s] = jnp.where(lane <= base + sub, inverse_rows, 0.0)
    return jnp.concatenate(upper, 0), jnp.concatenate(strips, 0)


def factor_kernel(row_count, gram_ref, inverse_ref, factor_ref, head_ref, tail_ref, work):
    size = work.shape[0]
    work[:HALF, :HALF] = gram_ref[:HALF, :] / row_count
    work[:HALF, HALF:] = gram_ref[HALF : 2 * HALF, :] / row_count
    work[HALF:, HALF:] = gram_ref[2 * HALF :, :] / row_count
    work[HALF:, :HALF] = jnp.zeros((HALF, HALF), jnp.float32)

    @pl.loop(0, size // BLOCK)
    def _(k):
        offset = pl.multiple_of(k * BLOCK, BLOCK)
        here = pl.ds(offset, BLOCK)
        upper, inverse = sweep(work[here, here])
        right = dot32(inverse, work[here, :])
        lane = lax.broadcasted_iota(jnp.int32, (BLOCK, size), 1)
        beyond = jnp.where(lane >= offset + BLOCK, right, 0.0)
        factor_ref[here, :] = beyond
        factor_ref[here, here] = upper
        work[here, :] = right
        work[here, here] = inverse

        @pl.when(k < size // BLOCK - 1)
        def _():
            row = lax.broadcasted_iota(jnp.int32, (size, BLOCK), 0)
            work[:, here] = jnp.where(row >= offset + BLOCK, 0.0, work[:, here])
            work[...] = work[...] - dot32(beyond, work[here, :], 0, 0)

    row = lax.broadcasted_iota(jnp.int32, work.shape, 0)
    lane = lax.broadcasted_iota(jnp.int32, work.shape, 1)
    inverse = jnp.where(lane <= row, work[...], 0.0)
    head_ref[...], tail_ref[...] = split(dot32(inverse_ref[...], inverse, 1, 1))


def factor(gram_sum, inverse_factor, row_count):
    vmem = pl.BlockSpec(memory_space=pltpu.VMEM)
    size = inverse_factor.shape[0]
    return pl.pallas_call(
        functools.partial(factor_kernel, row_count),
        out_shape=(
            jax.ShapeDtypeStruct((size, size), jnp.float32),
            jax.ShapeDtypeStruct((size, size), jnp.bfloat16),
            jax.ShapeDtypeStruct((size, size), jnp.bfloat16),
        ),
        in_specs=[vmem, vmem],
        out_specs=(vmem, vmem, vmem),
        scratch_shapes=[pltpu.VMEM((size, size), jnp.float32)],
        compiler_params=pltpu.CompilerParams(vmem_limit_bytes=24 << 20),
        cost_estimate=pl.CostEstimate(
            flops=1_000_000, bytes_accessed=1 << 16, transcendentals=0
        ),
        name="factor",
    )(gram_sum, inverse_factor)


def finish_kernel(
    slot_ref, head_ref, tail_ref, early_ref, late_ref, out_ref, tiles, results, in_sems, out_sems
):
    late = late_ref.shape[1] // 2

    def fetch(owner, rank, slot):
        return (
            pltpu.make_async_copy(
                early_ref.at[owner, pl.ds(rank * EARLY, EARLY)],
                tiles.at[slot, pl.ds(0, EARLY)],
                in_sems.at[slot, 0],
            ),
            pltpu.make_async_copy(
                late_ref.at[owner, pl.ds(rank * late, late)],
                tiles.at[slot, pl.ds(EARLY, late)],
                in_sems.at[slot, 1],
            ),
        )

    for seat in range(slot_ref.shape[0]):
        slot = slot_ref[seat]

        @pl.when(slot >= 0)
        def _():
            for copy in fetch(seat // 2, seat % 2, slot):
                copy.start()

    def result_copy(j):
        return pltpu.make_async_copy(results.at[j], out_ref.at[j], out_sems.at[j])

    @pl.loop(0, OWN_TILES)
    def _(j):
        for copy in fetch(0, 0, j):
            copy.wait()
        head, tail = split(tiles[j])
        results[j, :, :HALF] = dot_split(
            (head[:, :HALF], tail[:, :HALF]), (head_ref[:HALF, :HALF], tail_ref[:HALF, :HALF])
        )
        results[j, :, HALF:] = dot_split((head, tail), (head_ref[:, HALF:], tail_ref[:, HALF:]))
        result_copy(j).start()

    @pl.loop(0, OWN_TILES)
    def _(j):
        result_copy(j).wait()


def finish(slots, early, late, head, tail):
    columns = early.shape[2]
    rows = EARLY + late.shape[1] // 2
    hbm = pl.BlockSpec(memory_space=pl.ANY)
    vmem = pl.BlockSpec(memory_space=pltpu.VMEM)
    return pl.pallas_call(
        finish_kernel,
        out_shape=jax.ShapeDtypeStruct((OWN_TILES, rows, columns), jnp.float32),
        in_specs=[pl.BlockSpec(memory_space=pltpu.SMEM), vmem, vmem, hbm, hbm],
        out_specs=hbm,
        scratch_shapes=[
            pltpu.VMEM((OWN_TILES, rows, columns), jnp.float32),
            pltpu.VMEM((OWN_TILES, rows, columns), jnp.float32),
            pltpu.SemaphoreType.DMA((OWN_TILES, 2)),
            pltpu.SemaphoreType.DMA((OWN_TILES,)),
        ],
        compiler_params=pltpu.CompilerParams(vmem_limit_bytes=32 << 20),
        cost_estimate=pl.CostEstimate(
            flops=5_000_000_000, bytes_accessed=8 << 20, transcendentals=0
        ),
        name="finish",
    )(slots, head, tail, early, late)


def shards(observations, inverse_factor, tile_count, tile_owner, tile_slot):
    scenes, rows = lax.axis_size("scene"), lax.axis_size("rows")
    tile_rows, columns = observations.shape[1:]

    def exchange(packed):
        return lax.all_to_all(packed, "scene", 0, 0, tiled=True)

    packed = pack(observations, tile_count, tile_owner, tile_slot, scenes)
    early = exchange(packed)
    tiles, _ = lax.optimization_barrier((observations, packed))
    value, rest = gram(tiles, inverse_factor, tile_count, tile_owner, scenes)
    stages = reduction_stages(scenes, rows)
    for axis, span, stride in stages:
        value = scatter_sum(value, axis, span, stride)
    value, rest = sum_along_z(value, scenes, rest)
    late = exchange(rest)
    for axis, span, stride in reversed(stages):
        value = gather(value, axis, span, stride)
    upper, head, tail = factor(value, inverse_factor, scenes * rows * OWN_TILES * tile_rows)
    slots = early[:, 2 * EARLY, :: columns // 2].astype(jnp.int32).reshape(-1)
    return finish(slots, early, late, head, tail), upper


def solution(mesh):
    in_specs = (
        P(("scene", "rows"), None, None),
        P(),
        P(("scene", "rows")),
        P(("scene", "rows")),
        P(("scene", "rows")),
    )
    out_specs = (P(("scene", "rows"), None, None), P())
    return jax.shard_map(shards, mesh=mesh, in_specs=in_specs, out_specs=out_specs, check_vma=False)
```

```python
import functools

import jax
import jax.numpy as jnp
from jax import lax
from jax.experimental import pallas as pl
from jax.experimental.pallas import tpu as pltpu
from jax.sharding import PartitionSpec as P

OWN_TILES = 8
BLOCK = 128
PIVOT = 8
HALF = 256
PAIR = 2
GROUP = 4


def split(value):
    head = value.astype(jnp.bfloat16)
    return head, (value - head.astype(jnp.float32)).astype(jnp.bfloat16)


def dot16(left, right, left_dim=1, right_dim=0):
    return lax.dot_general(
        left,
        right,
        (((left_dim,), (right_dim,)), ((), ())),
        preferred_element_type=jnp.float32,
    )


def dot32(left, right, left_dim=1, right_dim=0):
    return lax.dot_general(
        left,
        right,
        (((left_dim,), (right_dim,)), ((), ())),
        precision=lax.Precision.HIGHEST,
        preferred_element_type=jnp.float32,
    )


def dot_split(left, right):
    return dot16(left[0], right[0]) + (dot16(left[0], right[1]) + dot16(left[1], right[0]))


def seats_of_tiles(count_ref, owner_ref, used, note):
    me = lax.axis_index("scene")
    chips = used.shape[0] // 2
    for pair in range(used.shape[0]):
        used[pair] = 0
    for i in range(owner_ref.shape[0]):

        @pl.when(i < count_ref[0])
        def _():
            owner = owner_ref[i]
            up = lax.rem(owner // 2 - me // 2 + chips, chips)
            other = lax.rem(owner + me, 2)
            pair = 2 * up + other
            rank = used[pair]
            used[pair] = rank + 1
            note(i, pair, rank)


def pack_kernel(
    count_ref, owner_ref, slot_ref, tiles_ref, up_ref, down_ref, cross_ref, seat_ref, table_ref,
    staged, used, sems,
):
    capacity = owner_ref.shape[0]
    targets = {
        2: up_ref.at[0], 3: up_ref.at[1], 6: down_ref.at[0], 7: down_ref.at[1],
        1: cross_ref.at[0], 5: cross_ref.at[1],
    }
    for seat in range(capacity):
        table_ref[seat] = -1
        seat_ref[seat] = 0

    def note(i, pair, rank):
        seat_ref[i] = PAIR * pair + rank
        table_ref[PAIR * pair + rank] = slot_ref[i]

    seats_of_tiles(count_ref, owner_ref, used, note)

    def load(i):
        return pltpu.make_async_copy(tiles_ref.at[i], staged.at[i], sems.at[i])

    def store(i, target, rank):
        return pltpu.make_async_copy(staged.at[i], target.at[rank], sems.at[i])

    def sent(i):
        pair = seat_ref[i] // PAIR
        return (i < count_ref[0]) & (pair != 0) & (pair != 4)

    for i in range(capacity):

        @pl.when(sent(i))
        def _():
            load(i).start()

    for i in range(capacity):

        @pl.when(sent(i))
        def _():
            load(i).wait()
            for pair, target in targets.items():

                @pl.when(seat_ref[i] // PAIR == pair)
                def _():
                    store(i, target, lax.rem(seat_ref[i], PAIR)).start()

    for i in range(capacity):

        @pl.when(sent(i))
        def _():
            store(i, up_ref.at[0], 0).wait()


def pack(tiles, tile_count, tile_owner, tile_slot, scenes):
    smem = pl.BlockSpec(memory_space=pltpu.SMEM)
    hbm = pl.BlockSpec(memory_space=pl.ANY)
    capacity = tile_owner.shape[0]
    two_pairs = jax.ShapeDtypeStruct((2, PAIR) + tiles.shape[1:], tiles.dtype)
    table = jax.ShapeDtypeStruct((capacity,), jnp.int32)
    return pl.pallas_call(
        pack_kernel,
        out_shape=(two_pairs, two_pairs, two_pairs, table, table),
        in_specs=[smem, smem, smem, hbm],
        out_specs=(hbm, hbm, hbm, smem, smem),
        scratch_shapes=[
            pltpu.VMEM(tiles.shape, jnp.float32),
            pltpu.SMEM((scenes,), jnp.int32),
            pltpu.SemaphoreType.DMA((capacity,)),
        ],
        compiler_params=pltpu.CompilerParams(vmem_limit_bytes=56 << 20),
        cost_estimate=pl.CostEstimate(flops=0, bytes_accessed=8 << 20, transcendentals=0),
        name="pack",
    )(tile_count, tile_owner, tile_slot, tiles)


def gram_kernel(
    count_ref, seat_ref, tile_ref, inverse_ref, gram_ref, own_ref, far_ref, inv_head, inv_tail, cross, sems
):
    step = pl.program_id(0)
    tiles = tile_ref.shape[0]

    def kept(i, target, rank):
        return pltpu.make_async_copy(tile_ref.at[i], target.at[rank], sems.at[i])

    @pl.when(step == 0)
    def _():
        head, tail = split(inverse_ref[...])
        inv_head[...] = head
        inv_tail[...] = tail
        gram_ref[...] = jnp.zeros_like(gram_ref)
        cross[...] = jnp.zeros_like(cross)

    for i in range(tiles):
        for pair, target in ((0, own_ref), (4, far_ref.at[0])):
            seat = seat_ref[tiles * step + i]

            @pl.when((tiles * step + i < count_ref[0]) & (seat // PAIR == pair))
            def _():
                kept(i, target, lax.rem(seat, PAIR)).start()

    @pl.when(tiles * step < count_ref[0])
    def _():
        live = [tile_ref[0]]
        for i in range(1, tiles):
            live.append(jnp.where(tiles * step + i < count_ref[0], tile_ref[i], 0.0))
        head, tail = split(jnp.concatenate(live, 0))
        left = dot_split(
            (head[:, :HALF], tail[:, :HALF]), (inv_head[:HALF, :HALF], inv_tail[:HALF, :HALF])
        )
        right = dot_split((head, tail), (inv_head[:, HALF:], inv_tail[:, HALF:]))
        left_head, left_tail = split(left)
        right_head, right_tail = split(right)
        gram_ref[:HALF, :] += dot16(left_head, left_head, 0, 0)
        cross[:HALF, :] += dot16(left_head, left_tail, 0, 0)
        gram_ref[HALF : 2 * HALF, :] += (
            dot16(left_head, right_head, 0, 0)
            + dot16(left_head, right_tail, 0, 0)
            + dot16(left_tail, right_head, 0, 0)
        )
        gram_ref[2 * HALF :, :] += dot16(right_head, right_head, 0, 0)
        cross[HALF:, :] += dot16(right_head, right_tail, 0, 0)

    for i in range(tiles):
        pair = seat_ref[tiles * step + i] // PAIR

        @pl.when((tiles * step + i < count_ref[0]) & ((pair == 0) | (pair == 4)))
        def _():
            kept(i, own_ref, 0).wait()

    @pl.when(step == pl.num_programs(0) - 1)
    def _():
        gram_ref[:HALF, :] += cross[:HALF, :] + cross[:HALF, :].T
        gram_ref[2 * HALF :, :] += cross[HALF:, :] + cross[HALF:, :].T


def gram(tiles, inverse_factor, tile_count, seats):
    capacity, rows, columns = tiles.shape
    pair = jax.ShapeDtypeStruct((PAIR, rows, columns), jnp.float32)
    hbm = pl.BlockSpec(memory_space=pl.ANY)
    return pl.pallas_call(
        gram_kernel,
        out_shape=(
            jax.ShapeDtypeStruct((3 * HALF, HALF), jnp.float32),
            pair,
            jax.ShapeDtypeStruct((2, PAIR, rows, columns), jnp.float32),
        ),
        grid_spec=pltpu.PrefetchScalarGridSpec(
            num_scalar_prefetch=2,
            grid=(capacity // GROUP,),
            in_specs=[
                pl.BlockSpec(
                    (GROUP, rows, columns),
                    lambda i, count, _: (
                        jnp.minimum(i, jnp.maximum(count[0] - 1, 0) // GROUP), 0, 0
                    ),
                ),
                pl.BlockSpec((columns, columns), lambda i, *_: (0, 0)),
            ],
            out_specs=(
                pl.BlockSpec((3 * HALF, HALF), lambda i, *_: (0, 0)),
                hbm,
                hbm,
            ),
            scratch_shapes=[
                pltpu.VMEM((columns, columns), jnp.bfloat16),
                pltpu.VMEM((columns, columns), jnp.bfloat16),
                pltpu.VMEM((2 * HALF, HALF), jnp.float32),
                pltpu.SemaphoreType.DMA((GROUP,)),
            ],
        ),
        compiler_params=pltpu.CompilerParams(
            dimension_semantics=("arbitrary",), vmem_limit_bytes=56 << 20
        ),
        cost_estimate=pl.CostEstimate(
            flops=1_000_000, bytes_accessed=1 << 16, transcendentals=0
        ),
        name="gram",
    )(tile_count, seats, tiles, inverse_factor)


def ring_pairs(size, span, stride, shift):
    ring = [i // stride % span for i in range(size)]
    return [(i, i + ((r + shift) % span - r) * stride) for i, r in enumerate(ring)]


def scatter_sum(value, axis, span, stride):
    size = lax.axis_size(axis)
    me = lax.axis_index(axis) // stride % span
    parts = value.reshape((span, -1) + value.shape[1:])
    total = lax.dynamic_index_in_dim(parts, me, 0, keepdims=False)
    for shift in range(1, span):
        sent = lax.dynamic_index_in_dim(parts, (me + shift) % span, 0, keepdims=False)
        total = total + lax.ppermute(sent, axis, ring_pairs(size, span, stride, shift))
    return total


def select_one(tests, values):
    chosen = values[0]
    for test, value in zip(tests[1:], values[1:]):
        chosen = jnp.where(test, value, chosen)
    return chosen


def from_ahead(value, axis, span, stride):
    size = lax.axis_size(axis)
    return [value] + [
        lax.ppermute(value, axis, ring_pairs(size, span, stride, span - ahead))
        for ahead in range(1, span)
    ]


def in_order(ahead_values, axis, stride):
    span = len(ahead_values)
    me = lax.axis_index(axis) // stride % span
    return [
        select_one([(me + ahead) % span == place for ahead in range(span)], ahead_values)
        for place in range(span)
    ]


def gather(value, axis, span, stride):
    return jnp.concatenate(in_order(from_ahead(value, axis, span, stride), axis, stride), 0)


def reduction_stages(scenes, rows):
    side = 4
    return [("scene", 2, 1), ("rows", side, 1), ("rows", rows // side, side)]


def sum_in_order(ahead_values, axis, stride):
    total, *more = in_order(ahead_values, axis, stride)
    for value in more:
        total = total + value
    return total


def sweep(block):
    shape = (PIVOT, BLOCK)
    lane = lax.broadcasted_iota(jnp.int32, shape, 1)
    sub = lax.broadcasted_iota(jnp.int32, shape, 0)
    strips = [block[PIVOT * v : PIVOT * (v + 1), :] for v in range(BLOCK // PIVOT)]
    upper = []
    for s in range(len(strips)):
        base = PIVOT * s
        inside = (lane >= base) & (lane < base + PIVOT)
        own = [jnp.broadcast_to(strips[s][q : q + 1, :], shape) for q in range(PIVOT)]
        pivot = {
            (r, c): jnp.broadcast_to(own[r][:, base + c : base + c + 1], shape)
            for r in range(PIVOT)
            for c in range(r, PIVOT)
        }
        u = {}
        scale = []
        for q in range(PIVOT):
            scale.append(lax.rsqrt(pivot[q, q]))
            for c in range(q + 1, PIVOT):
                u[q, c] = pivot[q, c] * scale[q]
            for r in range(q + 1, PIVOT):
                for c in range(r, PIVOT):
                    pivot[r, c] = pivot[r, c] - u[q, r] * u[q, c]
        swept = [
            jnp.where(inside, jnp.where(lane == base + q, 1.0, 0.0), own[q]) for q in range(PIVOT)
        ]
        for q in range(PIVOT):
            for r in range(q):
                own[q] = own[q] - u[r, q] * own[r]
                swept[q] = swept[q] - u[r, q] * swept[r]
            own[q] = own[q] * scale[q]
            swept[q] = swept[q] * scale[q]
        for v in range(s + 1, len(strips)):
            column = []
            for q in range(PIVOT):
                entry = jnp.broadcast_to(strips[v][:, base + q : base + q + 1], shape)
                for r in range(q):
                    entry = entry - u[r, q] * column[r]
                column.append(entry * scale[q])
            rest = jnp.where(inside, 0.0, strips[v])
            for q in range(PIVOT):
                rest = rest - column[q] * swept[q]
            strips[v] = rest
        factor_rows, inverse_rows = own[0], swept[0]
        for q in range(1, PIVOT):
            factor_rows = jnp.where(sub == q, own[q], factor_rows)
            inverse_rows = jnp.where(sub == q, swept[q], inverse_rows)
        upper.append(jnp.where(lane >= base + sub, factor_rows, 0.0))
        strips[s] = jnp.where(lane <= base + sub, inverse_rows, 0.0)
    return jnp.concatenate(upper, 0), jnp.concatenate(strips, 0)


def factor_kernel(row_count, gram_ref, inverse_ref, factor_ref, head_ref, tail_ref, work):
    size = work.shape[0]
    work[:HALF, :HALF] = gram_ref[:HALF, :] / row_count
    work[:HALF, HALF:] = gram_ref[HALF : 2 * HALF, :] / row_count
    work[HALF:, HALF:] = gram_ref[2 * HALF :, :] / row_count
    work[HALF:, :HALF] = jnp.zeros((HALF, HALF), jnp.float32)

    @pl.loop(0, size // BLOCK)
    def _(k):
        offset = pl.multiple_of(k * BLOCK, BLOCK)
        here = pl.ds(offset, BLOCK)
        upper, inverse = sweep(work[here, here])
        right = dot32(inverse, work[here, :])
        lane = lax.broadcasted_iota(jnp.int32, (BLOCK, size), 1)
        beyond = jnp.where(lane >= offset + BLOCK, right, 0.0)
        factor_ref[here, :] = beyond
        factor_ref[here, here] = upper
        work[here, :] = right
        work[here, here] = inverse

        @pl.when(k < size // BLOCK - 1)
        def _():
            row = lax.broadcasted_iota(jnp.int32, (size, BLOCK), 0)
            work[:, here] = jnp.where(row >= offset + BLOCK, 0.0, work[:, here])
            work[...] = work[...] - dot32(beyond, work[here, :], 0, 0)

    row = lax.broadcasted_iota(jnp.int32, work.shape, 0)
    lane = lax.broadcasted_iota(jnp.int32, work.shape, 1)
    inverse = jnp.where(lane <= row, work[...], 0.0)
    head_ref[...], tail_ref[...] = split(dot32(inverse_ref[...], inverse, 1, 1))


def factor(gram_sum, inverse_factor, row_count):
    vmem = pl.BlockSpec(memory_space=pltpu.VMEM)
    size = inverse_factor.shape[0]
    return pl.pallas_call(
        functools.partial(factor_kernel, row_count),
        out_shape=(
            jax.ShapeDtypeStruct((size, size), jnp.float32),
            jax.ShapeDtypeStruct((size, size), jnp.bfloat16),
            jax.ShapeDtypeStruct((size, size), jnp.bfloat16),
        ),
        in_specs=[vmem, vmem],
        out_specs=(vmem, vmem, vmem),
        scratch_shapes=[pltpu.VMEM((size, size), jnp.float32)],
        compiler_params=pltpu.CompilerParams(vmem_limit_bytes=24 << 20),
        cost_estimate=pl.CostEstimate(
            flops=1_000_000, bytes_accessed=1 << 16, transcendentals=0
        ),
        name="factor",
    )(gram_sum, inverse_factor)


def finish_kernel(pairs, slot_ref, head_ref, tail_ref, *refs):
    out_ref, tiles, results, slots, in_sems, out_sems = refs[-6:]
    count = jnp.int32(0)
    for p, place in enumerate(pairs):
        source = refs[p].at[place] if place is not None else refs[p]
        for rank in range(PAIR):
            slot = slot_ref[PAIR * p + rank]

            @pl.when(slot >= 0)
            def _(source=source, rank=rank, slot=slot, count=count):
                slots[count] = slot
                pltpu.make_async_copy(source.at[rank], tiles.at[count], in_sems.at[count]).start()

            count = count + jnp.where(slot >= 0, 1, 0)

    def result_copy(j, slot):
        return pltpu.make_async_copy(results.at[j], out_ref.at[slot], out_sems.at[j])

    @pl.loop(0, count)
    def _(j):
        pltpu.make_async_copy(out_ref.at[0], tiles.at[j], in_sems.at[j]).wait()
        head, tail = split(tiles[j])
        results[j, :, :HALF] = dot_split(
            (head[:, :HALF], tail[:, :HALF]), (head_ref[:HALF, :HALF], tail_ref[:HALF, :HALF])
        )
        results[j, :, HALF:] = dot_split((head, tail), (head_ref[:, HALF:], tail_ref[:, HALF:]))
        result_copy(j, slots[j]).start()

    @pl.loop(0, count)
    def _(j):
        result_copy(j, 0).wait()


def finish(slots, head, tail, received, pairs, before, name):
    rows, columns = received[0].shape[-2:]
    most = min(PAIR * len(pairs), OWN_TILES)
    hbm = pl.BlockSpec(memory_space=pl.ANY)
    vmem = pl.BlockSpec(memory_space=pltpu.VMEM)
    operands = [slots, head, tail, *received] + ([] if before is None else [before])
    return pl.pallas_call(
        functools.partial(finish_kernel, pairs),
        out_shape=jax.ShapeDtypeStruct((OWN_TILES, rows, columns), jnp.float32),
        in_specs=[pl.BlockSpec(memory_space=pltpu.SMEM), vmem, vmem] + [hbm] * (len(operands) - 3),
        out_specs=hbm,
        input_output_aliases={} if before is None else {len(operands) - 1: 0},
        scratch_shapes=[
            pltpu.VMEM((most, rows, columns), jnp.float32),
            pltpu.VMEM((most, rows, columns), jnp.float32),
            pltpu.SMEM((most,), jnp.int32),
            pltpu.SemaphoreType.DMA((most,)),
            pltpu.SemaphoreType.DMA((most,)),
        ],
        compiler_params=pltpu.CompilerParams(vmem_limit_bytes=32 << 20),
        cost_estimate=pl.CostEstimate(
            flops=1_000_000, bytes_accessed=1 << 16, transcendentals=0
        ),
        name=name,
    )(*operands)


def shards(observations, inverse_factor, tile_count, tile_owner, tile_slot):
    scenes, rows = lax.axis_size("scene"), lax.axis_size("rows")
    tile_rows, columns = observations.shape[1:]
    chips = scenes // 2

    def along_z(value, up):
        return lax.ppermute(value, "scene", ring_pairs(scenes, chips, 2, up))

    def other_core(value):
        return lax.ppermute(value, "scene", ring_pairs(scenes, 2, 1, 1))

    up, down, cross, seats, table = pack(observations, tile_count, tile_owner, tile_slot, scenes)
    from_below, from_above = along_z(up, 1), along_z(down, chips - 1)
    crossed = other_core(cross)
    tiles, _ = lax.optimization_barrier((observations, seats))
    value, own, far = gram(tiles, inverse_factor, tile_count, seats)
    value, crossed = lax.optimization_barrier((value, crossed))
    mine = jnp.zeros((8, 128), jnp.float32).at[0, : table.shape[0]].set(table.astype(jnp.float32))
    tables = jnp.concatenate([mine, other_core(mine)], 1)
    stages = reduction_stages(scenes, rows)
    for axis, span, stride in stages:
        value = scatter_sum(value, axis, span, stride)
    height = value.shape[0]
    parts = from_ahead(jnp.concatenate([value, tables], 0), "scene", chips, 2)
    far = lax.dynamic_update_slice_in_dim(far, crossed[1:], 1, 0)
    *parts, far, from_below, from_above = lax.optimization_barrier(
        (*parts, far, from_below, from_above)
    )
    far_in = along_z(far, 2)
    value = sum_in_order([part[:height] for part in parts], "scene", 2)
    for axis, span, stride in reversed(stages):
        value = gather(value, axis, span, stride)
    passed_on = other_core(jnp.concatenate([from_below[1:], from_above[1:]], 0))
    upper, head, tail = factor(value, inverse_factor, scenes * rows * OWN_TILES * tile_rows)

    def slots_of(ahead, other):
        start = 128 * other + 2 * PAIR * ((chips - ahead) % chips) + PAIR * other
        return parts[ahead][height, start : start + PAIR]

    near = [(0, 0), (0, 1), (3, 0), (1, 0), (3, 1), (1, 1)]
    near_slots = jnp.concatenate([slots_of(*source) for source in near]).astype(jnp.int32)
    far_slots = jnp.concatenate([slots_of(2, 0), slots_of(2, 1)]).astype(jnp.int32)
    out = finish(
        near_slots,
        head,
        tail,
        [own, crossed, from_below, from_above, passed_on, passed_on],
        (None, 0, 0, 0, 0, 1),
        None,
        "finish_near",
    )
    return finish(far_slots, head, tail, [far_in, far_in], (0, 1), out, "finish_far"), upper


def solution(mesh):
    in_specs = (
        P(("scene", "rows"), None, None),
        P(),
        P(("scene", "rows")),
        P(("scene", "rows")),
        P(("scene", "rows")),
    )
    out_specs = (P(("scene", "rows"), None, None), P())
    return jax.shard_map(shards, mesh=mesh, in_specs=in_specs, out_specs=out_specs, check_vma=False)
```

```python
import functools

import jax
import jax.numpy as jnp
from jax import lax
from jax.experimental import pallas as pl
from jax.experimental.pallas import tpu as pltpu
from jax.sharding import PartitionSpec as P

OWN_TILES = 8
BLOCK = 128
PIVOT = 8
HALF = 256
PAIR = 2
GROUP = 4


def split(value):
    head = value.astype(jnp.bfloat16)
    return head, (value - head.astype(jnp.float32)).astype(jnp.bfloat16)


def dot16(left, right, left_dim=1, right_dim=0):
    return lax.dot_general(
        left,
        right,
        (((left_dim,), (right_dim,)), ((), ())),
        preferred_element_type=jnp.float32,
    )


def dot32(left, right, left_dim=1, right_dim=0):
    return lax.dot_general(
        left,
        right,
        (((left_dim,), (right_dim,)), ((), ())),
        precision=lax.Precision.HIGHEST,
        preferred_element_type=jnp.float32,
    )


def dot_split(left, right):
    return dot16(left[0], right[0]) + (dot16(left[0], right[1]) + dot16(left[1], right[0]))


def seats_of_tiles(count_ref, owner_ref, used, note):
    me = lax.axis_index("scene")
    chips = used.shape[0] // 2
    for pair in range(used.shape[0]):
        used[pair] = 0
    for i in range(owner_ref.shape[0]):

        @pl.when(i < count_ref[0])
        def _():
            owner = owner_ref[i]
            up = lax.rem(owner // 2 - me // 2 + chips, chips)
            other = lax.rem(owner + me, 2)
            pair = 2 * up + other
            rank = used[pair]
            used[pair] = rank + 1
            note(i, pair, rank)


def pack_kernel(
    count_ref, owner_ref, slot_ref, tiles_ref, up_ref, down_ref, cross_ref, seat_ref, table_ref,
    staged, used, sems,
):
    capacity = owner_ref.shape[0]
    targets = {
        2: up_ref.at[0], 3: up_ref.at[1], 6: down_ref.at[0], 7: down_ref.at[1],
        1: cross_ref.at[0], 5: cross_ref.at[1],
    }
    for seat in range(capacity):
        table_ref[seat] = -1
        seat_ref[seat] = 0

    def note(i, pair, rank):
        seat_ref[i] = PAIR * pair + rank
        table_ref[PAIR * pair + rank] = slot_ref[i]

    seats_of_tiles(count_ref, owner_ref, used, note)

    def load(i):
        return pltpu.make_async_copy(tiles_ref.at[i], staged.at[i], sems.at[i])

    def store(i, target, rank):
        return pltpu.make_async_copy(staged.at[i], target.at[rank], sems.at[i])

    def sent(i):
        pair = seat_ref[i] // PAIR
        return (i < count_ref[0]) & (pair != 0) & (pair != 4)

    for i in range(capacity):

        @pl.when(sent(i))
        def _():
            load(i).start()

    for i in range(capacity):

        @pl.when(sent(i))
        def _():
            load(i).wait()
            for pair, target in targets.items():

                @pl.when(seat_ref[i] // PAIR == pair)
                def _():
                    store(i, target, lax.rem(seat_ref[i], PAIR)).start()

    for i in range(capacity):

        @pl.when(sent(i))
        def _():
            store(i, up_ref.at[0], 0).wait()


def pack(tiles, tile_count, tile_owner, tile_slot, scenes):
    smem = pl.BlockSpec(memory_space=pltpu.SMEM)
    hbm = pl.BlockSpec(memory_space=pl.ANY)
    capacity = tile_owner.shape[0]
    two_pairs = jax.ShapeDtypeStruct((2, PAIR) + tiles.shape[1:], tiles.dtype)
    table = jax.ShapeDtypeStruct((capacity,), jnp.int32)
    return pl.pallas_call(
        pack_kernel,
        out_shape=(two_pairs, two_pairs, two_pairs, table, table),
        in_specs=[smem, smem, smem, hbm],
        out_specs=(hbm, hbm, hbm, smem, smem),
        scratch_shapes=[
            pltpu.VMEM(tiles.shape, jnp.float32),
            pltpu.SMEM((scenes,), jnp.int32),
            pltpu.SemaphoreType.DMA((capacity,)),
        ],
        compiler_params=pltpu.CompilerParams(vmem_limit_bytes=56 << 20),
        cost_estimate=pl.CostEstimate(flops=0, bytes_accessed=8 << 20, transcendentals=0),
        name="pack",
    )(tile_count, tile_owner, tile_slot, tiles)


def gram_kernel(
    count_ref, seat_ref, tile_ref, inverse_ref, gram_ref, own_ref, far_ref, inv_head, inv_tail, cross, sems
):
    step = pl.program_id(0)
    tiles = tile_ref.shape[0]

    def kept(i, target, rank):
        return pltpu.make_async_copy(tile_ref.at[i], target.at[rank], sems.at[i])

    @pl.when(step == 0)
    def _():
        head, tail = split(inverse_ref[...])
        inv_head[...] = head
        inv_tail[...] = tail
        gram_ref[...] = jnp.zeros_like(gram_ref)
        cross[...] = jnp.zeros_like(cross)

    for i in range(tiles):
        for pair, target in ((0, own_ref), (4, far_ref.at[0])):
            seat = seat_ref[tiles * step + i]

            @pl.when((tiles * step + i < count_ref[0]) & (seat // PAIR == pair))
            def _():
                kept(i, target, lax.rem(seat, PAIR)).start()

    @pl.when(tiles * step < count_ref[0])
    def _():
        live = [tile_ref[0]]
        for i in range(1, tiles):
            live.append(jnp.where(tiles * step + i < count_ref[0], tile_ref[i], 0.0))
        head, tail = split(jnp.concatenate(live, 0))
        left = dot_split(
            (head[:, :HALF], tail[:, :HALF]), (inv_head[:HALF, :HALF], inv_tail[:HALF, :HALF])
        )
        right = dot_split((head, tail), (inv_head[:, HALF:], inv_tail[:, HALF:]))
        left_head, left_tail = split(left)
        right_head, right_tail = split(right)
        gram_ref[:HALF, :] += dot16(left_head, left_head, 0, 0)
        cross[:HALF, :] += dot16(left_head, left_tail, 0, 0)
        gram_ref[HALF : 2 * HALF, :] += (
            dot16(left_head, right_head, 0, 0)
            + dot16(left_head, right_tail, 0, 0)
            + dot16(left_tail, right_head, 0, 0)
        )
        gram_ref[2 * HALF :, :] += dot16(right_head, right_head, 0, 0)
        cross[HALF:, :] += dot16(right_head, right_tail, 0, 0)

    for i in range(tiles):
        pair = seat_ref[tiles * step + i] // PAIR

        @pl.when((tiles * step + i < count_ref[0]) & ((pair == 0) | (pair == 4)))
        def _():
            kept(i, own_ref, 0).wait()

    @pl.when(step == pl.num_programs(0) - 1)
    def _():
        gram_ref[:HALF, :] += cross[:HALF, :] + cross[:HALF, :].T
        gram_ref[2 * HALF :, :] += cross[HALF:, :] + cross[HALF:, :].T


def gram(tiles, inverse_factor, tile_count, seats):
    capacity, rows, columns = tiles.shape
    pair = jax.ShapeDtypeStruct((PAIR, rows, columns), jnp.float32)
    hbm = pl.BlockSpec(memory_space=pl.ANY)
    return pl.pallas_call(
        gram_kernel,
        out_shape=(
            jax.ShapeDtypeStruct((3 * HALF, HALF), jnp.float32),
            pair,
            jax.ShapeDtypeStruct((2, PAIR, rows, columns), jnp.float32),
        ),
        grid_spec=pltpu.PrefetchScalarGridSpec(
            num_scalar_prefetch=2,
            grid=(capacity // GROUP,),
            in_specs=[
                pl.BlockSpec(
                    (GROUP, rows, columns),
                    lambda i, count, _: (
                        jnp.minimum(i, jnp.maximum(count[0] - 1, 0) // GROUP), 0, 0
                    ),
                ),
                pl.BlockSpec((columns, columns), lambda i, *_: (0, 0)),
            ],
            out_specs=(
                pl.BlockSpec((3 * HALF, HALF), lambda i, *_: (0, 0)),
                hbm,
                hbm,
            ),
            scratch_shapes=[
                pltpu.VMEM((columns, columns), jnp.bfloat16),
                pltpu.VMEM((columns, columns), jnp.bfloat16),
                pltpu.VMEM((2 * HALF, HALF), jnp.float32),
                pltpu.SemaphoreType.DMA((GROUP,)),
            ],
        ),
        compiler_params=pltpu.CompilerParams(
            dimension_semantics=("arbitrary",), vmem_limit_bytes=56 << 20
        ),
        cost_estimate=pl.CostEstimate(
            flops=1_000_000, bytes_accessed=1 << 16, transcendentals=0
        ),
        name="gram",
    )(tile_count, seats, tiles, inverse_factor)


def ring_pairs(size, span, stride, shift):
    ring = [i // stride % span for i in range(size)]
    return [(i, i + ((r + shift) % span - r) * stride) for i, r in enumerate(ring)]


def scatter_sum(value, axis, span, stride):
    size = lax.axis_size(axis)
    me = lax.axis_index(axis) // stride % span
    parts = value.reshape((span, -1) + value.shape[1:])
    total = lax.dynamic_index_in_dim(parts, me, 0, keepdims=False)
    for shift in range(1, span):
        sent = lax.dynamic_index_in_dim(parts, (me + shift) % span, 0, keepdims=False)
        total = total + lax.ppermute(sent, axis, ring_pairs(size, span, stride, shift))
    return total


def select_one(tests, values):
    chosen = values[0]
    for test, value in zip(tests[1:], values[1:]):
        chosen = jnp.where(test, value, chosen)
    return chosen


def from_ahead(value, axis, span, stride):
    size = lax.axis_size(axis)
    return [value] + [
        lax.ppermute(value, axis, ring_pairs(size, span, stride, span - ahead))
        for ahead in range(1, span)
    ]


def in_order(ahead_values, axis, stride):
    span = len(ahead_values)
    me = lax.axis_index(axis) // stride % span
    return [
        select_one([(me + ahead) % span == place for ahead in range(span)], ahead_values)
        for place in range(span)
    ]


def gather(value, axis, span, stride):
    return jnp.concatenate(in_order(from_ahead(value, axis, span, stride), axis, stride), 0)


def reduction_stages(scenes, rows):
    side = 4
    return [("scene", 2, 1), ("rows", side, 1), ("rows", rows // side, side)]


def sum_in_order(ahead_values, axis, stride):
    total, *more = in_order(ahead_values, axis, stride)
    for value in more:
        total = total + value
    return total


def sweep(block):
    shape = (PIVOT, BLOCK)
    lane = lax.broadcasted_iota(jnp.int32, shape, 1)
    sub = lax.broadcasted_iota(jnp.int32, shape, 0)
    strips = [block[PIVOT * v : PIVOT * (v + 1), :] for v in range(BLOCK // PIVOT)]
    upper = []
    for s in range(len(strips)):
        base = PIVOT * s
        inside = (lane >= base) & (lane < base + PIVOT)
        own = [jnp.broadcast_to(strips[s][q : q + 1, :], shape) for q in range(PIVOT)]
        pivot = {
            (r, c): jnp.broadcast_to(own[r][:, base + c : base + c + 1], shape)
            for r in range(PIVOT)
            for c in range(r, PIVOT)
        }
        u = {}
        scale = []
        for q in range(PIVOT):
            scale.append(lax.rsqrt(pivot[q, q]))
            for c in range(q + 1, PIVOT):
                u[q, c] = pivot[q, c] * scale[q]
            for r in range(q + 1, PIVOT):
                for c in range(r, PIVOT):
                    pivot[r, c] = pivot[r, c] - u[q, r] * u[q, c]
        swept = [
            jnp.where(inside, jnp.where(lane == base + q, 1.0, 0.0), own[q]) for q in range(PIVOT)
        ]
        for q in range(PIVOT):
            for r in range(q):
                own[q] = own[q] - u[r, q] * own[r]
                swept[q] = swept[q] - u[r, q] * swept[r]
            own[q] = own[q] * scale[q]
            swept[q] = swept[q] * scale[q]
        for v in range(s + 1, len(strips)):
            column = []
            for q in range(PIVOT):
                entry = jnp.broadcast_to(strips[v][:, base + q : base + q + 1], shape)
                for r in range(q):
                    entry = entry - u[r, q] * column[r]
                column.append(entry * scale[q])
            rest = jnp.where(inside, 0.0, strips[v])
            for q in range(PIVOT):
                rest = rest - column[q] * swept[q]
            strips[v] = rest
        factor_rows, inverse_rows = own[0], swept[0]
        for q in range(1, PIVOT):
            factor_rows = jnp.where(sub == q, own[q], factor_rows)
            inverse_rows = jnp.where(sub == q, swept[q], inverse_rows)
        upper.append(jnp.where(lane >= base + sub, factor_rows, 0.0))
        strips[s] = jnp.where(lane <= base + sub, inverse_rows, 0.0)
    return jnp.concatenate(upper, 0), jnp.concatenate(strips, 0)


def factor_kernel(row_count, inverse_ref, *refs):
    *pieces, factor_ref, head_ref, tail_ref, gram_ref, work = refs
    size = work.shape[0]
    core = lax.rem(lax.axis_index("scene"), 2)
    ring = len(pieces) // 2
    x = lax.rem(lax.axis_index("rows"), ring)
    height = pieces[0].shape[0]
    for i, piece in enumerate(pieces):
        half = core if i < ring else 1 - core
        row = (half * ring + lax.rem(x + i % ring, ring)) * height
        gram_ref[pl.ds(pl.multiple_of(row, 8), height), :] = piece[...]
    work[:HALF, :HALF] = gram_ref[:HALF, :] / row_count
    work[:HALF, HALF:] = gram_ref[HALF : 2 * HALF, :] / row_count
    work[HALF:, HALF:] = gram_ref[2 * HALF :, :] / row_count
    work[HALF:, :HALF] = jnp.zeros((HALF, HALF), jnp.float32)

    @pl.loop(0, size // BLOCK)
    def _(k):
        offset = pl.multiple_of(k * BLOCK, BLOCK)
        here = pl.ds(offset, BLOCK)
        upper, inverse = sweep(work[here, here])
        right = dot32(inverse, work[here, :])
        lane = lax.broadcasted_iota(jnp.int32, (BLOCK, size), 1)
        beyond = jnp.where(lane >= offset + BLOCK, right, 0.0)
        factor_ref[here, :] = beyond
        factor_ref[here, here] = upper
        work[here, :] = right
        work[here, here] = inverse

        @pl.when(k < size // BLOCK - 1)
        def _():
            row = lax.broadcasted_iota(jnp.int32, (size, BLOCK), 0)
            work[:, here] = jnp.where(row >= offset + BLOCK, 0.0, work[:, here])
            work[...] = work[...] - dot32(beyond, work[here, :], 0, 0)

    row = lax.broadcasted_iota(jnp.int32, work.shape, 0)
    lane = lax.broadcasted_iota(jnp.int32, work.shape, 1)
    inverse = jnp.where(lane <= row, work[...], 0.0)
    head_ref[...], tail_ref[...] = split(dot32(inverse_ref[...], inverse, 1, 1))


def factor(pieces, inverse_factor, row_count):
    vmem = pl.BlockSpec(memory_space=pltpu.VMEM)
    size = inverse_factor.shape[0]
    return pl.pallas_call(
        functools.partial(factor_kernel, row_count),
        out_shape=(
            jax.ShapeDtypeStruct((size, size), jnp.float32),
            jax.ShapeDtypeStruct((size, size), jnp.bfloat16),
            jax.ShapeDtypeStruct((size, size), jnp.bfloat16),
        ),
        in_specs=[vmem] * (1 + len(pieces)),
        out_specs=(vmem, vmem, vmem),
        scratch_shapes=[
            pltpu.VMEM((3 * HALF, HALF), jnp.float32),
            pltpu.VMEM((size, size), jnp.float32),
        ],
        compiler_params=pltpu.CompilerParams(vmem_limit_bytes=24 << 20),
        cost_estimate=pl.CostEstimate(
            flops=1_000_000, bytes_accessed=1 << 16, transcendentals=0
        ),
        name="factor",
    )(inverse_factor, *pieces)


def finish_kernel(places, slot_ref, head_ref, tail_ref, *refs):
    *received, out_ref, tiles, results, in_sems, out_sems = refs
    for p, place in enumerate(places):
        source = received[p] if place is None else received[p].at[place]
        for rank in range(PAIR):
            slot = slot_ref[PAIR * p + rank]

            @pl.when(slot >= 0)
            def _():
                pltpu.make_async_copy(source.at[rank], tiles.at[slot], in_sems.at[slot]).start()

    def result_copy(j):
        return pltpu.make_async_copy(results.at[j], out_ref.at[j], out_sems.at[j])

    rows, columns = tiles.shape[1:]
    for j in range(0, OWN_TILES, 2):
        for i in (j, j + 1):
            pltpu.make_async_copy(out_ref.at[i], tiles.at[i], in_sems.at[i]).wait()
        head, tail = split(tiles[j : j + 2].reshape(2 * rows, columns))
        left = dot_split(
            (head[:, :HALF], tail[:, :HALF]), (head_ref[:HALF, :HALF], tail_ref[:HALF, :HALF])
        )
        right = dot_split((head, tail), (head_ref[:, HALF:], tail_ref[:, HALF:]))
        results[j : j + 2, :, :HALF] = left.reshape(2, rows, HALF)
        results[j : j + 2, :, HALF:] = right.reshape(2, rows, HALF)
        for i in (j, j + 1):
            result_copy(i).start()

    for j in range(OWN_TILES):
        result_copy(j).wait()


def finish(slots, head, tail, received, places):
    rows, columns = received[0].shape[-2:]
    hbm = pl.BlockSpec(memory_space=pl.ANY)
    vmem = pl.BlockSpec(memory_space=pltpu.VMEM)
    return pl.pallas_call(
        functools.partial(finish_kernel, places),
        out_shape=jax.ShapeDtypeStruct((OWN_TILES, rows, columns), jnp.float32),
        in_specs=[pl.BlockSpec(memory_space=pltpu.SMEM), vmem, vmem] + [hbm] * len(received),
        out_specs=hbm,
        scratch_shapes=[
            pltpu.VMEM((OWN_TILES, rows, columns), jnp.float32),
            pltpu.VMEM((OWN_TILES, rows, columns), jnp.float32),
            pltpu.SemaphoreType.DMA((OWN_TILES,)),
            pltpu.SemaphoreType.DMA((OWN_TILES,)),
        ],
        compiler_params=pltpu.CompilerParams(vmem_limit_bytes=48 << 20),
        cost_estimate=pl.CostEstimate(
            flops=1_000_000, bytes_accessed=1 << 16, transcendentals=0
        ),
        name="finish",
    )(slots, head, tail, *received)


def second_pairs_kernel(first_ref, second_ref, out_ref, sems):
    copies = [
        pltpu.make_async_copy(ref.at[1], out_ref.at[i], sems.at[i])
        for i, ref in enumerate((first_ref, second_ref))
    ]
    for copy in copies:
        copy.start()
    for copy in copies:
        copy.wait()


def second_pairs(first, second):
    hbm = pl.BlockSpec(memory_space=pl.ANY)
    return pl.pallas_call(
        second_pairs_kernel,
        out_shape=jax.ShapeDtypeStruct(first.shape, first.dtype),
        in_specs=[hbm, hbm],
        out_specs=pl.BlockSpec(memory_space=pltpu.VMEM),
        scratch_shapes=[pltpu.SemaphoreType.DMA((2,))],
        cost_estimate=pl.CostEstimate(
            flops=1_000_000, bytes_accessed=1 << 16, transcendentals=0
        ),
        name="second_pairs",
    )(first, second)


def shards(observations, inverse_factor, tile_count, tile_owner, tile_slot):
    scenes, rows = lax.axis_size("scene"), lax.axis_size("rows")
    tile_rows, columns = observations.shape[1:]
    chips = scenes // 2

    def along_z(value, up):
        return lax.ppermute(value, "scene", ring_pairs(scenes, chips, 2, up))

    def other_core(value):
        return lax.ppermute(value, "scene", ring_pairs(scenes, 2, 1, 1))

    up, down, cross, seats, table = pack(observations, tile_count, tile_owner, tile_slot, scenes)
    from_below, from_above = along_z(up, 1), along_z(down, chips - 1)
    crossed = other_core(cross)
    tiles, _ = lax.optimization_barrier((observations, seats))
    value, own, far = gram(tiles, inverse_factor, tile_count, seats)
    value, crossed = lax.optimization_barrier((value, crossed))
    mine = jnp.zeros((8, 128), jnp.float32).at[0, : table.shape[0]].set(table.astype(jnp.float32))
    tables = jnp.concatenate([mine, other_core(mine)], 1)
    stages = reduction_stages(scenes, rows)
    for axis, span, stride in stages:
        value = scatter_sum(value, axis, span, stride)
    height = value.shape[0]
    parts = from_ahead(jnp.concatenate([value, tables], 0), "scene", chips, 2)
    far = lax.dynamic_update_slice_in_dim(far, crossed[1:], 1, 0)
    *parts, far, from_below, from_above = lax.optimization_barrier(
        (*parts, far, from_below, from_above)
    )
    far_in = along_z(far, 2)
    value = sum_in_order([part[:height] for part in parts], "scene", 2)
    (x_axis, x_span, x_stride), (y_axis, y_span, y_stride) = stages[1:]
    value = gather(value, y_axis, y_span, y_stride)
    pieces = from_ahead(value, x_axis, x_span, x_stride)
    pieces = pieces + [other_core(piece) for piece in pieces]
    passed_on = other_core(second_pairs(from_below, from_above))
    upper, head, tail = factor(pieces, inverse_factor, scenes * rows * OWN_TILES * tile_rows)

    def slots_of(ahead, other):
        start = 128 * other + 2 * PAIR * ((chips - ahead) % chips) + PAIR * other
        return parts[ahead][height, start : start + PAIR]

    sources = [(0, 0), (0, 1), (3, 0), (1, 0), (3, 1), (1, 1), (2, 0), (2, 1)]
    slots = jnp.concatenate([slots_of(*source) for source in sources]).astype(jnp.int32)
    received = [own, crossed, from_below, from_above, passed_on, passed_on, far_in, far_in]
    return finish(slots, head, tail, received, (None, 0, 0, 0, 0, 1, 0, 1)), upper


def solution(mesh):
    in_specs = (
        P(("scene", "rows"), None, None),
        P(),
        P(("scene", "rows")),
        P(("scene", "rows")),
        P(("scene", "rows")),
    )
    out_specs = (P(("scene", "rows"), None, None), P())
    return jax.shard_map(shards, mesh=mesh, in_specs=in_specs, out_specs=out_specs, check_vma=False)
```

```python
import functools

import jax
import jax.numpy as jnp
from jax import lax
from jax.experimental import pallas as pl
from jax.experimental.pallas import tpu as pltpu
from jax.sharding import PartitionSpec as P

OWN_TILES = 8
BLOCK = 128
PIVOT = 8
HALF = 256
PAIR = 2
GROUP = 4


def split(value):
    head = value.astype(jnp.bfloat16)
    return head, (value - head.astype(jnp.float32)).astype(jnp.bfloat16)


def dot16(left, right, left_dim=1, right_dim=0):
    return lax.dot_general(
        left,
        right,
        (((left_dim,), (right_dim,)), ((), ())),
        preferred_element_type=jnp.float32,
    )


def dot32(left, right, left_dim=1, right_dim=0):
    return lax.dot_general(
        left,
        right,
        (((left_dim,), (right_dim,)), ((), ())),
        precision=lax.Precision.HIGHEST,
        preferred_element_type=jnp.float32,
    )


def dot_split(left, right):
    return dot16(left[0], right[0]) + (dot16(left[0], right[1]) + dot16(left[1], right[0]))


def seats_of_tiles(count_ref, owner_ref, used, note):
    me = lax.axis_index("scene")
    chips = used.shape[0] // 2
    for pair in range(used.shape[0]):
        used[pair] = 0
    for i in range(owner_ref.shape[0]):

        @pl.when(i < count_ref[0])
        def _():
            owner = owner_ref[i]
            up = lax.rem(owner // 2 - me // 2 + chips, chips)
            other = lax.rem(owner + me, 2)
            pair = 2 * up + other
            rank = used[pair]
            used[pair] = rank + 1
            note(i, pair, rank)


def pack_kernel(
    count_ref, owner_ref, slot_ref, tiles_ref, up_ref, down_ref, cross_ref, seat_ref, table_ref,
    staged, used, sems,
):
    capacity = owner_ref.shape[0]
    targets = {
        2: up_ref.at[0], 3: up_ref.at[1], 6: down_ref.at[0], 7: down_ref.at[1],
        1: cross_ref.at[0], 5: cross_ref.at[1],
    }
    for seat in range(capacity):
        table_ref[seat] = -1
        seat_ref[seat] = 0

    def note(i, pair, rank):
        seat_ref[i] = PAIR * pair + rank
        table_ref[PAIR * pair + rank] = slot_ref[i]

    seats_of_tiles(count_ref, owner_ref, used, note)

    def load(i):
        return pltpu.make_async_copy(tiles_ref.at[i], staged.at[i], sems.at[i])

    def store(i, target, rank):
        return pltpu.make_async_copy(staged.at[i], target.at[rank], sems.at[i])

    def sent(i):
        pair = seat_ref[i] // PAIR
        return (i < count_ref[0]) & (pair != 0) & (pair != 4)

    for i in range(capacity):

        @pl.when(sent(i))
        def _():
            load(i).start()

    for i in range(capacity):

        @pl.when(sent(i))
        def _():
            load(i).wait()
            for pair, target in targets.items():

                @pl.when(seat_ref[i] // PAIR == pair)
                def _():
                    store(i, target, lax.rem(seat_ref[i], PAIR)).start()

    for i in range(capacity):

        @pl.when(sent(i))
        def _():
            store(i, up_ref.at[0], 0).wait()


def pack(tiles, tile_count, tile_owner, tile_slot, scenes):
    smem = pl.BlockSpec(memory_space=pltpu.SMEM)
    hbm = pl.BlockSpec(memory_space=pl.ANY)
    capacity = tile_owner.shape[0]
    two_pairs = jax.ShapeDtypeStruct((2, PAIR) + tiles.shape[1:], tiles.dtype)
    table = jax.ShapeDtypeStruct((capacity,), jnp.int32)
    return pl.pallas_call(
        pack_kernel,
        out_shape=(two_pairs, two_pairs, two_pairs, table, table),
        in_specs=[smem, smem, smem, hbm],
        out_specs=(hbm, hbm, hbm, smem, smem),
        scratch_shapes=[
            pltpu.VMEM(tiles.shape, jnp.float32),
            pltpu.SMEM((scenes,), jnp.int32),
            pltpu.SemaphoreType.DMA((capacity,)),
        ],
        compiler_params=pltpu.CompilerParams(vmem_limit_bytes=56 << 20),
        cost_estimate=pl.CostEstimate(flops=0, bytes_accessed=8 << 20, transcendentals=0),
        name="pack",
    )(tile_count, tile_owner, tile_slot, tiles)


def gram_kernel(
    count_ref, seat_ref, tile_ref, inverse_ref, gram_ref, own_ref, far_ref, inv_head, inv_tail, cross, sems
):
    step = pl.program_id(0)
    tiles = tile_ref.shape[0]

    def kept(i, target, rank):
        return pltpu.make_async_copy(tile_ref.at[i], target.at[rank], sems.at[i])

    @pl.when(step == 0)
    def _():
        head, tail = split(inverse_ref[...])
        inv_head[...] = head
        inv_tail[...] = tail
        gram_ref[...] = jnp.zeros_like(gram_ref)
        cross[...] = jnp.zeros_like(cross)

    for i in range(tiles):
        for pair, target in ((0, own_ref), (4, far_ref.at[0])):
            seat = seat_ref[tiles * step + i]

            @pl.when((tiles * step + i < count_ref[0]) & (seat // PAIR == pair))
            def _():
                kept(i, target, lax.rem(seat, PAIR)).start()

    @pl.when(tiles * step < count_ref[0])
    def _():
        live = [tile_ref[0]]
        for i in range(1, tiles):
            live.append(jnp.where(tiles * step + i < count_ref[0], tile_ref[i], 0.0))
        head, tail = split(jnp.concatenate(live, 0))
        left = dot_split(
            (head[:, :HALF], tail[:, :HALF]), (inv_head[:HALF, :HALF], inv_tail[:HALF, :HALF])
        )
        right = dot_split((head, tail), (inv_head[:, HALF:], inv_tail[:, HALF:]))
        left_head, left_tail = split(left)
        right_head, right_tail = split(right)
        gram_ref[:HALF, :] += dot16(left_head, left_head, 0, 0)
        cross[:HALF, :] += dot16(left_head, left_tail, 0, 0)
        gram_ref[HALF : 2 * HALF, :] += (
            dot16(left_head, right_head, 0, 0)
            + dot16(left_head, right_tail, 0, 0)
            + dot16(left_tail, right_head, 0, 0)
        )
        gram_ref[2 * HALF :, :] += dot16(right_head, right_head, 0, 0)
        cross[HALF:, :] += dot16(right_head, right_tail, 0, 0)

    for i in range(tiles):
        pair = seat_ref[tiles * step + i] // PAIR

        @pl.when((tiles * step + i < count_ref[0]) & ((pair == 0) | (pair == 4)))
        def _():
            kept(i, own_ref, 0).wait()

    @pl.when(step == pl.num_programs(0) - 1)
    def _():
        gram_ref[:HALF, :] += cross[:HALF, :] + cross[:HALF, :].T
        gram_ref[2 * HALF :, :] += cross[HALF:, :] + cross[HALF:, :].T


def gram(tiles, inverse_factor, tile_count, seats):
    capacity, rows, columns = tiles.shape
    pair = jax.ShapeDtypeStruct((PAIR, rows, columns), jnp.float32)
    hbm = pl.BlockSpec(memory_space=pl.ANY)
    return pl.pallas_call(
        gram_kernel,
        out_shape=(
            jax.ShapeDtypeStruct((3 * HALF, HALF), jnp.float32),
            pair,
            jax.ShapeDtypeStruct((2, PAIR, rows, columns), jnp.float32),
        ),
        grid_spec=pltpu.PrefetchScalarGridSpec(
            num_scalar_prefetch=2,
            grid=(capacity // GROUP,),
            in_specs=[
                pl.BlockSpec(
                    (GROUP, rows, columns),
                    lambda i, count, _: (
                        jnp.minimum(i, jnp.maximum(count[0] - 1, 0) // GROUP), 0, 0
                    ),
                ),
                pl.BlockSpec((columns, columns), lambda i, *_: (0, 0)),
            ],
            out_specs=(
                pl.BlockSpec((3 * HALF, HALF), lambda i, *_: (0, 0)),
                hbm,
                hbm,
            ),
            scratch_shapes=[
                pltpu.VMEM((columns, columns), jnp.bfloat16),
                pltpu.VMEM((columns, columns), jnp.bfloat16),
                pltpu.VMEM((2 * HALF, HALF), jnp.float32),
                pltpu.SemaphoreType.DMA((GROUP,)),
            ],
        ),
        compiler_params=pltpu.CompilerParams(
            dimension_semantics=("arbitrary",), vmem_limit_bytes=56 << 20
        ),
        cost_estimate=pl.CostEstimate(
            flops=1_000_000, bytes_accessed=1 << 16, transcendentals=0
        ),
        name="gram",
    )(tile_count, seats, tiles, inverse_factor)


def ring_pairs(size, span, stride, shift):
    ring = [i // stride % span for i in range(size)]
    return [(i, i + ((r + shift) % span - r) * stride) for i, r in enumerate(ring)]


def scatter_sum(value, axis, span, stride):
    size = lax.axis_size(axis)
    me = lax.axis_index(axis) // stride % span
    parts = value.reshape((span, -1) + value.shape[1:])
    total = lax.dynamic_index_in_dim(parts, me, 0, keepdims=False)
    for shift in range(1, span):
        sent = lax.dynamic_index_in_dim(parts, (me + shift) % span, 0, keepdims=False)
        total = total + lax.ppermute(sent, axis, ring_pairs(size, span, stride, shift))
    return total


def select_one(tests, values):
    chosen = values[0]
    for test, value in zip(tests[1:], values[1:]):
        chosen = jnp.where(test, value, chosen)
    return chosen


def from_ahead(value, axis, span, stride):
    size = lax.axis_size(axis)
    return [value] + [
        lax.ppermute(value, axis, ring_pairs(size, span, stride, span - ahead))
        for ahead in range(1, span)
    ]


def in_order(ahead_values, axis, stride):
    span = len(ahead_values)
    me = lax.axis_index(axis) // stride % span
    return [
        select_one([(me + ahead) % span == place for ahead in range(span)], ahead_values)
        for place in range(span)
    ]


def gather(value, axis, span, stride):
    return jnp.concatenate(in_order(from_ahead(value, axis, span, stride), axis, stride), 0)


def reduction_stages(scenes, rows):
    side = 4
    return [("scene", 2, 1), ("rows", side, 1), ("rows", rows // side, side)]


def sum_in_order(ahead_values, axis, stride):
    total, *more = in_order(ahead_values, axis, stride)
    for value in more:
        total = total + value
    return total


def sweep(block):
    shape = (PIVOT, BLOCK)
    lane = lax.broadcasted_iota(jnp.int32, shape, 1)
    sub = lax.broadcasted_iota(jnp.int32, shape, 0)
    strips = [block[PIVOT * v : PIVOT * (v + 1), :] for v in range(BLOCK // PIVOT)]
    upper = []
    for s in range(len(strips)):
        base = PIVOT * s
        inside = (lane >= base) & (lane < base + PIVOT)
        own = [jnp.broadcast_to(strips[s][q : q + 1, :], shape) for q in range(PIVOT)]
        pivot = {
            (r, c): jnp.broadcast_to(own[r][:, base + c : base + c + 1], shape)
            for r in range(PIVOT)
            for c in range(r, PIVOT)
        }
        u = {}
        scale = []
        for q in range(PIVOT):
            scale.append(lax.rsqrt(pivot[q, q]))
            for c in range(q + 1, PIVOT):
                u[q, c] = pivot[q, c] * scale[q]
            for r in range(q + 1, PIVOT):
                for c in range(r, PIVOT):
                    pivot[r, c] = pivot[r, c] - u[q, r] * u[q, c]
        swept = [
            jnp.where(inside, jnp.where(lane == base + q, 1.0, 0.0), own[q]) for q in range(PIVOT)
        ]
        for q in range(PIVOT):
            for r in range(q):
                own[q] = own[q] - u[r, q] * own[r]
                swept[q] = swept[q] - u[r, q] * swept[r]
            own[q] = own[q] * scale[q]
            swept[q] = swept[q] * scale[q]
        for v in range(s + 1, len(strips)):
            column = []
            for q in range(PIVOT):
                entry = jnp.broadcast_to(strips[v][:, base + q : base + q + 1], shape)
                for r in range(q):
                    entry = entry - u[r, q] * column[r]
                column.append(entry * scale[q])
            rest = jnp.where(inside, 0.0, strips[v])
            for q in range(PIVOT):
                rest = rest - column[q] * swept[q]
            strips[v] = rest
        factor_rows, inverse_rows = own[0], swept[0]
        for q in range(1, PIVOT):
            factor_rows = jnp.where(sub == q, own[q], factor_rows)
            inverse_rows = jnp.where(sub == q, swept[q], inverse_rows)
        upper.append(jnp.where(lane >= base + sub, factor_rows, 0.0))
        strips[s] = jnp.where(lane <= base + sub, inverse_rows, 0.0)
    return jnp.concatenate(upper, 0), jnp.concatenate(strips, 0)


def factor_kernel(row_count, inverse_ref, *refs):
    *pieces, factor_ref, head_ref, tail_ref, gram_ref, work = refs
    size = work.shape[0]
    core = lax.rem(lax.axis_index("scene"), 2)
    ring = len(pieces) // 2
    x = lax.rem(lax.axis_index("rows"), ring)
    height = pieces[0].shape[0]
    for i, piece in enumerate(pieces):
        half = core if i < ring else 1 - core
        row = (half * ring + lax.rem(x + i % ring, ring)) * height
        gram_ref[pl.ds(pl.multiple_of(row, 8), height), :] = piece[...]
    work[:HALF, :HALF] = gram_ref[:HALF, :] / row_count
    work[:HALF, HALF:] = gram_ref[HALF : 2 * HALF, :] / row_count
    work[HALF:, HALF:] = gram_ref[2 * HALF :, :] / row_count
    work[HALF:, :HALF] = jnp.zeros((HALF, HALF), jnp.float32)

    @pl.loop(0, size // BLOCK)
    def _(k):
        offset = pl.multiple_of(k * BLOCK, BLOCK)
        here = pl.ds(offset, BLOCK)
        upper, inverse = sweep(work[here, here])
        right = dot32(inverse, work[here, :])
        lane = lax.broadcasted_iota(jnp.int32, (BLOCK, size), 1)
        beyond = jnp.where(lane >= offset + BLOCK, right, 0.0)
        factor_ref[here, :] = beyond
        factor_ref[here, here] = upper
        work[here, :] = right
        work[here, here] = inverse

        @pl.when(k < size // BLOCK - 1)
        def _():
            row = lax.broadcasted_iota(jnp.int32, (size, BLOCK), 0)
            work[:, here] = jnp.where(row >= offset + BLOCK, 0.0, work[:, here])
            work[...] = work[...] - dot32(beyond, work[here, :], 0, 0)

    row = lax.broadcasted_iota(jnp.int32, work.shape, 0)
    lane = lax.broadcasted_iota(jnp.int32, work.shape, 1)
    inverse = jnp.where(lane <= row, work[...], 0.0)
    head_ref[...], tail_ref[...] = split(dot32(inverse_ref[...], inverse, 1, 1))


def factor(pieces, inverse_factor, row_count):
    vmem = pl.BlockSpec(memory_space=pltpu.VMEM)
    size = inverse_factor.shape[0]
    return pl.pallas_call(
        functools.partial(factor_kernel, row_count),
        out_shape=(
            jax.ShapeDtypeStruct((size, size), jnp.float32),
            jax.ShapeDtypeStruct((size, size), jnp.bfloat16),
            jax.ShapeDtypeStruct((size, size), jnp.bfloat16),
        ),
        in_specs=[vmem] * (1 + len(pieces)),
        out_specs=(vmem, vmem, vmem),
        scratch_shapes=[
            pltpu.VMEM((3 * HALF, HALF), jnp.float32),
            pltpu.VMEM((size, size), jnp.float32),
        ],
        compiler_params=pltpu.CompilerParams(vmem_limit_bytes=24 << 20),
        cost_estimate=pl.CostEstimate(
            flops=1_000_000, bytes_accessed=1 << 16, transcendentals=0
        ),
        name="factor",
    )(inverse_factor, *pieces)


def finish_kernel(pairs, slot_ref, head_ref, tail_ref, *refs):
    out_ref, tiles, results, slots, in_sems, out_sems = refs[-6:]
    count = jnp.int32(0)
    for p, place in enumerate(pairs):
        source = refs[p].at[place] if place is not None else refs[p]
        for rank in range(PAIR):
            slot = slot_ref[PAIR * p + rank]

            @pl.when(slot >= 0)
            def _(source=source, rank=rank, slot=slot, count=count):
                slots[count] = slot
                pltpu.make_async_copy(source.at[rank], tiles.at[count], in_sems.at[count]).start()

            count = count + jnp.where(slot >= 0, 1, 0)

    def result_copy(j, slot):
        return pltpu.make_async_copy(results.at[j], out_ref.at[slot], out_sems.at[j])

    @pl.loop(0, count)
    def _(j):
        pltpu.make_async_copy(out_ref.at[0], tiles.at[j], in_sems.at[j]).wait()
        head, tail = split(tiles[j])
        results[j, :, :HALF] = dot_split(
            (head[:, :HALF], tail[:, :HALF]), (head_ref[:HALF, :HALF], tail_ref[:HALF, :HALF])
        )
        results[j, :, HALF:] = dot_split((head, tail), (head_ref[:, HALF:], tail_ref[:, HALF:]))
        result_copy(j, slots[j]).start()

    @pl.loop(0, count)
    def _(j):
        result_copy(j, 0).wait()


def finish(slots, head, tail, received, pairs, before, name):
    rows, columns = received[0].shape[-2:]
    most = min(PAIR * len(pairs), OWN_TILES)
    hbm = pl.BlockSpec(memory_space=pl.ANY)
    vmem = pl.BlockSpec(memory_space=pltpu.VMEM)
    operands = [slots, head, tail, *received] + ([] if before is None else [before])
    return pl.pallas_call(
        functools.partial(finish_kernel, pairs),
        out_shape=jax.ShapeDtypeStruct((OWN_TILES, rows, columns), jnp.float32),
        in_specs=[pl.BlockSpec(memory_space=pltpu.SMEM), vmem, vmem] + [hbm] * (len(operands) - 3),
        out_specs=hbm,
        input_output_aliases={} if before is None else {len(operands) - 1: 0},
        scratch_shapes=[
            pltpu.VMEM((most, rows, columns), jnp.float32),
            pltpu.VMEM((most, rows, columns), jnp.float32),
            pltpu.SMEM((most,), jnp.int32),
            pltpu.SemaphoreType.DMA((most,)),
            pltpu.SemaphoreType.DMA((most,)),
        ],
        compiler_params=pltpu.CompilerParams(vmem_limit_bytes=24 << 20),
        cost_estimate=pl.CostEstimate(
            flops=1_000_000, bytes_accessed=1 << 16, transcendentals=0
        ),
        name=name,
    )(*operands)


def second_pairs_kernel(first_ref, second_ref, out_ref, sems):
    copies = [
        pltpu.make_async_copy(ref.at[1], out_ref.at[i], sems.at[i])
        for i, ref in enumerate((first_ref, second_ref))
    ]
    for copy in copies:
        copy.start()
    for copy in copies:
        copy.wait()


def second_pairs(first, second):
    hbm = pl.BlockSpec(memory_space=pl.ANY)
    return pl.pallas_call(
        second_pairs_kernel,
        out_shape=jax.ShapeDtypeStruct(first.shape, first.dtype),
        in_specs=[hbm, hbm],
        out_specs=pl.BlockSpec(memory_space=pltpu.VMEM),
        scratch_shapes=[pltpu.SemaphoreType.DMA((2,))],
        cost_estimate=pl.CostEstimate(
            flops=1_000_000, bytes_accessed=1 << 16, transcendentals=0
        ),
        name="second_pairs",
    )(first, second)


def shards(observations, inverse_factor, tile_count, tile_owner, tile_slot):
    scenes, rows = lax.axis_size("scene"), lax.axis_size("rows")
    tile_rows, columns = observations.shape[1:]
    chips = scenes // 2

    def along_z(value, up):
        return lax.ppermute(value, "scene", ring_pairs(scenes, chips, 2, up))

    def other_core(value):
        return lax.ppermute(value, "scene", ring_pairs(scenes, 2, 1, 1))

    up, down, cross, seats, table = pack(observations, tile_count, tile_owner, tile_slot, scenes)
    from_below, from_above = along_z(up, 1), along_z(down, chips - 1)
    crossed = other_core(cross)
    tiles, _ = lax.optimization_barrier((observations, seats))
    value, own, far = gram(tiles, inverse_factor, tile_count, seats)
    value, crossed = lax.optimization_barrier((value, crossed))
    mine = jnp.zeros((8, 128), jnp.float32).at[0, : table.shape[0]].set(table.astype(jnp.float32))
    tables = jnp.concatenate([mine, other_core(mine)], 1)
    stages = reduction_stages(scenes, rows)
    for axis, span, stride in stages:
        value = scatter_sum(value, axis, span, stride)
    height = value.shape[0]
    parts = from_ahead(jnp.concatenate([value, tables], 0), "scene", chips, 2)
    far = lax.dynamic_update_slice_in_dim(far, crossed[1:], 1, 0)
    *parts, far, from_below, from_above = lax.optimization_barrier(
        (*parts, far, from_below, from_above)
    )
    far_in = along_z(far, 2)
    value = sum_in_order([part[:height] for part in parts], "scene", 2)

    def slots_of(ahead, other):
        start = 128 * other + 2 * PAIR * ((chips - ahead) % chips) + PAIR * other
        return parts[ahead][height, start : start + PAIR]

    sources = [(0, 0), (0, 1), (3, 0), (1, 0), (3, 1), (1, 1), (2, 0), (2, 1)]
    slots = jnp.concatenate([slots_of(*source) for source in sources]).astype(jnp.int32)
    value, from_below, from_above = lax.optimization_barrier((value, from_below, from_above))
    passed_on = other_core(second_pairs(from_below, from_above))
    (x_axis, x_span, x_stride), (y_axis, y_span, y_stride) = stages[1:]
    value = gather(value, y_axis, y_span, y_stride)
    value, slots = lax.optimization_barrier((value, slots))
    pieces = from_ahead(value, x_axis, x_span, x_stride)
    pieces = pieces + [other_core(piece) for piece in pieces]
    upper, head, tail = factor(pieces, inverse_factor, scenes * rows * OWN_TILES * tile_rows)
    near = [own, crossed, from_below, from_above, passed_on, passed_on]
    first = PAIR * len(near)
    out = finish(slots[:first], head, tail, near, (None, 0, 0, 0, 0, 1), None, "finish_near")
    far = [far_in, far_in]
    return finish(slots[first:], head, tail, far, (0, 1), out, "finish_far"), upper


def solution(mesh):
    in_specs = (
        P(("scene", "rows"), None, None),
        P(),
        P(("scene", "rows")),
        P(("scene", "rows")),
        P(("scene", "rows")),
    )
    out_specs = (P(("scene", "rows"), None, None), P())
    return jax.shard_map(shards, mesh=mesh, in_specs=in_specs, out_specs=out_specs, check_vma=False)
```

```python
import functools

import jax
import jax.numpy as jnp
from jax import lax
from jax.experimental import pallas as pl
from jax.experimental.pallas import tpu as pltpu
from jax.sharding import PartitionSpec as P

OWN_TILES = 8
BLOCK = 128
PIVOT = 8
HALF = 256
PAIR = 2
GROUP = 4


def split(value):
    head = value.astype(jnp.bfloat16)
    return head, (value - head.astype(jnp.float32)).astype(jnp.bfloat16)


def dot16(left, right, left_dim=1, right_dim=0):
    return lax.dot_general(
        left,
        right,
        (((left_dim,), (right_dim,)), ((), ())),
        preferred_element_type=jnp.float32,
    )


def dot32(left, right, left_dim=1, right_dim=0):
    return lax.dot_general(
        left,
        right,
        (((left_dim,), (right_dim,)), ((), ())),
        precision=lax.Precision.HIGHEST,
        preferred_element_type=jnp.float32,
    )


def dot_split(left, right):
    return dot16(left[0], right[0]) + (dot16(left[0], right[1]) + dot16(left[1], right[0]))


def seats_of_tiles(count_ref, owner_ref, used, note):
    me = lax.axis_index("scene")
    chips = used.shape[0] // 2
    for pair in range(used.shape[0]):
        used[pair] = 0
    for i in range(owner_ref.shape[0]):

        @pl.when(i < count_ref[0])
        def _():
            owner = owner_ref[i]
            up = lax.rem(owner // 2 - me // 2 + chips, chips)
            other = lax.rem(owner + me, 2)
            pair = 2 * up + other
            rank = used[pair]
            used[pair] = rank + 1
            note(i, pair, rank)


def pack_kernel(
    count_ref, owner_ref, slot_ref, tiles_ref, up_ref, down_ref, cross_ref, seat_ref, table_ref,
    staged, used, sems,
):
    capacity = owner_ref.shape[0]
    targets = {
        2: up_ref.at[0], 3: up_ref.at[1], 6: down_ref.at[0], 7: down_ref.at[1],
        1: cross_ref.at[0], 5: cross_ref.at[1],
    }
    for seat in range(capacity):
        table_ref[seat] = -1
        seat_ref[seat] = 0

    def note(i, pair, rank):
        seat_ref[i] = PAIR * pair + rank
        table_ref[PAIR * pair + rank] = slot_ref[i]

    seats_of_tiles(count_ref, owner_ref, used, note)

    def load(i):
        return pltpu.make_async_copy(tiles_ref.at[i], staged.at[i], sems.at[i])

    def store(i, target, rank):
        return pltpu.make_async_copy(staged.at[i], target.at[rank], sems.at[i])

    def sent(i):
        pair = seat_ref[i] // PAIR
        return (i < count_ref[0]) & (pair != 0) & (pair != 4)

    for i in range(capacity):

        @pl.when(sent(i))
        def _():
            load(i).start()

    for i in range(capacity):

        @pl.when(sent(i))
        def _():
            load(i).wait()
            for pair, target in targets.items():

                @pl.when(seat_ref[i] // PAIR == pair)
                def _():
                    store(i, target, lax.rem(seat_ref[i], PAIR)).start()

    for i in range(capacity):

        @pl.when(sent(i))
        def _():
            store(i, up_ref.at[0], 0).wait()


def pack(tiles, tile_count, tile_owner, tile_slot, scenes):
    smem = pl.BlockSpec(memory_space=pltpu.SMEM)
    hbm = pl.BlockSpec(memory_space=pl.ANY)
    capacity = tile_owner.shape[0]
    two_pairs = jax.ShapeDtypeStruct((2, PAIR) + tiles.shape[1:], tiles.dtype)
    table = jax.ShapeDtypeStruct((capacity,), jnp.int32)
    return pl.pallas_call(
        pack_kernel,
        out_shape=(two_pairs, two_pairs, two_pairs, table, table),
        in_specs=[smem, smem, smem, hbm],
        out_specs=(hbm, hbm, hbm, smem, smem),
        scratch_shapes=[
            pltpu.VMEM(tiles.shape, jnp.float32),
            pltpu.SMEM((scenes,), jnp.int32),
            pltpu.SemaphoreType.DMA((capacity,)),
        ],
        compiler_params=pltpu.CompilerParams(vmem_limit_bytes=56 << 20),
        cost_estimate=pl.CostEstimate(flops=0, bytes_accessed=8 << 20, transcendentals=0),
        name="pack",
    )(tile_count, tile_owner, tile_slot, tiles)


def gram_kernel(
    count_ref, seat_ref, tile_ref, inverse_ref, gram_ref, own_ref, far_ref, inv_head, inv_tail, cross, sems
):
    step = pl.program_id(0)
    tiles = tile_ref.shape[0]

    def kept(i, target, rank):
        return pltpu.make_async_copy(tile_ref.at[i], target.at[rank], sems.at[i])

    @pl.when(step == 0)
    def _():
        head, tail = split(inverse_ref[...])
        inv_head[...] = head
        inv_tail[...] = tail
        gram_ref[...] = jnp.zeros_like(gram_ref)
        cross[...] = jnp.zeros_like(cross)

    for i in range(tiles):
        for pair, target in ((0, own_ref), (4, far_ref.at[0])):
            seat = seat_ref[tiles * step + i]

            @pl.when((tiles * step + i < count_ref[0]) & (seat // PAIR == pair))
            def _():
                kept(i, target, lax.rem(seat, PAIR)).start()

    @pl.when(tiles * step < count_ref[0])
    def _():
        live = [tile_ref[0]]
        for i in range(1, tiles):
            live.append(jnp.where(tiles * step + i < count_ref[0], tile_ref[i], 0.0))
        head, tail = split(jnp.concatenate(live, 0))
        left = dot_split(
            (head[:, :HALF], tail[:, :HALF]), (inv_head[:HALF, :HALF], inv_tail[:HALF, :HALF])
        )
        right = dot_split((head, tail), (inv_head[:, HALF:], inv_tail[:, HALF:]))
        left_head, left_tail = split(left)
        right_head, right_tail = split(right)
        gram_ref[:HALF, :] += dot16(left_head, left_head, 0, 0)
        cross[:HALF, :] += dot16(left_head, left_tail, 0, 0)
        gram_ref[HALF : 2 * HALF, :] += (
            dot16(left_head, right_head, 0, 0)
            + dot16(left_head, right_tail, 0, 0)
            + dot16(left_tail, right_head, 0, 0)
        )
        gram_ref[2 * HALF :, :] += dot16(right_head, right_head, 0, 0)
        cross[HALF:, :] += dot16(right_head, right_tail, 0, 0)

    for i in range(tiles):
        pair = seat_ref[tiles * step + i] // PAIR

        @pl.when((tiles * step + i < count_ref[0]) & ((pair == 0) | (pair == 4)))
        def _():
            kept(i, own_ref, 0).wait()

    @pl.when(step == pl.num_programs(0) - 1)
    def _():
        gram_ref[:HALF, :] += cross[:HALF, :] + cross[:HALF, :].T
        gram_ref[2 * HALF :, :] += cross[HALF:, :] + cross[HALF:, :].T


def gram(tiles, inverse_factor, tile_count, seats):
    capacity, rows, columns = tiles.shape
    pair = jax.ShapeDtypeStruct((PAIR, rows, columns), jnp.float32)
    hbm = pl.BlockSpec(memory_space=pl.ANY)
    return pl.pallas_call(
        gram_kernel,
        out_shape=(
            jax.ShapeDtypeStruct((3 * HALF, HALF), jnp.float32),
            pair,
            jax.ShapeDtypeStruct((2, PAIR, rows, columns), jnp.float32),
        ),
        grid_spec=pltpu.PrefetchScalarGridSpec(
            num_scalar_prefetch=2,
            grid=(capacity // GROUP,),
            in_specs=[
                pl.BlockSpec(
                    (GROUP, rows, columns),
                    lambda i, count, _: (
                        jnp.minimum(i, jnp.maximum(count[0] - 1, 0) // GROUP), 0, 0
                    ),
                ),
                pl.BlockSpec((columns, columns), lambda i, *_: (0, 0)),
            ],
            out_specs=(
                pl.BlockSpec((3 * HALF, HALF), lambda i, *_: (0, 0)),
                hbm,
                hbm,
            ),
            scratch_shapes=[
                pltpu.VMEM((columns, columns), jnp.bfloat16),
                pltpu.VMEM((columns, columns), jnp.bfloat16),
                pltpu.VMEM((2 * HALF, HALF), jnp.float32),
                pltpu.SemaphoreType.DMA((GROUP,)),
            ],
        ),
        compiler_params=pltpu.CompilerParams(
            dimension_semantics=("arbitrary",), vmem_limit_bytes=56 << 20
        ),
        cost_estimate=pl.CostEstimate(
            flops=1_000_000, bytes_accessed=1 << 16, transcendentals=0
        ),
        name="gram",
    )(tile_count, seats, tiles, inverse_factor)


def ring_pairs(size, span, stride, shift):
    ring = [i // stride % span for i in range(size)]
    return [(i, i + ((r + shift) % span - r) * stride) for i, r in enumerate(ring)]


def scatter_sum(value, axis, span, stride):
    size = lax.axis_size(axis)
    me = lax.axis_index(axis) // stride % span
    parts = value.reshape((span, -1) + value.shape[1:])
    total = lax.dynamic_index_in_dim(parts, me, 0, keepdims=False)
    for shift in range(1, span):
        sent = lax.dynamic_index_in_dim(parts, (me + shift) % span, 0, keepdims=False)
        total = total + lax.ppermute(sent, axis, ring_pairs(size, span, stride, shift))
    return total


def select_one(tests, values):
    chosen = values[0]
    for test, value in zip(tests[1:], values[1:]):
        chosen = jnp.where(test, value, chosen)
    return chosen


def from_ahead(value, axis, span, stride):
    size = lax.axis_size(axis)
    return [value] + [
        lax.ppermute(value, axis, ring_pairs(size, span, stride, span - ahead))
        for ahead in range(1, span)
    ]


def in_order(ahead_values, axis, stride):
    span = len(ahead_values)
    me = lax.axis_index(axis) // stride % span
    return [
        select_one([(me + ahead) % span == place for ahead in range(span)], ahead_values)
        for place in range(span)
    ]


def gather(value, axis, span, stride):
    return jnp.concatenate(in_order(from_ahead(value, axis, span, stride), axis, stride), 0)


def reduction_stages(scenes, rows):
    side = 4
    return [("scene", 2, 1), ("rows", side, 1), ("rows", rows // side, side)]


def sum_in_order(ahead_values, axis, stride):
    total, *more = in_order(ahead_values, axis, stride)
    for value in more:
        total = total + value
    return total


def sweep(block):
    shape = (PIVOT, BLOCK)
    lane = lax.broadcasted_iota(jnp.int32, shape, 1)
    sub = lax.broadcasted_iota(jnp.int32, shape, 0)
    strips = [block[PIVOT * v : PIVOT * (v + 1), :] for v in range(BLOCK // PIVOT)]
    upper = []
    for s in range(len(strips)):
        base = PIVOT * s
        inside = (lane >= base) & (lane < base + PIVOT)
        own = [jnp.broadcast_to(strips[s][q : q + 1, :], shape) for q in range(PIVOT)]
        pivot = {
            (r, c): jnp.broadcast_to(own[r][:, base + c : base + c + 1], shape)
            for r in range(PIVOT)
            for c in range(r, PIVOT)
        }
        u = {}
        scale = []
        for q in range(PIVOT):
            scale.append(lax.rsqrt(pivot[q, q]))
            for c in range(q + 1, PIVOT):
                u[q, c] = pivot[q, c] * scale[q]
            for r in range(q + 1, PIVOT):
                for c in range(r, PIVOT):
                    pivot[r, c] = pivot[r, c] - u[q, r] * u[q, c]
        swept = [
            jnp.where(inside, jnp.where(lane == base + q, 1.0, 0.0), own[q]) for q in range(PIVOT)
        ]
        for q in range(PIVOT):
            for r in range(q):
                own[q] = own[q] - u[r, q] * own[r]
                swept[q] = swept[q] - u[r, q] * swept[r]
            own[q] = own[q] * scale[q]
            swept[q] = swept[q] * scale[q]
        for v in range(s + 1, len(strips)):
            column = []
            for q in range(PIVOT):
                entry = jnp.broadcast_to(strips[v][:, base + q : base + q + 1], shape)
                for r in range(q):
                    entry = entry - u[r, q] * column[r]
                column.append(entry * scale[q])
            rest = jnp.where(inside, 0.0, strips[v])
            for q in range(PIVOT):
                rest = rest - column[q] * swept[q]
            strips[v] = rest
        factor_rows, inverse_rows = own[0], swept[0]
        for q in range(1, PIVOT):
            factor_rows = jnp.where(sub == q, own[q], factor_rows)
            inverse_rows = jnp.where(sub == q, swept[q], inverse_rows)
        upper.append(jnp.where(lane >= base + sub, factor_rows, 0.0))
        strips[s] = jnp.where(lane <= base + sub, inverse_rows, 0.0)
    return jnp.concatenate(upper, 0), jnp.concatenate(strips, 0)


def factor_kernel(row_count, inverse_ref, *refs):
    *pieces, factor_ref, head_ref, tail_ref, gram_ref, work = refs
    size = work.shape[0]
    core = lax.rem(lax.axis_index("scene"), 2)
    ring = len(pieces) // 2
    x = lax.rem(lax.axis_index("rows"), ring)
    height = pieces[0].shape[0]
    for i, piece in enumerate(pieces):
        half = core if i < ring else 1 - core
        row = (half * ring + lax.rem(x + i % ring, ring)) * height
        gram_ref[pl.ds(pl.multiple_of(row, 8), height), :] = piece[...]
    work[:HALF, :HALF] = gram_ref[:HALF, :] / row_count
    work[:HALF, HALF:] = gram_ref[HALF : 2 * HALF, :] / row_count
    work[HALF:, HALF:] = gram_ref[2 * HALF :, :] / row_count
    work[HALF:, :HALF] = jnp.zeros((HALF, HALF), jnp.float32)

    @pl.loop(0, size // BLOCK)
    def _(k):
        offset = pl.multiple_of(k * BLOCK, BLOCK)
        here = pl.ds(offset, BLOCK)
        upper, inverse = sweep(work[here, here])
        right = dot32(inverse, work[here, :])
        lane = lax.broadcasted_iota(jnp.int32, (BLOCK, size), 1)
        beyond = jnp.where(lane >= offset + BLOCK, right, 0.0)
        factor_ref[here, :] = beyond
        factor_ref[here, here] = upper
        work[here, :] = right
        work[here, here] = inverse

        @pl.when(k < size // BLOCK - 1)
        def _():
            row = lax.broadcasted_iota(jnp.int32, (size, BLOCK), 0)
            work[:, here] = jnp.where(row >= offset + BLOCK, 0.0, work[:, here])
            work[...] = work[...] - dot32(beyond, work[here, :], 0, 0)

    row = lax.broadcasted_iota(jnp.int32, work.shape, 0)
    lane = lax.broadcasted_iota(jnp.int32, work.shape, 1)
    inverse = jnp.where(lane <= row, work[...], 0.0)
    head_ref[...], tail_ref[...] = split(dot32(inverse_ref[...], inverse, 1, 1))


def factor(pieces, inverse_factor, row_count):
    vmem = pl.BlockSpec(memory_space=pltpu.VMEM)
    size = inverse_factor.shape[0]
    return pl.pallas_call(
        functools.partial(factor_kernel, row_count),
        out_shape=(
            jax.ShapeDtypeStruct((size, size), jnp.float32),
            jax.ShapeDtypeStruct((size, size), jnp.bfloat16),
            jax.ShapeDtypeStruct((size, size), jnp.bfloat16),
        ),
        in_specs=[vmem] * (1 + len(pieces)),
        out_specs=(vmem, vmem, vmem),
        scratch_shapes=[
            pltpu.VMEM((3 * HALF, HALF), jnp.float32),
            pltpu.VMEM((size, size), jnp.float32),
        ],
        compiler_params=pltpu.CompilerParams(vmem_limit_bytes=24 << 20),
        cost_estimate=pl.CostEstimate(
            flops=1_000_000, bytes_accessed=1 << 16, transcendentals=0
        ),
        name="factor",
    )(inverse_factor, *pieces)


def finish_kernel(pairs, slot_ref, head_ref, tail_ref, *refs):
    out_ref, tiles, results, slots, in_sems, out_sems = refs[-6:]
    count = jnp.int32(0)
    for p, place in enumerate(pairs):
        source = refs[p].at[place] if place is not None else refs[p]
        for rank in range(PAIR):
            slot = slot_ref[PAIR * p + rank]

            @pl.when(slot >= 0)
            def _(source=source, rank=rank, slot=slot, count=count):
                slots[count] = slot
                pltpu.make_async_copy(source.at[rank], tiles.at[count], in_sems.at[count]).start()

            count = count + jnp.where(slot >= 0, 1, 0)

    def result_copy(j, slot):
        return pltpu.make_async_copy(results.at[j], out_ref.at[slot], out_sems.at[j])

    @pl.loop(0, count)
    def _(j):
        pltpu.make_async_copy(out_ref.at[0], tiles.at[j], in_sems.at[j]).wait()
        head, tail = split(tiles[j])
        results[j, :, :HALF] = dot_split(
            (head[:, :HALF], tail[:, :HALF]), (head_ref[:HALF, :HALF], tail_ref[:HALF, :HALF])
        )
        results[j, :, HALF:] = dot_split((head, tail), (head_ref[:, HALF:], tail_ref[:, HALF:]))
        result_copy(j, slots[j]).start()

    @pl.loop(0, count)
    def _(j):
        result_copy(j, 0).wait()


def finish(slots, head, tail, received, pairs, before, name):
    rows, columns = received[0].shape[-2:]
    most = min(PAIR * len(pairs), OWN_TILES)
    hbm = pl.BlockSpec(memory_space=pl.ANY)
    vmem = pl.BlockSpec(memory_space=pltpu.VMEM)
    operands = [slots, head, tail, *received] + ([] if before is None else [before])
    return pl.pallas_call(
        functools.partial(finish_kernel, pairs),
        out_shape=jax.ShapeDtypeStruct((OWN_TILES, rows, columns), jnp.float32),
        in_specs=[pl.BlockSpec(memory_space=pltpu.SMEM), vmem, vmem] + [hbm] * (len(operands) - 3),
        out_specs=hbm,
        input_output_aliases={} if before is None else {len(operands) - 1: 0},
        scratch_shapes=[
            pltpu.VMEM((most, rows, columns), jnp.float32),
            pltpu.VMEM((most, rows, columns), jnp.float32),
            pltpu.SMEM((most,), jnp.int32),
            pltpu.SemaphoreType.DMA((most,)),
            pltpu.SemaphoreType.DMA((most,)),
        ],
        compiler_params=pltpu.CompilerParams(vmem_limit_bytes=24 << 20),
        cost_estimate=pl.CostEstimate(
            flops=1_000_000, bytes_accessed=1 << 16, transcendentals=0
        ),
        name=name,
    )(*operands)


def second_pairs_kernel(first_ref, second_ref, first_out, second_out, sems):
    copies = [
        pltpu.make_async_copy(first_ref.at[1], first_out, sems.at[0]),
        pltpu.make_async_copy(second_ref.at[1], second_out, sems.at[1]),
    ]
    for copy in copies:
        copy.start()
    for copy in copies:
        copy.wait()


def second_pairs(first, second):
    hbm = pl.BlockSpec(memory_space=pl.ANY)
    return pl.pallas_call(
        second_pairs_kernel,
        out_shape=(jax.ShapeDtypeStruct(first.shape[1:], first.dtype),) * 2,
        in_specs=[hbm, hbm],
        out_specs=(pl.BlockSpec(memory_space=pltpu.VMEM),) * 2,
        scratch_shapes=[pltpu.SemaphoreType.DMA((2,))],
        cost_estimate=pl.CostEstimate(
            flops=1_000_000, bytes_accessed=1 << 16, transcendentals=0
        ),
        name="second_pairs",
    )(first, second)


def shards(observations, inverse_factor, tile_count, tile_owner, tile_slot):
    scenes, rows = lax.axis_size("scene"), lax.axis_size("rows")
    tile_rows, columns = observations.shape[1:]
    chips = scenes // 2

    def along_z(value, up):
        return lax.ppermute(value, "scene", ring_pairs(scenes, chips, 2, up))

    def other_core(value):
        return lax.ppermute(value, "scene", ring_pairs(scenes, 2, 1, 1))

    up, down, cross, seats, table = pack(observations, tile_count, tile_owner, tile_slot, scenes)
    from_below, from_above = along_z(up, 1), along_z(down, chips - 1)
    crossed = other_core(cross)
    tiles, _ = lax.optimization_barrier((observations, seats))
    value, own, far = gram(tiles, inverse_factor, tile_count, seats)
    value, crossed = lax.optimization_barrier((value, crossed))
    mine = jnp.zeros((8, 128), jnp.float32).at[0, : table.shape[0]].set(table.astype(jnp.float32))
    tables = jnp.concatenate([mine, other_core(mine)], 1)
    stages = reduction_stages(scenes, rows)
    for axis, span, stride in stages:
        value = scatter_sum(value, axis, span, stride)
    height = value.shape[0]
    parts = from_ahead(jnp.concatenate([value, tables], 0), "scene", chips, 2)
    far = lax.dynamic_update_slice_in_dim(far, crossed[1:], 1, 0)
    *parts, far, from_below, from_above = lax.optimization_barrier(
        (*parts, far, from_below, from_above)
    )
    far_in = along_z(far, 2)
    value = sum_in_order([part[:height] for part in parts], "scene", 2)

    def slots_of(ahead, other):
        start = 128 * other + 2 * PAIR * ((chips - ahead) % chips) + PAIR * other
        return parts[ahead][height, start : start + PAIR]

    sources = [(0, 0), (0, 1), (3, 0), (1, 0), (3, 1), (1, 1), (2, 0), (2, 1)]
    slots = jnp.concatenate([slots_of(*source) for source in sources]).astype(jnp.int32)
    value, from_below, from_above = lax.optimization_barrier((value, from_below, from_above))
    passed_up, passed_down = (other_core(pair) for pair in second_pairs(from_below, from_above))
    (x_axis, x_span, x_stride), (y_axis, y_span, y_stride) = stages[1:]
    value = gather(value, y_axis, y_span, y_stride)
    value, slots = lax.optimization_barrier((value, slots))
    pieces = from_ahead(value, x_axis, x_span, x_stride)
    pieces = pieces + [other_core(piece) for piece in pieces]
    upper, head, tail = factor(pieces, inverse_factor, scenes * rows * OWN_TILES * tile_rows)
    near = [own, crossed, from_below, from_above, passed_up, passed_down]
    first = PAIR * len(near)
    out = finish(slots[:first], head, tail, near, (None, 0, 0, 0, None, None), None, "finish_near")
    far = [far_in, far_in]
    return finish(slots[first:], head, tail, far, (0, 1), out, "finish_far"), upper


def solution(mesh):
    in_specs = (
        P(("scene", "rows"), None, None),
        P(),
        P(("scene", "rows")),
        P(("scene", "rows")),
        P(("scene", "rows")),
    )
    out_specs = (P(("scene", "rows"), None, None), P())
    return jax.shard_map(shards, mesh=mesh, in_specs=in_specs, out_specs=out_specs, check_vma=False)
```

```python
import functools

import jax
import jax.numpy as jnp
from jax import lax
from jax.experimental import pallas as pl
from jax.experimental.pallas import tpu as pltpu
from jax.sharding import PartitionSpec as P

OWN_TILES = 8
BLOCK = 128
PIVOT = 8
HALF = 256
PAIR = 2
SPARE = 8
GROUP = 4


def split(value):
    head = value.astype(jnp.bfloat16)
    return head, (value - head.astype(jnp.float32)).astype(jnp.bfloat16)


def dot16(left, right, left_dim=1, right_dim=0):
    return lax.dot_general(
        left,
        right,
        (((left_dim,), (right_dim,)), ((), ())),
        preferred_element_type=jnp.float32,
    )


def dot32(left, right, left_dim=1, right_dim=0):
    return lax.dot_general(
        left,
        right,
        (((left_dim,), (right_dim,)), ((), ())),
        precision=lax.Precision.HIGHEST,
        preferred_element_type=jnp.float32,
    )


def dot_split(left, right):
    return dot16(left[0], right[0]) + (dot16(left[0], right[1]) + dot16(left[1], right[0]))


def seats_of_tiles(count_ref, owner_ref, used, note):
    me = lax.axis_index("scene")
    chips = used.shape[0] // 2
    for pair in range(used.shape[0]):
        used[pair] = 0
    for i in range(owner_ref.shape[0]):

        @pl.when(i < count_ref[0])
        def _():
            owner = owner_ref[i]
            up = lax.rem(owner // 2 - me // 2 + chips, chips)
            other = lax.rem(owner + me, 2)
            pair = 2 * up + other
            rank = used[pair]
            used[pair] = rank + 1
            note(i, pair, rank)


def pack_kernel(
    count_ref, owner_ref, slot_ref, tiles_ref, up_ref, down_ref, cross_ref, seat_ref, table_ref,
    staged, used, sems,
):
    capacity = owner_ref.shape[0]
    targets = {
        2: up_ref.at[0], 3: up_ref.at[1], 6: down_ref.at[0], 7: down_ref.at[1],
        1: cross_ref.at[0], 5: cross_ref.at[1],
    }
    for seat in range(capacity):
        table_ref[seat] = -1
        seat_ref[seat] = 0

    def note(i, pair, rank):
        seat_ref[i] = PAIR * pair + rank
        table_ref[PAIR * pair + rank] = slot_ref[i]

    seats_of_tiles(count_ref, owner_ref, used, note)

    def load(i):
        return pltpu.make_async_copy(tiles_ref.at[i], staged.at[i], sems.at[i])

    def store(i, target, rank):
        return pltpu.make_async_copy(staged.at[i], target.at[rank], sems.at[i])

    def sent(i):
        pair = seat_ref[i] // PAIR
        return (i < count_ref[0]) & (pair != 0) & (pair != 4)

    for i in range(capacity):

        @pl.when(sent(i))
        def _():
            load(i).start()

    for i in range(capacity):

        @pl.when(sent(i))
        def _():
            load(i).wait()
            for pair, target in targets.items():

                @pl.when(seat_ref[i] // PAIR == pair)
                def _():
                    store(i, target, lax.rem(seat_ref[i], PAIR)).start()

    for i in range(capacity):

        @pl.when(sent(i))
        def _():
            store(i, up_ref.at[0], 0).wait()


def pack(tiles, tile_count, tile_owner, tile_slot, scenes):
    smem = pl.BlockSpec(memory_space=pltpu.SMEM)
    hbm = pl.BlockSpec(memory_space=pl.ANY)
    capacity = tile_owner.shape[0]
    two_pairs = jax.ShapeDtypeStruct((2, PAIR) + tiles.shape[1:], tiles.dtype)
    table = jax.ShapeDtypeStruct((capacity,), jnp.int32)
    return pl.pallas_call(
        pack_kernel,
        out_shape=(two_pairs, two_pairs, two_pairs, table, table),
        in_specs=[smem, smem, smem, hbm],
        out_specs=(hbm, hbm, hbm, smem, smem),
        scratch_shapes=[
            pltpu.VMEM(tiles.shape, jnp.float32),
            pltpu.SMEM((scenes,), jnp.int32),
            pltpu.SemaphoreType.DMA((capacity,)),
        ],
        compiler_params=pltpu.CompilerParams(vmem_limit_bytes=56 << 20),
        cost_estimate=pl.CostEstimate(flops=0, bytes_accessed=8 << 20, transcendentals=0),
        name="pack",
    )(tile_count, tile_owner, tile_slot, tiles)


def gram_kernel(
    count_ref, seat_ref, tile_ref, inverse_ref, gram_ref, own_ref, far_ref, inv_head, inv_tail, cross, sems
):
    step = pl.program_id(0)
    tiles = tile_ref.shape[0]

    height = tile_ref.shape[1]

    def kept(i, target, rank):
        rows = pl.ds(pl.multiple_of(rank * height, 8), height)
        return pltpu.make_async_copy(tile_ref.at[i], target.at[rows], sems.at[i])

    @pl.when(step == 0)
    def _():
        head, tail = split(inverse_ref[...])
        inv_head[...] = head
        inv_tail[...] = tail
        gram_ref[...] = jnp.zeros_like(gram_ref)
        cross[...] = jnp.zeros_like(cross)

    for i in range(tiles):
        for pair, target in ((0, own_ref), (4, far_ref)):
            seat = seat_ref[tiles * step + i]

            @pl.when((tiles * step + i < count_ref[0]) & (seat // PAIR == pair))
            def _():
                kept(i, target, lax.rem(seat, PAIR)).start()

    @pl.when(tiles * step < count_ref[0])
    def _():
        live = [tile_ref[0]]
        for i in range(1, tiles):
            live.append(jnp.where(tiles * step + i < count_ref[0], tile_ref[i], 0.0))
        head, tail = split(jnp.concatenate(live, 0))
        left = dot_split(
            (head[:, :HALF], tail[:, :HALF]), (inv_head[:HALF, :HALF], inv_tail[:HALF, :HALF])
        )
        right = dot_split((head, tail), (inv_head[:, HALF:], inv_tail[:, HALF:]))
        left_head, left_tail = split(left)
        right_head, right_tail = split(right)
        gram_ref[:HALF, :] += dot16(left_head, left_head, 0, 0)
        cross[:HALF, :] += dot16(left_head, left_tail, 0, 0)
        gram_ref[HALF : 2 * HALF, :] += (
            dot16(left_head, right_head, 0, 0)
            + dot16(left_head, right_tail, 0, 0)
            + dot16(left_tail, right_head, 0, 0)
        )
        gram_ref[2 * HALF :, :] += dot16(right_head, right_head, 0, 0)
        cross[HALF:, :] += dot16(right_head, right_tail, 0, 0)

    for i in range(tiles):
        pair = seat_ref[tiles * step + i] // PAIR

        @pl.when((tiles * step + i < count_ref[0]) & ((pair == 0) | (pair == 4)))
        def _():
            kept(i, own_ref, 0).wait()

    @pl.when(step == pl.num_programs(0) - 1)
    def _():
        gram_ref[:HALF, :] += cross[:HALF, :] + cross[:HALF, :].T
        gram_ref[2 * HALF :, :] += cross[HALF:, :] + cross[HALF:, :].T


def gram(tiles, inverse_factor, tile_count, seats):
    capacity, rows, columns = tiles.shape
    pair = jax.ShapeDtypeStruct((PAIR * rows, columns), jnp.float32)
    hbm = pl.BlockSpec(memory_space=pl.ANY)
    return pl.pallas_call(
        gram_kernel,
        out_shape=(
            jax.ShapeDtypeStruct((3 * HALF, HALF), jnp.float32),
            pair,
            jax.ShapeDtypeStruct((2 * PAIR * rows + SPARE, columns), jnp.float32),
        ),
        grid_spec=pltpu.PrefetchScalarGridSpec(
            num_scalar_prefetch=2,
            grid=(capacity // GROUP,),
            in_specs=[
                pl.BlockSpec(
                    (GROUP, rows, columns),
                    lambda i, count, _: (
                        jnp.minimum(i, jnp.maximum(count[0] - 1, 0) // GROUP), 0, 0
                    ),
                ),
                pl.BlockSpec((columns, columns), lambda i, *_: (0, 0)),
            ],
            out_specs=(
                pl.BlockSpec((3 * HALF, HALF), lambda i, *_: (0, 0)),
                hbm,
                hbm,
            ),
            scratch_shapes=[
                pltpu.VMEM((columns, columns), jnp.bfloat16),
                pltpu.VMEM((columns, columns), jnp.bfloat16),
                pltpu.VMEM((2 * HALF, HALF), jnp.float32),
                pltpu.SemaphoreType.DMA((GROUP,)),
            ],
        ),
        compiler_params=pltpu.CompilerParams(
            dimension_semantics=("arbitrary",), vmem_limit_bytes=56 << 20
        ),
        cost_estimate=pl.CostEstimate(
            flops=1_000_000, bytes_accessed=1 << 16, transcendentals=0
        ),
        name="gram",
    )(tile_count, seats, tiles, inverse_factor)


def ring_pairs(size, span, stride, shift):
    ring = [i // stride % span for i in range(size)]
    return [(i, i + ((r + shift) % span - r) * stride) for i, r in enumerate(ring)]


def scatter_sum(value, axis, span, stride):
    size = lax.axis_size(axis)
    me = lax.axis_index(axis) // stride % span
    parts = value.reshape((span, -1) + value.shape[1:])
    total = lax.dynamic_index_in_dim(parts, me, 0, keepdims=False)
    for shift in range(1, span):
        sent = lax.dynamic_index_in_dim(parts, (me + shift) % span, 0, keepdims=False)
        total = total + lax.ppermute(sent, axis, ring_pairs(size, span, stride, shift))
    return total


def select_one(tests, values):
    chosen = values[0]
    for test, value in zip(tests[1:], values[1:]):
        chosen = jnp.where(test, value, chosen)
    return chosen


def from_ahead(value, axis, span, stride):
    size = lax.axis_size(axis)
    return [value] + [
        lax.ppermute(value, axis, ring_pairs(size, span, stride, span - ahead))
        for ahead in range(1, span)
    ]


def in_order(ahead_values, axis, stride):
    span = len(ahead_values)
    me = lax.axis_index(axis) // stride % span
    return [
        select_one([(me + ahead) % span == place for ahead in range(span)], ahead_values)
        for place in range(span)
    ]


def gather(value, axis, span, stride):
    return jnp.concatenate(in_order(from_ahead(value, axis, span, stride), axis, stride), 0)


def reduction_stages(scenes, rows):
    side = 4
    return [("scene", 2, 1), ("rows", side, 1), ("rows", rows // side, side)]


def sum_in_order(ahead_values, axis, stride):
    total, *more = in_order(ahead_values, axis, stride)
    for value in more:
        total = total + value
    return total


def sweep(block):
    shape = (PIVOT, BLOCK)
    lane = lax.broadcasted_iota(jnp.int32, shape, 1)
    sub = lax.broadcasted_iota(jnp.int32, shape, 0)
    strips = [block[PIVOT * v : PIVOT * (v + 1), :] for v in range(BLOCK // PIVOT)]
    upper = []
    for s in range(len(strips)):
        base = PIVOT * s
        inside = (lane >= base) & (lane < base + PIVOT)
        own = [jnp.broadcast_to(strips[s][q : q + 1, :], shape) for q in range(PIVOT)]
        pivot = {
            (r, c): jnp.broadcast_to(own[r][:, base + c : base + c + 1], shape)
            for r in range(PIVOT)
            for c in range(r, PIVOT)
        }
        u = {}
        scale = []
        for q in range(PIVOT):
            scale.append(lax.rsqrt(pivot[q, q]))
            for c in range(q + 1, PIVOT):
                u[q, c] = pivot[q, c] * scale[q]
            for r in range(q + 1, PIVOT):
                for c in range(r, PIVOT):
                    pivot[r, c] = pivot[r, c] - u[q, r] * u[q, c]
        swept = [
            jnp.where(inside, jnp.where(lane == base + q, 1.0, 0.0), own[q]) for q in range(PIVOT)
        ]
        for q in range(PIVOT):
            for r in range(q):
                own[q] = own[q] - u[r, q] * own[r]
                swept[q] = swept[q] - u[r, q] * swept[r]
            own[q] = own[q] * scale[q]
            swept[q] = swept[q] * scale[q]
        for v in range(s + 1, len(strips)):
            column = []
            for q in range(PIVOT):
                entry = jnp.broadcast_to(strips[v][:, base + q : base + q + 1], shape)
                for r in range(q):
                    entry = entry - u[r, q] * column[r]
                column.append(entry * scale[q])
            rest = jnp.where(inside, 0.0, strips[v])
            for q in range(PIVOT):
                rest = rest - column[q] * swept[q]
            strips[v] = rest
        factor_rows, inverse_rows = own[0], swept[0]
        for q in range(1, PIVOT):
            factor_rows = jnp.where(sub == q, own[q], factor_rows)
            inverse_rows = jnp.where(sub == q, swept[q], inverse_rows)
        upper.append(jnp.where(lane >= base + sub, factor_rows, 0.0))
        strips[s] = jnp.where(lane <= base + sub, inverse_rows, 0.0)
    return jnp.concatenate(upper, 0), jnp.concatenate(strips, 0)


def factor_kernel(row_count, inverse_ref, *refs):
    *pieces, factor_ref, head_ref, tail_ref, gram_ref, work = refs
    size = work.shape[0]
    core = lax.rem(lax.axis_index("scene"), 2)
    ring = len(pieces) // 2
    x = lax.rem(lax.axis_index("rows"), ring)
    height = pieces[0].shape[0]
    for i, piece in enumerate(pieces):
        half = core if i < ring else 1 - core
        row = (half * ring + lax.rem(x + i % ring, ring)) * height
        gram_ref[pl.ds(pl.multiple_of(row, 8), height), :] = piece[...]
    work[:HALF, :HALF] = gram_ref[:HALF, :] / row_count
    work[:HALF, HALF:] = gram_ref[HALF : 2 * HALF, :] / row_count
    work[HALF:, HALF:] = gram_ref[2 * HALF :, :] / row_count
    work[HALF:, :HALF] = jnp.zeros((HALF, HALF), jnp.float32)

    @pl.loop(0, size // BLOCK)
    def _(k):
        offset = pl.multiple_of(k * BLOCK, BLOCK)
        here = pl.ds(offset, BLOCK)
        upper, inverse = sweep(work[here, here])
        right = dot32(inverse, work[here, :])
        lane = lax.broadcasted_iota(jnp.int32, (BLOCK, size), 1)
        beyond = jnp.where(lane >= offset + BLOCK, right, 0.0)
        factor_ref[here, :] = beyond
        factor_ref[here, here] = upper
        work[here, :] = right
        work[here, here] = inverse

        @pl.when(k < size // BLOCK - 1)
        def _():
            row = lax.broadcasted_iota(jnp.int32, (size, BLOCK), 0)
            work[:, here] = jnp.where(row >= offset + BLOCK, 0.0, work[:, here])
            work[...] = work[...] - dot32(beyond, work[here, :], 0, 0)

    row = lax.broadcasted_iota(jnp.int32, work.shape, 0)
    lane = lax.broadcasted_iota(jnp.int32, work.shape, 1)
    inverse = jnp.where(lane <= row, work[...], 0.0)
    head_ref[...], tail_ref[...] = split(dot32(inverse_ref[...], inverse, 1, 1))


def factor(pieces, inverse_factor, row_count):
    vmem = pl.BlockSpec(memory_space=pltpu.VMEM)
    size = inverse_factor.shape[0]
    return pl.pallas_call(
        functools.partial(factor_kernel, row_count),
        out_shape=(
            jax.ShapeDtypeStruct((size, size), jnp.float32),
            jax.ShapeDtypeStruct((size, size), jnp.bfloat16),
            jax.ShapeDtypeStruct((size, size), jnp.bfloat16),
        ),
        in_specs=[vmem] * (1 + len(pieces)),
        out_specs=(vmem, vmem, vmem),
        scratch_shapes=[
            pltpu.VMEM((3 * HALF, HALF), jnp.float32),
            pltpu.VMEM((size, size), jnp.float32),
        ],
        compiler_params=pltpu.CompilerParams(vmem_limit_bytes=24 << 20),
        cost_estimate=pl.CostEstimate(
            flops=1_000_000, bytes_accessed=1 << 16, transcendentals=0
        ),
        name="factor",
    )(inverse_factor, *pieces)


def finish_kernel(pairs, slot_ref, head_ref, tail_ref, *refs):
    out_ref, tiles, results, slots, in_sems, out_sems = refs[-6:]
    count = jnp.int32(0)
    for p, place in enumerate(pairs):
        flat = len(refs[p].shape) == 2
        first = PAIR * place if flat else 0
        source = refs[p] if flat else refs[p].at[place]
        height = tiles.shape[1]
        for rank in range(PAIR):
            slot = slot_ref[PAIR * p + rank]

            @pl.when(slot >= 0)
            def _(source=source, rank=rank, slot=slot, count=count, first=first):
                slots[count] = slot
                rows = pl.ds((first + rank) * height, height)
                own_rows = source.at[rows] if len(source.shape) == 2 else source.at[rank]
                pltpu.make_async_copy(own_rows, tiles.at[count], in_sems.at[count]).start()

            count = count + jnp.where(slot >= 0, 1, 0)

    def result_copy(j, slot):
        return pltpu.make_async_copy(results.at[j], out_ref.at[slot], out_sems.at[j])

    @pl.loop(0, count)
    def _(j):
        pltpu.make_async_copy(out_ref.at[0], tiles.at[j], in_sems.at[j]).wait()
        head, tail = split(tiles[j])
        results[j, :, :HALF] = dot_split(
            (head[:, :HALF], tail[:, :HALF]), (head_ref[:HALF, :HALF], tail_ref[:HALF, :HALF])
        )
        results[j, :, HALF:] = dot_split((head, tail), (head_ref[:, HALF:], tail_ref[:, HALF:]))
        result_copy(j, slots[j]).start()

    @pl.loop(0, count)
    def _(j):
        result_copy(j, 0).wait()


def finish(slots, head, tail, received, pairs, before, name, rows):
    columns = received[0].shape[-1]
    most = min(PAIR * len(pairs), OWN_TILES)
    hbm = pl.BlockSpec(memory_space=pl.ANY)
    vmem = pl.BlockSpec(memory_space=pltpu.VMEM)
    operands = [slots, head, tail, *received] + ([] if before is None else [before])
    return pl.pallas_call(
        functools.partial(finish_kernel, pairs),
        out_shape=jax.ShapeDtypeStruct((OWN_TILES, rows, columns), jnp.float32),
        in_specs=[pl.BlockSpec(memory_space=pltpu.SMEM), vmem, vmem] + [hbm] * (len(operands) - 3),
        out_specs=hbm,
        input_output_aliases={} if before is None else {len(operands) - 1: 0},
        scratch_shapes=[
            pltpu.VMEM((most, rows, columns), jnp.float32),
            pltpu.VMEM((most, rows, columns), jnp.float32),
            pltpu.SMEM((most,), jnp.int32),
            pltpu.SemaphoreType.DMA((most,)),
            pltpu.SemaphoreType.DMA((most,)),
        ],
        compiler_params=pltpu.CompilerParams(vmem_limit_bytes=24 << 20),
        cost_estimate=pl.CostEstimate(
            flops=1_000_000, bytes_accessed=1 << 16, transcendentals=0
        ),
        name=name,
    )(*operands)


def second_pairs_kernel(first_ref, second_ref, out_ref, sems):
    copies = [
        pltpu.make_async_copy(ref.at[1], out_ref.at[i], sems.at[i])
        for i, ref in enumerate((first_ref, second_ref))
    ]
    for copy in copies:
        copy.start()
    for copy in copies:
        copy.wait()


def second_pairs(first, second):
    hbm = pl.BlockSpec(memory_space=pl.ANY)
    return pl.pallas_call(
        second_pairs_kernel,
        out_shape=jax.ShapeDtypeStruct(first.shape, first.dtype),
        in_specs=[hbm, hbm],
        out_specs=pl.BlockSpec(memory_space=pltpu.VMEM),
        scratch_shapes=[pltpu.SemaphoreType.DMA((2,))],
        cost_estimate=pl.CostEstimate(
            flops=1_000_000, bytes_accessed=1 << 16, transcendentals=0
        ),
        name="second_pairs",
    )(first, second)


def shards(observations, inverse_factor, tile_count, tile_owner, tile_slot):
    scenes, rows = lax.axis_size("scene"), lax.axis_size("rows")
    tile_rows, columns = observations.shape[1:]
    chips = scenes // 2

    def along_z(value, up):
        return lax.ppermute(value, "scene", ring_pairs(scenes, chips, 2, up))

    def other_core(value):
        return lax.ppermute(value, "scene", ring_pairs(scenes, 2, 1, 1))

    up, down, cross, seats, table = pack(observations, tile_count, tile_owner, tile_slot, scenes)
    from_below, from_above = along_z(up, 1), along_z(down, chips - 1)
    crossed = other_core(cross)
    tiles, _ = lax.optimization_barrier((observations, seats))
    value, own, far = gram(tiles, inverse_factor, tile_count, seats)
    value, crossed = lax.optimization_barrier((value, crossed))
    mine = jnp.zeros((8, 128), jnp.float32).at[0, : table.shape[0]].set(table.astype(jnp.float32))
    tables = jnp.concatenate([mine, other_core(mine)], 1)
    stages = reduction_stages(scenes, rows)
    for axis, span, stride in stages:
        value = scatter_sum(value, axis, span, stride)
    height = value.shape[0]
    parts = from_ahead(jnp.concatenate([value, tables], 0), "scene", chips, 2)
    far = lax.dynamic_update_slice_in_dim(
        far, crossed[1].reshape(PAIR * tile_rows, columns), PAIR * tile_rows, 0
    )
    *parts, far, from_below, from_above = lax.optimization_barrier(
        (*parts, far, from_below, from_above)
    )
    far_in = along_z(far, 2)
    value = sum_in_order([part[:height] for part in parts], "scene", 2)

    def slots_of(ahead, other):
        start = 128 * other + 2 * PAIR * ((chips - ahead) % chips) + PAIR * other
        return parts[ahead][height, start : start + PAIR]

    sources = [(0, 0), (0, 1), (3, 0), (1, 0), (3, 1), (1, 1), (2, 0), (2, 1)]
    slots = jnp.concatenate([slots_of(*source) for source in sources]).astype(jnp.int32)
    value, from_below, from_above = lax.optimization_barrier((value, from_below, from_above))
    passed_on = other_core(second_pairs(from_below, from_above))
    (x_axis, x_span, x_stride), (y_axis, y_span, y_stride) = stages[1:]
    value = gather(value, y_axis, y_span, y_stride)
    value, slots = lax.optimization_barrier((value, slots))
    pieces = from_ahead(value, x_axis, x_span, x_stride)
    pieces = pieces + [other_core(piece) for piece in pieces]
    upper, head, tail = factor(pieces, inverse_factor, scenes * rows * OWN_TILES * tile_rows)
    near = [own, crossed, from_below, from_above, passed_on, passed_on]
    first = PAIR * len(near)
    out = finish(slots[:first], head, tail, near, (0, 0, 0, 0, 0, 1), None, "finish_near", tile_rows)
    far = [far_in, far_in]
    return finish(slots[first:], head, tail, far, (0, 1), out, "finish_far", tile_rows), upper


def solution(mesh):
    in_specs = (
        P(("scene", "rows"), None, None),
        P(),
        P(("scene", "rows")),
        P(("scene", "rows")),
        P(("scene", "rows")),
    )
    out_specs = (P(("scene", "rows"), None, None), P())
    return jax.shard_map(shards, mesh=mesh, in_specs=in_specs, out_specs=out_specs, check_vma=False)
```

```python
import functools

import jax
import jax.numpy as jnp
from jax import lax
from jax.experimental import pallas as pl
from jax.experimental.pallas import tpu as pltpu
from jax.sharding import PartitionSpec as P

OWN_TILES = 8
BLOCK = 128
PIVOT = 8
HALF = 256
PAIR = 2
SPARE = 8
GROUP = 4


def split(value):
    head = value.astype(jnp.bfloat16)
    return head, (value - head.astype(jnp.float32)).astype(jnp.bfloat16)


def dot16(left, right, left_dim=1, right_dim=0):
    return lax.dot_general(
        left,
        right,
        (((left_dim,), (right_dim,)), ((), ())),
        preferred_element_type=jnp.float32,
    )


def dot32(left, right, left_dim=1, right_dim=0):
    return lax.dot_general(
        left,
        right,
        (((left_dim,), (right_dim,)), ((), ())),
        precision=lax.Precision.HIGHEST,
        preferred_element_type=jnp.float32,
    )


def dot_split(left, right):
    return dot16(left[0], right[0]) + (dot16(left[0], right[1]) + dot16(left[1], right[0]))


def seats_of_tiles(count_ref, owner_ref, used, note):
    me = lax.axis_index("scene")
    chips = used.shape[0] // 2
    for pair in range(used.shape[0]):
        used[pair] = 0
    for i in range(owner_ref.shape[0]):

        @pl.when(i < count_ref[0])
        def _():
            owner = owner_ref[i]
            up = lax.rem(owner // 2 - me // 2 + chips, chips)
            other = lax.rem(owner + me, 2)
            pair = 2 * up + other
            rank = used[pair]
            used[pair] = rank + 1
            note(i, pair, rank)


def pack_kernel(
    count_ref, owner_ref, slot_ref, tiles_ref, up_ref, down_ref, cross_ref, seat_ref, table_ref,
    staged, used, sems,
):
    capacity = owner_ref.shape[0]
    targets = {
        2: up_ref.at[0], 3: up_ref.at[1], 6: down_ref.at[0], 7: down_ref.at[1],
        1: cross_ref.at[0], 5: cross_ref.at[1],
    }
    for seat in range(capacity):
        table_ref[seat] = -1
        seat_ref[seat] = 0

    def note(i, pair, rank):
        seat_ref[i] = PAIR * pair + rank
        table_ref[PAIR * pair + rank] = slot_ref[i]

    seats_of_tiles(count_ref, owner_ref, used, note)

    def load(i):
        return pltpu.make_async_copy(tiles_ref.at[i], staged.at[i], sems.at[i])

    def store(i, target, rank):
        return pltpu.make_async_copy(staged.at[i], target.at[rank], sems.at[i])

    def sent(i):
        pair = seat_ref[i] // PAIR
        return (i < count_ref[0]) & (pair != 0) & (pair != 4)

    for i in range(capacity):

        @pl.when(sent(i))
        def _():
            load(i).start()

    for i in range(capacity):

        @pl.when(sent(i))
        def _():
            load(i).wait()
            for pair, target in targets.items():

                @pl.when(seat_ref[i] // PAIR == pair)
                def _():
                    store(i, target, lax.rem(seat_ref[i], PAIR)).start()

    for i in range(capacity):

        @pl.when(sent(i))
        def _():
            store(i, up_ref.at[0], 0).wait()


def pack(tiles, tile_count, tile_owner, tile_slot, scenes):
    smem = pl.BlockSpec(memory_space=pltpu.SMEM)
    hbm = pl.BlockSpec(memory_space=pl.ANY)
    capacity = tile_owner.shape[0]
    two_pairs = jax.ShapeDtypeStruct((2, PAIR) + tiles.shape[1:], tiles.dtype)
    table = jax.ShapeDtypeStruct((capacity,), jnp.int32)
    return pl.pallas_call(
        pack_kernel,
        out_shape=(two_pairs, two_pairs, two_pairs, table, table),
        in_specs=[smem, smem, smem, hbm],
        out_specs=(hbm, hbm, hbm, smem, smem),
        scratch_shapes=[
            pltpu.VMEM(tiles.shape, jnp.float32),
            pltpu.SMEM((scenes,), jnp.int32),
            pltpu.SemaphoreType.DMA((capacity,)),
        ],
        compiler_params=pltpu.CompilerParams(vmem_limit_bytes=56 << 20),
        cost_estimate=pl.CostEstimate(flops=0, bytes_accessed=8 << 20, transcendentals=0),
        name="pack",
    )(tile_count, tile_owner, tile_slot, tiles)


def gram_kernel(
    count_ref, seat_ref, tile_ref, inverse_ref, gram_ref, own_ref, far_ref, inv_head, inv_tail, cross, sems
):
    step = pl.program_id(0)
    tiles = tile_ref.shape[0]

    height = tile_ref.shape[1]

    def kept(i, target, rank):
        rows = pl.ds(pl.multiple_of(rank * height, 8), height)
        return pltpu.make_async_copy(tile_ref.at[i], target.at[rows], sems.at[i])

    @pl.when(step == 0)
    def _():
        head, tail = split(inverse_ref[...])
        inv_head[...] = head
        inv_tail[...] = tail
        gram_ref[...] = jnp.zeros_like(gram_ref)
        cross[...] = jnp.zeros_like(cross)

    for i in range(tiles):
        for pair, target in ((0, own_ref), (4, far_ref)):
            seat = seat_ref[tiles * step + i]

            @pl.when((tiles * step + i < count_ref[0]) & (seat // PAIR == pair))
            def _():
                kept(i, target, lax.rem(seat, PAIR)).start()

    @pl.when(tiles * step < count_ref[0])
    def _():
        live = [tile_ref[0]]
        for i in range(1, tiles):
            live.append(jnp.where(tiles * step + i < count_ref[0], tile_ref[i], 0.0))
        head, tail = split(jnp.concatenate(live, 0))
        left = dot_split(
            (head[:, :HALF], tail[:, :HALF]), (inv_head[:HALF, :HALF], inv_tail[:HALF, :HALF])
        )
        right = dot_split((head, tail), (inv_head[:, HALF:], inv_tail[:, HALF:]))
        left_head, left_tail = split(left)
        right_head, right_tail = split(right)
        gram_ref[:HALF, :] += dot16(left_head, left_head, 0, 0)
        cross[:HALF, :] += dot16(left_head, left_tail, 0, 0)
        gram_ref[HALF : 2 * HALF, :] += (
            dot16(left_head, right_head, 0, 0)
            + dot16(left_head, right_tail, 0, 0)
            + dot16(left_tail, right_head, 0, 0)
        )
        gram_ref[2 * HALF :, :] += dot16(right_head, right_head, 0, 0)
        cross[HALF:, :] += dot16(right_head, right_tail, 0, 0)

    for i in range(tiles):
        pair = seat_ref[tiles * step + i] // PAIR

        @pl.when((tiles * step + i < count_ref[0]) & ((pair == 0) | (pair == 4)))
        def _():
            kept(i, own_ref, 0).wait()

    @pl.when(step == pl.num_programs(0) - 1)
    def _():
        gram_ref[:HALF, :] += cross[:HALF, :] + cross[:HALF, :].T
        gram_ref[2 * HALF :, :] += cross[HALF:, :] + cross[HALF:, :].T


def gram(tiles, inverse_factor, tile_count, seats):
    capacity, rows, columns = tiles.shape
    pair = jax.ShapeDtypeStruct((PAIR * rows, columns), jnp.float32)
    hbm = pl.BlockSpec(memory_space=pl.ANY)
    return pl.pallas_call(
        gram_kernel,
        out_shape=(
            jax.ShapeDtypeStruct((3 * HALF, HALF), jnp.float32),
            pair,
            jax.ShapeDtypeStruct((2 * PAIR * rows + SPARE, columns), jnp.float32),
        ),
        grid_spec=pltpu.PrefetchScalarGridSpec(
            num_scalar_prefetch=2,
            grid=(capacity // GROUP,),
            in_specs=[
                pl.BlockSpec(
                    (GROUP, rows, columns),
                    lambda i, count, _: (
                        jnp.minimum(i, jnp.maximum(count[0] - 1, 0) // GROUP), 0, 0
                    ),
                ),
                pl.BlockSpec((columns, columns), lambda i, *_: (0, 0)),
            ],
            out_specs=(
                pl.BlockSpec((3 * HALF, HALF), lambda i, *_: (0, 0)),
                hbm,
                hbm,
            ),
            scratch_shapes=[
                pltpu.VMEM((columns, columns), jnp.bfloat16),
                pltpu.VMEM((columns, columns), jnp.bfloat16),
                pltpu.VMEM((2 * HALF, HALF), jnp.float32),
                pltpu.SemaphoreType.DMA((GROUP,)),
            ],
        ),
        compiler_params=pltpu.CompilerParams(
            dimension_semantics=("arbitrary",), vmem_limit_bytes=56 << 20
        ),
        cost_estimate=pl.CostEstimate(
            flops=1_000_000, bytes_accessed=1 << 16, transcendentals=0
        ),
        name="gram",
    )(tile_count, seats, tiles, inverse_factor)


def ring_pairs(size, span, stride, shift):
    ring = [i // stride % span for i in range(size)]
    return [(i, i + ((r + shift) % span - r) * stride) for i, r in enumerate(ring)]


def scatter_sum(value, axis, span, stride):
    size = lax.axis_size(axis)
    me = lax.axis_index(axis) // stride % span
    parts = value.reshape((span, -1) + value.shape[1:])
    total = lax.dynamic_index_in_dim(parts, me, 0, keepdims=False)
    for shift in range(1, span):
        sent = lax.dynamic_index_in_dim(parts, (me + shift) % span, 0, keepdims=False)
        total = total + lax.ppermute(sent, axis, ring_pairs(size, span, stride, shift))
    return total


def select_one(tests, values):
    chosen = values[0]
    for test, value in zip(tests[1:], values[1:]):
        chosen = jnp.where(test, value, chosen)
    return chosen


def from_ahead(value, axis, span, stride):
    size = lax.axis_size(axis)
    return [value] + [
        lax.ppermute(value, axis, ring_pairs(size, span, stride, span - ahead))
        for ahead in range(1, span)
    ]


def in_order(ahead_values, axis, stride):
    span = len(ahead_values)
    me = lax.axis_index(axis) // stride % span
    return [
        select_one([(me + ahead) % span == place for ahead in range(span)], ahead_values)
        for place in range(span)
    ]


def gather(value, axis, span, stride):
    return jnp.concatenate(in_order(from_ahead(value, axis, span, stride), axis, stride), 0)


def reduction_stages(scenes, rows):
    side = 4
    return [("scene", 2, 1), ("rows", side, 1), ("rows", rows // side, side)]


def sum_in_order(ahead_values, axis, stride):
    total, *more = in_order(ahead_values, axis, stride)
    for value in more:
        total = total + value
    return total


def sweep(block):
    shape = (PIVOT, BLOCK)
    lane = lax.broadcasted_iota(jnp.int32, shape, 1)
    sub = lax.broadcasted_iota(jnp.int32, shape, 0)
    strips = [block[PIVOT * v : PIVOT * (v + 1), :] for v in range(BLOCK // PIVOT)]
    upper = []
    for s in range(len(strips)):
        base = PIVOT * s
        inside = (lane >= base) & (lane < base + PIVOT)
        own = [jnp.broadcast_to(strips[s][q : q + 1, :], shape) for q in range(PIVOT)]
        pivot = {
            (r, c): jnp.broadcast_to(own[r][:, base + c : base + c + 1], shape)
            for r in range(PIVOT)
            for c in range(r, PIVOT)
        }
        u = {}
        scale = []
        for q in range(PIVOT):
            scale.append(lax.rsqrt(pivot[q, q]))
            for c in range(q + 1, PIVOT):
                u[q, c] = pivot[q, c] * scale[q]
            for r in range(q + 1, PIVOT):
                for c in range(r, PIVOT):
                    pivot[r, c] = pivot[r, c] - u[q, r] * u[q, c]
        swept = [
            jnp.where(inside, jnp.where(lane == base + q, 1.0, 0.0), own[q]) for q in range(PIVOT)
        ]
        for q in range(PIVOT):
            for r in range(q):
                own[q] = own[q] - u[r, q] * own[r]
                swept[q] = swept[q] - u[r, q] * swept[r]
            own[q] = own[q] * scale[q]
            swept[q] = swept[q] * scale[q]
        for v in range(s + 1, len(strips)):
            column = []
            for q in range(PIVOT):
                entry = jnp.broadcast_to(strips[v][:, base + q : base + q + 1], shape)
                for r in range(q):
                    entry = entry - u[r, q] * column[r]
                column.append(entry * scale[q])
            rest = jnp.where(inside, 0.0, strips[v])
            for q in range(PIVOT):
                rest = rest - column[q] * swept[q]
            strips[v] = rest
        factor_rows, inverse_rows = own[0], swept[0]
        for q in range(1, PIVOT):
            factor_rows = jnp.where(sub == q, own[q], factor_rows)
            inverse_rows = jnp.where(sub == q, swept[q], inverse_rows)
        upper.append(jnp.where(lane >= base + sub, factor_rows, 0.0))
        strips[s] = jnp.where(lane <= base + sub, inverse_rows, 0.0)
    return jnp.concatenate(upper, 0), jnp.concatenate(strips, 0)


def factor_kernel(row_count, inverse_ref, *refs):
    *pieces, factor_ref, head_ref, tail_ref, gram_ref, work = refs
    size = work.shape[0]
    core = lax.rem(lax.axis_index("scene"), 2)
    ring = len(pieces) // 2
    x = lax.rem(lax.axis_index("rows"), ring)
    height = pieces[0].shape[0]
    for i, piece in enumerate(pieces):
        half = core if i < ring else 1 - core
        row = (half * ring + lax.rem(x + i % ring, ring)) * height
        gram_ref[pl.ds(pl.multiple_of(row, 8), height), :] = piece[...]
    work[:HALF, :HALF] = gram_ref[:HALF, :] / row_count
    work[:HALF, HALF:] = gram_ref[HALF : 2 * HALF, :] / row_count
    work[HALF:, HALF:] = gram_ref[2 * HALF :, :] / row_count
    work[HALF:, :HALF] = jnp.zeros((HALF, HALF), jnp.float32)

    steps = size // BLOCK
    block = work[:BLOCK, :BLOCK]
    for k in range(steps):
        offset, end = k * BLOCK, (k + 1) * BLOCK
        here, below = pl.ds(offset, BLOCK), pl.ds(end, size - end)
        upper, inverse = sweep(block)
        if k < steps - 1:
            ahead = dot32(inverse, work[here, end : end + BLOCK])
            block = work[end : end + BLOCK, end : end + BLOCK] - dot32(ahead, ahead, 0, 0)
        right = dot32(inverse, work[here, :])
        factor_ref[here, :] = jnp.zeros((BLOCK, size), jnp.float32)
        factor_ref[here, here] = upper
        work[here, :] = right
        work[here, here] = inverse
        if k < steps - 1:
            factor_ref[here, end:] = right[:, end:]
            work[below, here] = jnp.zeros((size - end, BLOCK), jnp.float32)
            work[below, :] = work[below, :] - dot32(right[:, end:], work[here, :], 0, 0)

    row = lax.broadcasted_iota(jnp.int32, work.shape, 0)
    lane = lax.broadcasted_iota(jnp.int32, work.shape, 1)
    inverse = jnp.where(lane <= row, work[...], 0.0)
    head_ref[...], tail_ref[...] = split(dot32(inverse_ref[...], inverse, 1, 1))


def factor(pieces, inverse_factor, row_count):
    vmem = pl.BlockSpec(memory_space=pltpu.VMEM)
    size = inverse_factor.shape[0]
    return pl.pallas_call(
        functools.partial(factor_kernel, row_count),
        out_shape=(
            jax.ShapeDtypeStruct((size, size), jnp.float32),
            jax.ShapeDtypeStruct((size, size), jnp.bfloat16),
            jax.ShapeDtypeStruct((size, size), jnp.bfloat16),
        ),
        in_specs=[vmem] * (1 + len(pieces)),
        out_specs=(vmem, vmem, vmem),
        scratch_shapes=[
            pltpu.VMEM((3 * HALF, HALF), jnp.float32),
            pltpu.VMEM((size, size), jnp.float32),
        ],
        compiler_params=pltpu.CompilerParams(vmem_limit_bytes=24 << 20),
        cost_estimate=pl.CostEstimate(
            flops=1_000_000, bytes_accessed=1 << 16, transcendentals=0
        ),
        name="factor",
    )(inverse_factor, *pieces)


def finish_kernel(pairs, slot_ref, head_ref, tail_ref, *refs):
    out_ref, tiles, results, slots, in_sems, out_sems = refs[-6:]
    count = jnp.int32(0)
    for p, place in enumerate(pairs):
        flat = len(refs[p].shape) == 2
        first = PAIR * place if flat else 0
        source = refs[p] if flat else refs[p].at[place]
        height = tiles.shape[1]
        for rank in range(PAIR):
            slot = slot_ref[PAIR * p + rank]

            @pl.when(slot >= 0)
            def _(source=source, rank=rank, slot=slot, count=count, first=first):
                slots[count] = slot
                rows = pl.ds((first + rank) * height, height)
                own_rows = source.at[rows] if len(source.shape) == 2 else source.at[rank]
                pltpu.make_async_copy(own_rows, tiles.at[count], in_sems.at[count]).start()

            count = count + jnp.where(slot >= 0, 1, 0)

    def result_copy(j, slot):
        return pltpu.make_async_copy(results.at[j], out_ref.at[slot], out_sems.at[j])

    @pl.loop(0, count)
    def _(j):
        pltpu.make_async_copy(out_ref.at[0], tiles.at[j], in_sems.at[j]).wait()
        head, tail = split(tiles[j])
        results[j, :, :HALF] = dot_split(
            (head[:, :HALF], tail[:, :HALF]), (head_ref[:HALF, :HALF], tail_ref[:HALF, :HALF])
        )
        results[j, :, HALF:] = dot_split((head, tail), (head_ref[:, HALF:], tail_ref[:, HALF:]))
        result_copy(j, slots[j]).start()

    @pl.loop(0, count)
    def _(j):
        result_copy(j, 0).wait()


def finish(slots, head, tail, received, pairs, before, name, rows):
    columns = received[0].shape[-1]
    most = min(PAIR * len(pairs), OWN_TILES)
    hbm = pl.BlockSpec(memory_space=pl.ANY)
    vmem = pl.BlockSpec(memory_space=pltpu.VMEM)
    operands = [slots, head, tail, *received] + ([] if before is None else [before])
    return pl.pallas_call(
        functools.partial(finish_kernel, pairs),
        out_shape=jax.ShapeDtypeStruct((OWN_TILES, rows, columns), jnp.float32),
        in_specs=[pl.BlockSpec(memory_space=pltpu.SMEM), vmem, vmem] + [hbm] * (len(operands) - 3),
        out_specs=hbm,
        input_output_aliases={} if before is None else {len(operands) - 1: 0},
        scratch_shapes=[
            pltpu.VMEM((most, rows, columns), jnp.float32),
            pltpu.VMEM((most, rows, columns), jnp.float32),
            pltpu.SMEM((most,), jnp.int32),
            pltpu.SemaphoreType.DMA((most,)),
            pltpu.SemaphoreType.DMA((most,)),
        ],
        compiler_params=pltpu.CompilerParams(vmem_limit_bytes=24 << 20),
        cost_estimate=pl.CostEstimate(
            flops=1_000_000, bytes_accessed=1 << 16, transcendentals=0
        ),
        name=name,
    )(*operands)


def second_pairs_kernel(first_ref, second_ref, out_ref, staged, sems):
    rows = staged.shape[2] // 2
    pieces = [
        (i, rank, part) for i in range(2) for rank in range(PAIR) for part in range(0, 2 * rows, rows)
    ]

    def load(n):
        i, rank, part = pieces[n]
        source = (first_ref, second_ref)[i].at[1, rank, pl.ds(part, rows)]
        return pltpu.make_async_copy(source, staged.at[i, rank, pl.ds(part, rows)], sems.at[n])

    def store(n):
        i, rank, part = pieces[n]
        source = staged.at[i, rank, pl.ds(part, rows)]
        return pltpu.make_async_copy(source, out_ref.at[i, rank, pl.ds(part, rows)], sems.at[n])

    for n in range(len(pieces)):
        load(n).start()
    for n in range(len(pieces)):
        load(n).wait()
        store(n).start()
    for n in range(len(pieces)):
        store(n).wait()


def second_pairs(first, second):
    hbm = pl.BlockSpec(memory_space=pl.ANY)
    return pl.pallas_call(
        second_pairs_kernel,
        out_shape=jax.ShapeDtypeStruct(first.shape, first.dtype),
        in_specs=[hbm, hbm],
        out_specs=hbm,
        scratch_shapes=[
            pltpu.VMEM(first.shape, first.dtype),
            pltpu.SemaphoreType.DMA((4 * PAIR,)),
        ],
        cost_estimate=pl.CostEstimate(
            flops=1_000_000, bytes_accessed=1 << 16, transcendentals=0
        ),
        name="second_pairs",
    )(first, second)


def shards(observations, inverse_factor, tile_count, tile_owner, tile_slot):
    scenes, rows = lax.axis_size("scene"), lax.axis_size("rows")
    tile_rows, columns = observations.shape[1:]
    chips = scenes // 2

    def along_z(value, up):
        return lax.ppermute(value, "scene", ring_pairs(scenes, chips, 2, up))

    def other_core(value):
        return lax.ppermute(value, "scene", ring_pairs(scenes, 2, 1, 1))

    up, down, cross, seats, table = pack(observations, tile_count, tile_owner, tile_slot, scenes)
    from_below, from_above = along_z(up, 1), along_z(down, chips - 1)
    crossed = other_core(cross)
    tiles, _ = lax.optimization_barrier((observations, seats))
    value, own, far = gram(tiles, inverse_factor, tile_count, seats)
    value, crossed = lax.optimization_barrier((value, crossed))
    mine = jnp.zeros((8, 128), jnp.float32).at[0, : table.shape[0]].set(table.astype(jnp.float32))
    tables = jnp.concatenate([mine, other_core(mine)], 1)
    stages = reduction_stages(scenes, rows)
    for axis, span, stride in stages:
        value = scatter_sum(value, axis, span, stride)
    height = value.shape[0]
    parts = from_ahead(jnp.concatenate([value, tables], 0), "scene", chips, 2)
    far = lax.dynamic_update_slice_in_dim(
        far, crossed[1].reshape(PAIR * tile_rows, columns), PAIR * tile_rows, 0
    )
    *parts, far, from_below, from_above = lax.optimization_barrier(
        (*parts, far, from_below, from_above)
    )
    far_in = along_z(far, 2)
    value = sum_in_order([part[:height] for part in parts], "scene", 2)

    def slots_of(ahead, other):
        start = 128 * other + 2 * PAIR * ((chips - ahead) % chips) + PAIR * other
        return parts[ahead][height, start : start + PAIR]

    sources = [(0, 0), (0, 1), (3, 0), (1, 0), (3, 1), (1, 1), (2, 0), (2, 1)]
    slots = jnp.concatenate([slots_of(*source) for source in sources]).astype(jnp.int32)
    value, from_below, from_above = lax.optimization_barrier((value, from_below, from_above))
    passed_on = other_core(second_pairs(from_below, from_above))
    (x_axis, x_span, x_stride), (y_axis, y_span, y_stride) = stages[1:]
    value = gather(value, y_axis, y_span, y_stride)
    value, slots = lax.optimization_barrier((value, slots))
    pieces = from_ahead(value, x_axis, x_span, x_stride)
    pieces = pieces + [other_core(piece) for piece in pieces]
    upper, head, tail = factor(pieces, inverse_factor, scenes * rows * OWN_TILES * tile_rows)
    near = [own, crossed, from_below, from_above, passed_on, passed_on]
    first = PAIR * len(near)
    out = finish(slots[:first], head, tail, near, (0, 0, 0, 0, 0, 1), None, "finish_near", tile_rows)
    far = [far_in, far_in]
    return finish(slots[first:], head, tail, far, (0, 1), out, "finish_far", tile_rows), upper


def solution(mesh):
    in_specs = (
        P(("scene", "rows"), None, None),
        P(),
        P(("scene", "rows")),
        P(("scene", "rows")),
        P(("scene", "rows")),
    )
    out_specs = (P(("scene", "rows"), None, None), P())
    return jax.shard_map(shards, mesh=mesh, in_specs=in_specs, out_specs=out_specs, check_vma=False)
```

```python
import functools

import jax
import jax.numpy as jnp
from jax import lax
from jax.experimental import pallas as pl
from jax.experimental.pallas import tpu as pltpu
from jax.sharding import PartitionSpec as P

OWN_TILES = 8
BLOCK = 128
PIVOT = 8
HALF = 256
PAIR = 2
SPARE = 8
ROOM = 24 << 10
GROUP = 4


def split(value):
    head = value.astype(jnp.bfloat16)
    return head, (value - head.astype(jnp.float32)).astype(jnp.bfloat16)


def dot16(left, right, left_dim=1, right_dim=0):
    return lax.dot_general(
        left,
        right,
        (((left_dim,), (right_dim,)), ((), ())),
        preferred_element_type=jnp.float32,
    )


def dot32(left, right, left_dim=1, right_dim=0):
    return lax.dot_general(
        left,
        right,
        (((left_dim,), (right_dim,)), ((), ())),
        precision=lax.Precision.HIGHEST,
        preferred_element_type=jnp.float32,
    )


def dot_split(left, right):
    return dot16(left[0], right[0]) + (dot16(left[0], right[1]) + dot16(left[1], right[0]))


def seats_of_tiles(count_ref, owner_ref, used, note):
    me = lax.axis_index("scene")
    chips = used.shape[0] // 2
    for pair in range(used.shape[0]):
        used[pair] = 0
    for i in range(owner_ref.shape[0]):

        @pl.when(i < count_ref[0])
        def _():
            owner = owner_ref[i]
            up = lax.rem(owner // 2 - me // 2 + chips, chips)
            other = lax.rem(owner + me, 2)
            pair = 2 * up + other
            rank = used[pair]
            used[pair] = rank + 1
            note(i, pair, rank)


def pack_kernel(
    count_ref, owner_ref, slot_ref, tiles_ref, up_ref, down_ref, cross_ref, seat_ref, table_ref,
    staged, used, sems,
):
    capacity = owner_ref.shape[0]
    targets = {
        2: up_ref.at[0], 3: up_ref.at[1], 6: down_ref.at[0], 7: down_ref.at[1],
        1: cross_ref.at[0], 5: cross_ref.at[1],
    }
    for seat in range(capacity):
        table_ref[seat] = -1
        seat_ref[seat] = 0

    def note(i, pair, rank):
        seat_ref[i] = PAIR * pair + rank
        table_ref[PAIR * pair + rank] = slot_ref[i]

    seats_of_tiles(count_ref, owner_ref, used, note)

    def load(i):
        return pltpu.make_async_copy(tiles_ref.at[i], staged.at[i], sems.at[i])

    def store(i, target, rank):
        return pltpu.make_async_copy(staged.at[i], target.at[rank], sems.at[i])

    def sent(i):
        pair = seat_ref[i] // PAIR
        return (i < count_ref[0]) & (pair != 0) & (pair != 4)

    for i in range(capacity):

        @pl.when(sent(i))
        def _():
            load(i).start()

    for i in range(capacity):

        @pl.when(sent(i))
        def _():
            load(i).wait()
            for pair, target in targets.items():

                @pl.when(seat_ref[i] // PAIR == pair)
                def _():
                    store(i, target, lax.rem(seat_ref[i], PAIR)).start()

    for i in range(capacity):

        @pl.when(sent(i))
        def _():
            store(i, up_ref.at[0], 0).wait()


def pack(tiles, tile_count, tile_owner, tile_slot, scenes):
    smem = pl.BlockSpec(memory_space=pltpu.SMEM)
    hbm = pl.BlockSpec(memory_space=pl.ANY)
    capacity = tile_owner.shape[0]
    two_pairs = jax.ShapeDtypeStruct((2, PAIR) + tiles.shape[1:], tiles.dtype)
    table = jax.ShapeDtypeStruct((capacity,), jnp.int32)
    return pl.pallas_call(
        pack_kernel,
        out_shape=(two_pairs, two_pairs, two_pairs, table, table),
        in_specs=[smem, smem, smem, hbm],
        out_specs=(hbm, hbm, hbm, smem, smem),
        scratch_shapes=[
            pltpu.VMEM(tiles.shape, jnp.float32),
            pltpu.SMEM((scenes,), jnp.int32),
            pltpu.SemaphoreType.DMA((capacity,)),
        ],
        compiler_params=pltpu.CompilerParams(vmem_limit_bytes=56 << 20),
        cost_estimate=pl.CostEstimate(flops=0, bytes_accessed=8 << 20, transcendentals=0),
        name="pack",
    )(tile_count, tile_owner, tile_slot, tiles)


def gram_kernel(
    count_ref, seat_ref, tile_ref, inverse_ref, gram_ref, own_ref, far_ref, inv_head, inv_tail, cross, sems
):
    step = pl.program_id(0)
    tiles = tile_ref.shape[0]

    height = tile_ref.shape[1]

    def kept(i, target, rank):
        rows = pl.ds(pl.multiple_of(rank * height, 8), height)
        return pltpu.make_async_copy(tile_ref.at[i], target.at[rows], sems.at[i])

    @pl.when(step == 0)
    def _():
        head, tail = split(inverse_ref[...])
        inv_head[...] = head
        inv_tail[...] = tail
        gram_ref[...] = jnp.zeros_like(gram_ref)
        cross[...] = jnp.zeros_like(cross)

    for i in range(tiles):
        for pair, target in ((0, own_ref), (4, far_ref)):
            seat = seat_ref[tiles * step + i]

            @pl.when((tiles * step + i < count_ref[0]) & (seat // PAIR == pair))
            def _():
                kept(i, target, lax.rem(seat, PAIR)).start()

    @pl.when(tiles * step < count_ref[0])
    def _():
        live = [tile_ref[0]]
        for i in range(1, tiles):
            live.append(jnp.where(tiles * step + i < count_ref[0], tile_ref[i], 0.0))
        head, tail = split(jnp.concatenate(live, 0))
        left = dot_split(
            (head[:, :HALF], tail[:, :HALF]), (inv_head[:HALF, :HALF], inv_tail[:HALF, :HALF])
        )
        right = dot_split((head, tail), (inv_head[:, HALF:], inv_tail[:, HALF:]))
        left_head, left_tail = split(left)
        right_head, right_tail = split(right)
        gram_ref[:HALF, :] += dot16(left_head, left_head, 0, 0)
        cross[:HALF, :] += dot16(left_head, left_tail, 0, 0)
        gram_ref[HALF : 2 * HALF, :] += (
            dot16(left_head, right_head, 0, 0)
            + dot16(left_head, right_tail, 0, 0)
            + dot16(left_tail, right_head, 0, 0)
        )
        gram_ref[2 * HALF :, :] += dot16(right_head, right_head, 0, 0)
        cross[HALF:, :] += dot16(right_head, right_tail, 0, 0)

    for i in range(tiles):
        pair = seat_ref[tiles * step + i] // PAIR

        @pl.when((tiles * step + i < count_ref[0]) & ((pair == 0) | (pair == 4)))
        def _():
            kept(i, own_ref, 0).wait()

    @pl.when(step == pl.num_programs(0) - 1)
    def _():
        gram_ref[:HALF, :] += cross[:HALF, :] + cross[:HALF, :].T
        gram_ref[2 * HALF :, :] += cross[HALF:, :] + cross[HALF:, :].T


def gram(tiles, inverse_factor, tile_count, seats):
    capacity, rows, columns = tiles.shape
    pair = jax.ShapeDtypeStruct((ROOM, columns), jnp.float32)
    hbm = pl.BlockSpec(memory_space=pl.ANY)
    return pl.pallas_call(
        gram_kernel,
        out_shape=(
            jax.ShapeDtypeStruct((3 * HALF, HALF), jnp.float32),
            pair,
            jax.ShapeDtypeStruct((2 * PAIR * rows + SPARE, columns), jnp.float32),
        ),
        grid_spec=pltpu.PrefetchScalarGridSpec(
            num_scalar_prefetch=2,
            grid=(capacity // GROUP,),
            in_specs=[
                pl.BlockSpec(
                    (GROUP, rows, columns),
                    lambda i, count, _: (
                        jnp.minimum(i, jnp.maximum(count[0] - 1, 0) // GROUP), 0, 0
                    ),
                ),
                pl.BlockSpec((columns, columns), lambda i, *_: (0, 0)),
            ],
            out_specs=(
                pl.BlockSpec((3 * HALF, HALF), lambda i, *_: (0, 0)),
                hbm,
                hbm,
            ),
            scratch_shapes=[
                pltpu.VMEM((columns, columns), jnp.bfloat16),
                pltpu.VMEM((columns, columns), jnp.bfloat16),
                pltpu.VMEM((2 * HALF, HALF), jnp.float32),
                pltpu.SemaphoreType.DMA((GROUP,)),
            ],
        ),
        compiler_params=pltpu.CompilerParams(
            dimension_semantics=("arbitrary",), vmem_limit_bytes=56 << 20
        ),
        cost_estimate=pl.CostEstimate(
            flops=1_000_000, bytes_accessed=1 << 16, transcendentals=0
        ),
        name="gram",
    )(tile_count, seats, tiles, inverse_factor)


def ring_pairs(size, span, stride, shift):
    ring = [i // stride % span for i in range(size)]
    return [(i, i + ((r + shift) % span - r) * stride) for i, r in enumerate(ring)]


def scatter_sum(value, axis, span, stride):
    size = lax.axis_size(axis)
    me = lax.axis_index(axis) // stride % span
    parts = value.reshape((span, -1) + value.shape[1:])
    total = lax.dynamic_index_in_dim(parts, me, 0, keepdims=False)
    for shift in range(1, span):
        sent = lax.dynamic_index_in_dim(parts, (me + shift) % span, 0, keepdims=False)
        total = total + lax.ppermute(sent, axis, ring_pairs(size, span, stride, shift))
    return total


def select_one(tests, values):
    chosen = values[0]
    for test, value in zip(tests[1:], values[1:]):
        chosen = jnp.where(test, value, chosen)
    return chosen


def from_ahead(value, axis, span, stride):
    size = lax.axis_size(axis)
    return [value] + [
        lax.ppermute(value, axis, ring_pairs(size, span, stride, span - ahead))
        for ahead in range(1, span)
    ]


def in_order(ahead_values, axis, stride):
    span = len(ahead_values)
    me = lax.axis_index(axis) // stride % span
    return [
        select_one([(me + ahead) % span == place for ahead in range(span)], ahead_values)
        for place in range(span)
    ]


def gather(value, axis, span, stride):
    return jnp.concatenate(in_order(from_ahead(value, axis, span, stride), axis, stride), 0)


def reduction_stages(scenes, rows):
    side = 4
    return [("scene", 2, 1), ("rows", side, 1), ("rows", rows // side, side)]


def sum_in_order(ahead_values, axis, stride):
    total, *more = in_order(ahead_values, axis, stride)
    for value in more:
        total = total + value
    return total


def sweep(block):
    shape = (PIVOT, BLOCK)
    lane = lax.broadcasted_iota(jnp.int32, shape, 1)
    sub = lax.broadcasted_iota(jnp.int32, shape, 0)
    strips = [block[PIVOT * v : PIVOT * (v + 1), :] for v in range(BLOCK // PIVOT)]
    upper = []
    for s in range(len(strips)):
        base = PIVOT * s
        inside = (lane >= base) & (lane < base + PIVOT)
        own = [jnp.broadcast_to(strips[s][q : q + 1, :], shape) for q in range(PIVOT)]
        pivot = {
            (r, c): jnp.broadcast_to(own[r][:, base + c : base + c + 1], shape)
            for r in range(PIVOT)
            for c in range(r, PIVOT)
        }
        u = {}
        scale = []
        for q in range(PIVOT):
            scale.append(lax.rsqrt(pivot[q, q]))
            for c in range(q + 1, PIVOT):
                u[q, c] = pivot[q, c] * scale[q]
            for r in range(q + 1, PIVOT):
                for c in range(r, PIVOT):
                    pivot[r, c] = pivot[r, c] - u[q, r] * u[q, c]
        swept = [
            jnp.where(inside, jnp.where(lane == base + q, 1.0, 0.0), own[q]) for q in range(PIVOT)
        ]
        for q in range(PIVOT):
            for r in range(q):
                own[q] = own[q] - u[r, q] * own[r]
                swept[q] = swept[q] - u[r, q] * swept[r]
            own[q] = own[q] * scale[q]
            swept[q] = swept[q] * scale[q]
        for v in range(s + 1, len(strips)):
            column = []
            for q in range(PIVOT):
                entry = jnp.broadcast_to(strips[v][:, base + q : base + q + 1], shape)
                for r in range(q):
                    entry = entry - u[r, q] * column[r]
                column.append(entry * scale[q])
            rest = jnp.where(inside, 0.0, strips[v])
            for q in range(PIVOT):
                rest = rest - column[q] * swept[q]
            strips[v] = rest
        factor_rows, inverse_rows = own[0], swept[0]
        for q in range(1, PIVOT):
            factor_rows = jnp.where(sub == q, own[q], factor_rows)
            inverse_rows = jnp.where(sub == q, swept[q], inverse_rows)
        upper.append(jnp.where(lane >= base + sub, factor_rows, 0.0))
        strips[s] = jnp.where(lane <= base + sub, inverse_rows, 0.0)
    return jnp.concatenate(upper, 0), jnp.concatenate(strips, 0)


def factor_kernel(row_count, inverse_ref, *refs):
    *pieces, factor_ref, head_ref, tail_ref, gram_ref, work = refs
    size = work.shape[0]
    core = lax.rem(lax.axis_index("scene"), 2)
    ring = len(pieces) // 2
    x = lax.rem(lax.axis_index("rows"), ring)
    height = pieces[0].shape[0]
    for i, piece in enumerate(pieces):
        half = core if i < ring else 1 - core
        row = (half * ring + lax.rem(x + i % ring, ring)) * height
        gram_ref[pl.ds(pl.multiple_of(row, 8), height), :] = piece[...]
    work[:HALF, :HALF] = gram_ref[:HALF, :] / row_count
    work[:HALF, HALF:] = gram_ref[HALF : 2 * HALF, :] / row_count
    work[HALF:, HALF:] = gram_ref[2 * HALF :, :] / row_count
    work[HALF:, :HALF] = jnp.zeros((HALF, HALF), jnp.float32)

    steps = size // BLOCK
    block = work[:BLOCK, :BLOCK]
    for k in range(steps):
        offset, end = k * BLOCK, (k + 1) * BLOCK
        here, below = pl.ds(offset, BLOCK), pl.ds(end, size - end)
        upper, inverse = sweep(block)
        if k < steps - 1:
            ahead = dot32(inverse, work[here, end : end + BLOCK])
            block = work[end : end + BLOCK, end : end + BLOCK] - dot32(ahead, ahead, 0, 0)
        right = dot32(inverse, work[here, :])
        factor_ref[here, :] = jnp.zeros((BLOCK, size), jnp.float32)
        factor_ref[here, here] = upper
        work[here, :] = right
        work[here, here] = inverse
        if k < steps - 1:
            factor_ref[here, end:] = right[:, end:]
            work[below, here] = jnp.zeros((size - end, BLOCK), jnp.float32)
            work[below, :] = work[below, :] - dot32(right[:, end:], work[here, :], 0, 0)

    row = lax.broadcasted_iota(jnp.int32, work.shape, 0)
    lane = lax.broadcasted_iota(jnp.int32, work.shape, 1)
    inverse = jnp.where(lane <= row, work[...], 0.0)
    head_ref[...], tail_ref[...] = split(dot32(inverse_ref[...], inverse, 1, 1))


def factor(pieces, inverse_factor, row_count):
    vmem = pl.BlockSpec(memory_space=pltpu.VMEM)
    size = inverse_factor.shape[0]
    return pl.pallas_call(
        functools.partial(factor_kernel, row_count),
        out_shape=(
            jax.ShapeDtypeStruct((size, size), jnp.float32),
            jax.ShapeDtypeStruct((size, size), jnp.bfloat16),
            jax.ShapeDtypeStruct((size, size), jnp.bfloat16),
        ),
        in_specs=[vmem] * (1 + len(pieces)),
        out_specs=(vmem, vmem, vmem),
        scratch_shapes=[
            pltpu.VMEM((3 * HALF, HALF), jnp.float32),
            pltpu.VMEM((size, size), jnp.float32),
        ],
        compiler_params=pltpu.CompilerParams(vmem_limit_bytes=24 << 20),
        cost_estimate=pl.CostEstimate(
            flops=1_000_000, bytes_accessed=1 << 16, transcendentals=0
        ),
        name="factor",
    )(inverse_factor, *pieces)


def finish_kernel(pairs, slot_ref, head_ref, tail_ref, *refs):
    out_ref, tiles, results, slots, in_sems, out_sems = refs[-6:]
    count = jnp.int32(0)
    for p, place in enumerate(pairs):
        flat = len(refs[p].shape) == 2
        first = PAIR * place if flat else 0
        source = refs[p] if flat else refs[p].at[place]
        height = tiles.shape[1]
        for rank in range(PAIR):
            slot = slot_ref[PAIR * p + rank]

            @pl.when(slot >= 0)
            def _(source=source, rank=rank, slot=slot, count=count, first=first):
                slots[count] = slot
                rows = pl.ds((first + rank) * height, height)
                own_rows = source.at[rows] if len(source.shape) == 2 else source.at[rank]
                pltpu.make_async_copy(own_rows, tiles.at[count], in_sems.at[count]).start()

            count = count + jnp.where(slot >= 0, 1, 0)

    def result_copy(j, slot):
        return pltpu.make_async_copy(results.at[j], out_ref.at[slot], out_sems.at[j])

    @pl.loop(0, count)
    def _(j):
        pltpu.make_async_copy(out_ref.at[0], tiles.at[j], in_sems.at[j]).wait()
        head, tail = split(tiles[j])
        results[j, :, :HALF] = dot_split(
            (head[:, :HALF], tail[:, :HALF]), (head_ref[:HALF, :HALF], tail_ref[:HALF, :HALF])
        )
        results[j, :, HALF:] = dot_split((head, tail), (head_ref[:, HALF:], tail_ref[:, HALF:]))
        result_copy(j, slots[j]).start()

    @pl.loop(0, count)
    def _(j):
        result_copy(j, 0).wait()


def finish(slots, head, tail, received, pairs, before, name, rows):
    columns = received[0].shape[-1]
    most = min(PAIR * len(pairs), OWN_TILES)
    hbm = pl.BlockSpec(memory_space=pl.ANY)
    vmem = pl.BlockSpec(memory_space=pltpu.VMEM)
    operands = [slots, head, tail, *received] + ([] if before is None else [before])
    return pl.pallas_call(
        functools.partial(finish_kernel, pairs),
        out_shape=jax.ShapeDtypeStruct((OWN_TILES, rows, columns), jnp.float32),
        in_specs=[pl.BlockSpec(memory_space=pltpu.SMEM), vmem, vmem] + [hbm] * (len(operands) - 3),
        out_specs=hbm,
        input_output_aliases={} if before is None else {len(operands) - 1: 0},
        scratch_shapes=[
            pltpu.VMEM((most, rows, columns), jnp.float32),
            pltpu.VMEM((most, rows, columns), jnp.float32),
            pltpu.SMEM((most,), jnp.int32),
            pltpu.SemaphoreType.DMA((most,)),
            pltpu.SemaphoreType.DMA((most,)),
        ],
        compiler_params=pltpu.CompilerParams(vmem_limit_bytes=24 << 20),
        cost_estimate=pl.CostEstimate(
            flops=1_000_000, bytes_accessed=1 << 16, transcendentals=0
        ),
        name=name,
    )(*operands)


def second_pairs_kernel(first_ref, second_ref, out_ref, staged, sems):
    rows = staged.shape[2] // 2
    pieces = [
        (i, rank, part) for i in range(2) for rank in range(PAIR) for part in range(0, 2 * rows, rows)
    ]

    def load(n):
        i, rank, part = pieces[n]
        source = (first_ref, second_ref)[i].at[1, rank, pl.ds(part, rows)]
        return pltpu.make_async_copy(source, staged.at[i, rank, pl.ds(part, rows)], sems.at[n])

    def store(n):
        i, rank, part = pieces[n]
        source = staged.at[i, rank, pl.ds(part, rows)]
        return pltpu.make_async_copy(source, out_ref.at[i, rank, pl.ds(part, rows)], sems.at[n])

    for n in range(len(pieces)):
        load(n).start()
    for n in range(len(pieces)):
        load(n).wait()
        store(n).start()
    for n in range(len(pieces)):
        store(n).wait()


def second_pairs(first, second):
    hbm = pl.BlockSpec(memory_space=pl.ANY)
    return pl.pallas_call(
        second_pairs_kernel,
        out_shape=jax.ShapeDtypeStruct(first.shape, first.dtype),
        in_specs=[hbm, hbm],
        out_specs=hbm,
        scratch_shapes=[
            pltpu.VMEM(first.shape, first.dtype),
            pltpu.SemaphoreType.DMA((4 * PAIR,)),
        ],
        cost_estimate=pl.CostEstimate(
            flops=1_000_000, bytes_accessed=1 << 16, transcendentals=0
        ),
        name="second_pairs",
    )(first, second)


def shards(observations, inverse_factor, tile_count, tile_owner, tile_slot):
    scenes, rows = lax.axis_size("scene"), lax.axis_size("rows")
    tile_rows, columns = observations.shape[1:]
    chips = scenes // 2

    def along_z(value, up):
        return lax.ppermute(value, "scene", ring_pairs(scenes, chips, 2, up))

    def other_core(value):
        return lax.ppermute(value, "scene", ring_pairs(scenes, 2, 1, 1))

    up, down, cross, seats, table = pack(observations, tile_count, tile_owner, tile_slot, scenes)
    from_below, from_above = along_z(up, 1), along_z(down, chips - 1)
    crossed = other_core(cross)
    tiles, _ = lax.optimization_barrier((observations, seats))
    value, own, far = gram(tiles, inverse_factor, tile_count, seats)
    value, crossed = lax.optimization_barrier((value, crossed))
    mine = jnp.zeros((8, 128), jnp.float32).at[0, : table.shape[0]].set(table.astype(jnp.float32))
    tables = jnp.concatenate([mine, other_core(mine)], 1)
    stages = reduction_stages(scenes, rows)
    for axis, span, stride in stages:
        value = scatter_sum(value, axis, span, stride)
    height = value.shape[0]
    parts = from_ahead(jnp.concatenate([value, tables], 0), "scene", chips, 2)
    far = lax.dynamic_update_slice_in_dim(
        far, crossed[1].reshape(PAIR * tile_rows, columns), PAIR * tile_rows, 0
    )
    *parts, far, from_below, from_above = lax.optimization_barrier(
        (*parts, far, from_below, from_above)
    )
    far_in = along_z(far, 2)
    value = sum_in_order([part[:height] for part in parts], "scene", 2)

    def slots_of(ahead, other):
        start = 128 * other + 2 * PAIR * ((chips - ahead) % chips) + PAIR * other
        return parts[ahead][height, start : start + PAIR]

    sources = [(0, 0), (0, 1), (3, 0), (1, 0), (3, 1), (1, 1), (2, 0), (2, 1)]
    slots = jnp.concatenate([slots_of(*source) for source in sources]).astype(jnp.int32)
    value, from_below, from_above = lax.optimization_barrier((value, from_below, from_above))
    passed_on = other_core(second_pairs(from_below, from_above))
    (x_axis, x_span, x_stride), (y_axis, y_span, y_stride) = stages[1:]
    value = gather(value, y_axis, y_span, y_stride)
    value, slots = lax.optimization_barrier((value, slots))
    pieces = from_ahead(value, x_axis, x_span, x_stride)
    pieces = pieces + [other_core(piece) for piece in pieces]
    upper, head, tail = factor(pieces, inverse_factor, scenes * rows * OWN_TILES * tile_rows)
    near = [own, crossed, from_below, from_above, passed_on, passed_on]
    first = PAIR * len(near)
    out = finish(slots[:first], head, tail, near, (0, 0, 0, 0, 0, 1), None, "finish_near", tile_rows)
    far = [far_in, far_in]
    return finish(slots[first:], head, tail, far, (0, 1), out, "finish_far", tile_rows), upper


def solution(mesh):
    in_specs = (
        P(("scene", "rows"), None, None),
        P(),
        P(("scene", "rows")),
        P(("scene", "rows")),
        P(("scene", "rows")),
    )
    out_specs = (P(("scene", "rows"), None, None), P())
    return jax.shard_map(shards, mesh=mesh, in_specs=in_specs, out_specs=out_specs, check_vma=False)
```
